512 devices in a mesh: dom: 128 (over y, z, core), rep: 4 (over x).
Axes of the slice: x: 4, y: 8, z: 8, core: 2. Of those that a mesh axis runs over, the one named last changes fastest.
Arguments:
- feats: bfloat16 [131072, 256], P('dom'), may hold values from -6 to 6
- history: bfloat16 [131072, 256], P('dom'), may hold values from -6 to 6
- adj_inner: bfloat16 [131072, 1024], P('dom'), may hold values from -0.15625 to 0.15625
- adj_halo: bfloat16 [131072, 256], P('dom'), may hold values from -0.15625 to 0.15625
- halo_rows: int32 [16384, 2], P('dom'), may hold values from 0 to 1023
- w_self: bfloat16 [256, 256], replicated, may hold values from -0.375 to 0.375
- w_nbr: bfloat16 [256, 256], replicated, may hold values from -0.375 to 0.375
- b_enc: float32 [256], replicated, may hold values from -3 to 3
- edge_owner: int32 [131072, 2], P(('dom', 'rep')), may hold values from 0 to 127, all different within a row; in each aligned block of 256 rows (0 to 255, 256 to 511, ...) at most 8 rows name the same one
- edge_rows: int32 [131072, 2], P(('dom', 'rep')), may hold values from 0 to 1023
- labels: int32 [131072], P(('dom', 'rep')), may hold values 0 or 1
- w_dec1: bfloat16 [256, 256], replicated, may hold values from -0.375 to 0.375
- b_dec1: float32 [256], replicated, may hold values from -3 to 3
- w_dec2: bfloat16 [256], replicated, may hold values from -0.375 to 0.375
Outputs:
- embed: bfloat16 [131072, 256], P('dom')
- grad_embed: float32 [131072, 256], P(('dom', 'rep'))
- grad_dec1: float32 [256, 256], replicated
- grad_bias1: float32 [256], replicated
- grad_dec2: float32 [256], replicated
The draws below stay inside these ranges and needn't reach their ends.
Inputs may be any that keep to these rules, and one draw needn't show every extreme that they name: `edge_owner`: among the rows of one device, no owner is named by more than 8 endpoints, a bound that some block reaches; the two endpoints of an edge have different owners.
All inputs are finite; a program needn't handle non-finite values. No bound on the sum of `labels` on one device may be relied on, other than what follows from the above.
Results may differ from the reference program's by a relative error of at most 0.0069.
Values may be sent and summed in bfloat16 or wider, within the bound.
A program may use at most 64 MiB of HBM per device.

```python
import math
import jax
import jax.numpy as jnp
import numpy as np
from jax import lax

W = 256
NPD = 1024
HALO = 256
QDEV = 256
NODES = 131072
CAP_H = 2
CAP_E = 8
Q_TOTAL = 131072
N_DOM = 128


def set_ends(result, own_key, low, top_value):
    index_at = [jax.random.randint(jax.random.fold_in(own_key, axis), (), 0, length) for axis, length in enumerate(result.shape)]
    main_axis = result.shape.index(max(result.shape))
    neighbour = index_at[:main_axis] + [(index_at[main_axis] + 1) % result.shape[main_axis]] + index_at[main_axis + 1:]
    return result.at[tuple(index_at)].set(low).at[tuple(neighbour)].set(top_value)


def level_of(rng, extent, cuts, least, top_value):
    def one(dim, blocks):
        heights = jax.random.uniform(jax.random.fold_in(jax.random.fold_in(rng, 6), dim), (blocks,), jnp.float32, least / len(cuts), top_value / len(cuts))
        return jnp.repeat(jnp.exp(heights), extent[dim] // blocks).reshape((-1,) + (1,) * (len(extent) - dim - 1))

    level = one(*cuts[0])
    for cut in cuts[1:]:
        level = level * one(*cut)
    return level


def shared_out(stream_key, own, number, rows, number_of, top, bound, slope):
    ranking = jax.random.permutation(stream_key, number_of)
    crowded, ordinary = portions_of(number_of, rows * top, bound, slope, True), portions_of(number_of, rows * top, bound, slope, False)
    places = jnp.arange(number_of)

    def named(lengths, turn):
        used = int((lengths > 0).sum())
        fixed = max(1, used // 4)
        passed = fixed + (places - fixed + turn * (used - fixed)) % max(1, number_of - fixed)
        return jnp.zeros((number_of,), jnp.int32).at[ranking[jnp.where(places < fixed, places, passed)]].set(jnp.asarray(lengths, jnp.int32))

    lengths = jnp.where(number % 4 == 0, named(crowded, number // 4), named(ordinary, number - number // 4 - 1))
    mixed = jax.random.permutation(jax.random.fold_in(own, 3), number_of)
    giver, sink = mixed[0:number_of // 2 * 2:2], mixed[1:number_of // 2 * 2:2]
    margin = jnp.minimum(lengths[giver] - 1, bound - lengths[sink]) // 2
    margin = jnp.where((giver == ranking[0]) | (sink == ranking[0]) | (lengths[sink] == 0), 0, jnp.maximum(margin, 0))
    passed = jax.random.randint(jax.random.fold_in(own, 4), (number_of // 2,), 0, 1 << 20) % (margin + 1)
    lengths = lengths.at[giver].add(-passed).at[sink].add(passed)
    items = jnp.searchsorted(jnp.cumsum(lengths), jnp.arange(rows * top), side="right").astype(jnp.int32)
    grid = items.reshape(top, rows).T
    grid = grid[jax.random.permutation(jax.random.fold_in(own, 1), rows)]
    turn = jax.random.randint(jax.random.fold_in(own, 2), (rows, 1), 0, top)
    return jnp.take_along_axis(grid, (jnp.arange(top)[None, :] + turn) % top, axis=1)


def portions_of(number_of, total, most, lean, full):
    weights = [(1 << 20) // math.isqrt(rank ** lean) + 1 for rank in range(1, number_of + 1)]
    largest = most if full else min(most, max(-(-total // number_of), total * weights[0] // sum(weights)))
    least = 1 if total - largest >= number_of - 1 else 0
    counts, rest = [largest] + [least] * (number_of - 1), total - largest - least * (number_of - 1)
    while rest > 0:
        movable = [i for i in range(1, number_of) if counts[i] < largest] or [i for i in range(1, number_of) if counts[i] < most]
        pool, remaining = sum([weights[i] for i in movable]), rest
        for i in movable:
            more = min(most - counts[i], max(1, remaining * weights[i] // pool), rest)
            counts[i] = counts[i] + more
            rest = rest - more
    return np.array(counts)


def scatter_about(rng, extent, spread, reach, pieces=(), held_as=jnp.bfloat16):
    array = jax.random.normal(rng, extent, jnp.float32) * spread
    if len(pieces) > 0:
        array = level_of(rng, extent, pieces, -0.22, 0.18) * array
    return jnp.clip(array, min=-reach, max=reach).astype(held_as)


def setup_inputs(seed: int = 0) -> dict:
    streams_of = jax.random.split(jax.random.key(seed), 15)
    feats = scatter_about(streams_of[0], (NODES, W), 1.0, 6.0, ((0, 128),))
    history = scatter_about(streams_of[1], (NODES, W), 1.0, 6.0, ((0, 128),))
    adj_inner = scatter_about(streams_of[2], (NODES, NPD), (NPD + HALO) ** -0.5, 0.15625, ((0, 128),))
    adj_halo = scatter_about(streams_of[3], (NODES, HALO), (NPD + HALO) ** -0.5, 0.15625, ((0, 128),))
    halo_rows = set_ends(jax.random.randint(streams_of[4], (N_DOM * N_DOM, CAP_H), 0, NPD), jax.random.fold_in(streams_of[4], 1), 0, NPD - 1).astype(jnp.int32)
    w_self = scatter_about(streams_of[5], (W, W), W ** -0.5, 0.375)
    w_nbr = scatter_about(streams_of[6], (W, W), W ** -0.5, 0.375)
    b_enc = scatter_about(streams_of[7], (W,), 0.5, 3.0, (), jnp.float32)
    edge_owner_keys = jax.random.split(jax.random.fold_in(streams_of[8], 1), Q_TOTAL // QDEV)
    edge_owner_turns = jax.random.permutation(jax.random.fold_in(streams_of[8], 3), Q_TOTAL // QDEV)
    edge_owner = jax.vmap(lambda own, number: shared_out(jax.random.fold_in(streams_of[8], 2), own, number, QDEV, N_DOM, 2, CAP_E, 2))(edge_owner_keys, edge_owner_turns).reshape((Q_TOTAL, 2))
    edge_rows = set_ends(jax.random.randint(streams_of[9], (Q_TOTAL, 2), 0, NPD), jax.random.fold_in(streams_of[9], 1), 0, NPD - 1).astype(jnp.int32)
    labels = set_ends((jax.random.randint(streams_of[10], (Q_TOTAL,), 0, 2) < 1).astype(jnp.int32), jax.random.fold_in(streams_of[10], 1), 0, 1)
    w_dec1 = scatter_about(streams_of[11], (W, W), W ** -0.5, 0.375)
    b_dec1 = scatter_about(streams_of[12], (W,), 0.5, 3.0, (), jnp.float32)
    w_dec2 = scatter_about(streams_of[13], (W,), W ** -0.5, 0.375)
    return {"feats": feats, "history": history, "adj_inner": adj_inner, "adj_halo": adj_halo, "halo_rows": halo_rows, "w_self": w_self, "w_nbr": w_nbr, "b_enc": b_enc, "edge_owner": edge_owner, "edge_rows": edge_rows, "labels": labels, "w_dec1": w_dec1, "b_dec1": b_dec1, "w_dec2": w_dec2}


def encode_block(rows_x, a_inner, a_halo, all_x, halo, w_self, w_nbr, b_enc):
    agg = (jnp.dot(a_inner, all_x, preferred_element_type=jnp.float32)
           + jnp.dot(a_halo, halo, preferred_element_type=jnp.float32)).astype(jnp.bfloat16)
    pre = (jnp.dot(rows_x, w_self, preferred_element_type=jnp.float32)
           + jnp.dot(agg, w_nbr, preferred_element_type=jnp.float32) + b_enc)
    return jnp.maximum(pre, 0.0).astype(jnp.bfloat16)


def decode(head, tail, target, w_dec1, b_dec1, w_dec2):
    zprod = (head.astype(jnp.float32) * tail.astype(jnp.float32)).astype(jnp.bfloat16)
    pre = jnp.dot(zprod, w_dec1, preferred_element_type=jnp.float32) + b_dec1
    sig = jax.nn.sigmoid(pre)
    hidden = (pre * sig).astype(jnp.bfloat16)
    logit = jnp.dot(hidden, w_dec2, preferred_element_type=jnp.float32)
    dlogit = jax.nn.sigmoid(logit) - target
    d_pre = (dlogit[:, None] * w_dec2.astype(jnp.float32) * (sig * (1.0 + pre * (1.0 - sig)))).astype(jnp.bfloat16)
    grad_w1 = jnp.dot(zprod.T, d_pre, preferred_element_type=jnp.float32)
    grad_b1 = jnp.sum(d_pre.astype(jnp.float32), axis=0)
    grad_w2 = jnp.sum(hidden.astype(jnp.float32) * dlogit[:, None], axis=0)
    dzval = jnp.dot(d_pre, w_dec1.T, preferred_element_type=jnp.float32)
    return dzval * tail.astype(jnp.float32), dzval * head.astype(jnp.float32), grad_w1, grad_b1, grad_w2


def reference(feats, history, adj_inner, adj_halo, halo_rows, w_self, w_nbr, b_enc,
              edge_owner, edge_rows, labels, w_dec1, b_dec1, w_dec2):
    def one_cluster(part):
        start = part * NPD
        rows_x = lax.dynamic_slice_in_dim(feats, start, NPD, 0)
        a_inner = lax.dynamic_slice_in_dim(adj_inner, start, NPD, 0)
        a_halo = lax.dynamic_slice_in_dim(adj_halo, start, NPD, 0)
        wanted = lax.dynamic_slice_in_dim(halo_rows, part * N_DOM, N_DOM, 0)
        owners = jnp.arange(N_DOM, dtype=jnp.int32)[:, None] * NPD
        glob = (owners + wanted).reshape(-1).astype(jnp.int32)
        halo = history[glob]
        return encode_block(rows_x, a_inner, a_halo, rows_x, halo, w_self, w_nbr, b_enc)

    embed = lax.map(one_cluster, jnp.arange(N_DOM, dtype=jnp.int32)).reshape(NODES, W)

    def step(carry, block):
        gacc, acc1, accb, acc2 = carry
        start = block * QDEV
        owner = lax.dynamic_slice_in_dim(edge_owner, start, QDEV, 0)
        local = lax.dynamic_slice_in_dim(edge_rows, start, QDEV, 0)
        target = lax.dynamic_slice_in_dim(labels, start, QDEV, 0).astype(jnp.float32)
        index = (owner * NPD + local).astype(jnp.int32)
        head = embed[index[:, 0]]
        tail = embed[index[:, 1]]
        g_head, g_tail, gw1, gb1, gw2 = decode(head, tail, target, w_dec1, b_dec1, w_dec2)
        gacc = gacc.at[index[:, 0]].add(g_head).at[index[:, 1]].add(g_tail)
        return (gacc, acc1 + gw1, accb + gb1, acc2 + gw2), None

    init = (jnp.zeros((NODES, W), jnp.float32), jnp.zeros((W, W), jnp.float32),
            jnp.zeros((W,), jnp.float32), jnp.zeros((W,), jnp.float32))
    blocks = jnp.arange(Q_TOTAL // QDEV, dtype=jnp.int32)
    (grad_embed, grad_dec1, grad_bias1, grad_dec2), _ = lax.scan(step, init, blocks)
    return embed, grad_embed, grad_dec1, grad_bias1, grad_dec2
```

```python
import functools

import jax
import jax.numpy as jnp
from jax import lax
from jax.experimental import pallas as pl
from jax.experimental.pallas import tpu as pltpu
from jax.sharding import PartitionSpec as P

BF = jnp.bfloat16
F32 = jnp.float32
I32 = jnp.int32
MESH = pl.DeviceIdType.MESH
SLOTS = 8
LANES = 128


def log2(value):
    return value.bit_length() - 1


def iota(shape, dim):
    return lax.broadcasted_iota(I32, shape, dim)


def nn(a, b):
    return lax.dot_general(a, b, (((1,), (0,)), ((), ())), preferred_element_type=F32)


def nt(a, b):
    return lax.dot_general(a, b, (((1,), (1,)), ((), ())), preferred_element_type=F32)


def tn(a, b):
    return lax.dot_general(a, b, (((0,), (0,)), ((), ())), preferred_element_type=F32)


def hot(cond):
    return jnp.where(cond, 1.0, 0.0).astype(BF)


def column_of(row):
    n = row.shape[1]
    return jnp.sum(jnp.where(iota((n, n), 0) == iota((n, n), 1), row, 0.0), axis=1, keepdims=True)


def row_of(column):
    n = column.shape[0]
    return jnp.sum(jnp.where(iota((n, n), 0) == iota((n, n), 1), column, 0.0), axis=0, keepdims=True)


def copies(ref, sem):
    return pltpu.make_async_copy(ref, ref, sem)


def kernel(
    n_y, n_zc, n_x,
    eo, er, hr, lab, b_enc, b_dec1, w_dec2,
    feats_h, hist_h, adji_h, adjh_h, wself_h, wnbr_h, wdec1_h,
    emb_o, ge_o, gd_o, gv_o,
    feats, hist, adji, adjh, wself, wnbr, wdec1,
    ids_s, ids_r1, ids_t, ids_r2,
    hal_s, hal_r1, hal_t, hal_r2, adjp,
    inner, selfp, place,
    hot_e, hot_et, hot_g, hot_gt,
    fet_s, fet_a, fet_b, fet_r,
    gra_s, gra_a, gra_b, gra_r, gpair,
    zbuf, dbuf,
    xs1, xr1, xs2, xr2, xk,
    dc_s, dc_r, dz_s, dz_r, dy_r, dx_r, dg_r,
    load_sem, out_sem,
    ssem, rsem,
):
    n_dom = n_y * n_zc
    nodes, width = feats.shape
    half = width // 2
    queries = eo.shape[1]
    ends = 2 * queries
    slots = n_dom * SLOTS
    halos = 2 * n_dom
    n_z = n_zc // 2
    ly, lzc = log2(n_y), log2(n_zc)
    me = lax.axis_index("dom")
    rep = lax.axis_index("rep")
    y = lax.div(me, n_zc)
    zc = lax.rem(me, n_zc)
    z = lax.div(zc, 2)
    core = lax.rem(zc, 2)

    loads = [
        pltpu.make_async_copy(src, dst, load_sem.at[i])
        for i, (src, dst) in enumerate(
            ((feats_h, feats), (adji_h, adji), (wself_h, wself), (adjh_h, adjh), (hist_h, hist), (wnbr_h, wnbr), (wdec1_h, wdec1))
        )
    ]
    for load in loads:
        load.start()

    barrier = pltpu.get_barrier_semaphore()

    def zc_peer(k):
        return lax.rem(zc + k, n_zc)

    def y_peer(k):
        return lax.rem(y + k, n_y)

    def greet_zc(k, carry):
        pl.semaphore_signal(barrier, inc=1, device_id={"dom": y * n_zc + zc_peer(k)}, device_id_type=MESH)
        return carry

    def greet_y(k, carry):
        pl.semaphore_signal(barrier, inc=1, device_id={"dom": y_peer(k) * n_zc + zc}, device_id_type=MESH)
        return carry

    lax.fori_loop(1, n_zc, greet_zc, 0)
    lax.fori_loop(1, n_y, greet_y, 0)
    for k in range(1, n_x):
        pl.semaphore_signal(barrier, inc=1, device_id={"rep": lax.rem(rep + k, n_x)}, device_id_type=MESH)

    def along_zc(index, source, target):
        def body(k, carry):
            peer = zc_peer(k)
            pltpu.make_async_remote_copy(
                src_ref=source(peer), dst_ref=target(zc), send_sem=ssem.at[index], recv_sem=rsem.at[index],
                device_id={"dom": y * n_zc + peer}, device_id_type=MESH,
            ).start()
            return carry

        lax.fori_loop(1, n_zc, body, 0)
        pltpu.make_async_copy(source(zc), target(zc), rsem.at[index]).start()

    def along_y(index, source, target):
        def body(k, carry):
            peer = y_peer(k)
            pltpu.make_async_remote_copy(
                src_ref=source(peer), dst_ref=target(y), send_sem=ssem.at[index], recv_sem=rsem.at[index],
                device_id={"dom": peer * n_zc + zc}, device_id_type=MESH,
            ).start()
            return carry

        lax.fori_loop(1, n_y, body, 0)
        pltpu.make_async_copy(source(y), target(y), rsem.at[index]).start()

    owner = jnp.concatenate([eo[0:1, :], eo[1:2, :]], axis=1)
    local = jnp.concatenate([er[0:1, :], er[1:2, :]], axis=1)
    rows = iota((n_dom, ends), 0)
    turned = ((rows & (n_y - 1)) << lzc) + (rows >> ly)
    match = owner == turned
    match_hot = hot(match)
    before = hot(iota((ends, ends), 0) < iota((ends, ends), 1))
    rank = nn(match_hot, before)
    slot = jnp.sum(jnp.where(match, rank, 0.0), axis=0, keepdims=True)
    place[...] = jnp.broadcast_to(owner.astype(F32) * float(SLOTS) + slot, place.shape)

    def lane_rows(at, value):
        lane = iota((LANES, value.shape[1]), 0)
        part = jnp.where(lane < 16, value >> 5, value & 31)
        return jnp.where(at & (lane < 32), part.astype(F32), 0.0).astype(BF)

    wanted = lane_rows(slot == (iota((LANES, ends), 0) & 15).astype(F32), local)
    lane = iota((LANES, n_dom), 0) & 15
    halo_ids = jnp.where(lane == SLOTS, hr[0:1, :], hr[1:2, :])
    halo_wanted = lane_rows((lane == SLOTS) | (lane == SLOTS + 1), halo_ids)
    prow, pcol = iota((n_dom, n_dom), 0), iota((n_dom, n_dom), 1)
    to_zc_y = hot(pcol == ((prow & (n_y - 1)) << lzc) + (prow >> ly))
    to_y_zc = hot(pcol == ((prow & (n_zc - 1)) << ly) + (prow >> lzc))
    requests = nt(match_hot, wanted) + nt(to_zc_y, halo_wanted)
    ids_s[...] = requests.astype(BF).reshape(n_zc, n_y, LANES)

    pl.semaphore_wait(barrier, (n_zc - 1) + (n_y - 1) + (n_x - 1))
    along_zc(0, lambda p: ids_s.at[p], lambda m: ids_r1.at[m])

    tile = min(256, nodes)
    loads[0].wait()
    loads[1].wait()

    @pl.loop(0, nodes // tile)
    def _(i):
        at = pl.ds(pl.multiple_of(i * tile, tile), tile)
        inner[at, :] = nn(adji[at, :], feats[...])

    copies(ids_r1, rsem.at[0]).wait()
    ids_t[...] = nn(to_y_zc, ids_r1[...].reshape(n_dom, LANES)).astype(BF).reshape(n_y, n_zc, LANES)
    along_y(1, lambda p: ids_t.at[p], lambda m: ids_r2.at[m])

    loads[2].wait()
    loads[3].wait()

    @pl.loop(0, nodes // tile)
    def _(i):
        at = pl.ds(pl.multiple_of(i * tile, tile), tile)
        selfp[at, :] = nn(feats[at, :], wself[...]) + b_enc[...]

    ko, jo = iota((halos, halos), 0), iota((halos, halos), 1)
    std = ((((jo >> (lzc + 1)) << lzc) + (jo & (n_zc - 1))) << 1) + ((jo >> lzc) & 1)
    adjp[...] = nn(adjh[...], hot(ko == std)).astype(BF)

    for i in (4, 5, 6):
        loads[i].wait()

    place_col = column_of(place[0:1, :])
    etile = min(256, ends)
    for i in range(ends // etile):
        hot_e[i * etile : (i + 1) * etile, :] = hot(
            place_col[i * etile : (i + 1) * etile, :] == iota((etile, slots), 1).astype(F32)
        )

    copies(ids_r2, rsem.at[1]).wait()
    asked = nn(to_zc_y, ids_r2[...].reshape(n_dom, LANES))
    for c in range(2):
        at = SLOTS + c
        asked_c = 32.0 * asked[:, at : at + 1] + asked[:, at + 16 : at + 17]
        pick = hot(asked_c == iota((n_dom, nodes), 1).astype(F32))
        hal_s[:, c] = nn(pick, hist[...]).astype(BF).reshape(n_zc, n_y, width)
    along_zc(2, lambda p: hal_s.at[p], lambda m: hal_r1.at[m])

    gtile = min(256, slots)
    per = gtile // SLOTS
    id_rows = []
    for i in range(slots // gtile):
        asked = ids_r2[...].reshape(n_dom, LANES)[i * per : (i + 1) * per].astype(F32)
        spread = jnp.broadcast_to(asked[:, None, :], (per, SLOTS, LANES)).reshape(gtile, LANES)
        lane, mine = iota((gtile, LANES), 1), iota((gtile, LANES), 0) & (SLOTS - 1)
        weight = jnp.where(lane == mine, 32.0, jnp.where(lane == mine + 16, 1.0, 0.0))
        id_col = jnp.sum(spread * weight, axis=1, keepdims=True)
        hot_g[i * gtile : (i + 1) * gtile, :] = hot(id_col == iota((gtile, nodes), 1).astype(F32))
        id_rows.append(row_of(id_col))
    id_row = jnp.concatenate(id_rows, axis=1)

    copies(hal_r1, rsem.at[2]).wait()
    io, oo = iota((halos, halos), 1), iota((halos, halos), 0)
    into = ((oo & (n_zc - 1)) << (ly + 1)) + (((oo >> lzc) & 1) << ly) + (oo >> (lzc + 1))
    hal_t[...] = nn(hot(io == into), hal_r1[...].reshape(halos, width)).astype(BF).reshape(n_y, 2 * n_zc, width)
    along_y(3, lambda p: hal_t.at[p], lambda m: hal_r2.at[m])

    @pl.loop(0, nodes // tile)
    def _(i):
        at = pl.ds(pl.multiple_of(i * tile, tile), tile)
        hot_gt[at, :] = hot((iota((tile, slots), 0) + i * tile).astype(F32) == id_row)

    @pl.loop(0, slots // gtile)
    def _(i):
        at = pl.ds(pl.multiple_of(i * gtile, gtile), gtile)
        hot_et[at, :] = hot((iota((gtile, ends), 0) + i * gtile).astype(F32) == place[0:1, :])

    target = column_of(lab[...].astype(F32))

    copies(hal_r2, rsem.at[3]).wait()

    @pl.loop(0, nodes // tile)
    def _(i):
        at = pl.ds(pl.multiple_of(i * tile, tile), tile)
        agg = (inner[at, :] + nn(adjp[at, :], hal_r2[...].reshape(halos, width))).astype(BF)
        emb_o[at, :] = jnp.maximum(selfp[at, :] + nn(agg, wnbr[...]), 0.0).astype(BF)

    @pl.loop(0, slots // gtile)
    def _(i):
        at = pl.ds(pl.multiple_of(i * gtile, gtile), gtile)
        block = nn(hot_g[at, :], emb_o[...]).astype(BF)
        fet_s[pl.ds(i * per, per)] = block.reshape(per, SLOTS, width)

    left, right = pl.ds(0, half), pl.ds(half, half)

    def both_ways(base, send, mid_a, mid_b, recv):
        send4 = send.reshape(n_y, n_zc, SLOTS, width)
        along_zc(base, lambda p: send4.at[:, p, :, left], lambda m: mid_a.at[m])
        along_y(base + 1, lambda p: send4.at[p, :, :, right], lambda m: mid_b.at[m])

    def both_ways_on(base, mid_a, mid_b, recv):
        copies(mid_a, rsem.at[base]).wait()
        along_y(base + 2, lambda p: mid_a.at[:, p], lambda m: recv.at[0, m])
        copies(mid_b, rsem.at[base + 1]).wait()
        along_zc(base + 3, lambda p: mid_b.at[:, p], lambda m: recv.at[1, :, m])

    both_ways(4, fet_s, fet_a, fet_b, fet_r)
    both_ways_on(4, fet_a, fet_b, fet_r)
    copies(fet_r.at[0], rsem.at[6]).wait()
    copies(fet_r.at[1], rsem.at[7]).wait()

    both = [nn(hot_e[...], fet_r[h].reshape(slots, half)) for h in range(2)]
    head = jnp.concatenate([part[:queries] for part in both], axis=1)
    tail = jnp.concatenate([part[queries:] for part in both], axis=1)
    zprod = (head * tail).astype(BF)
    pre = nn(zprod, wdec1[...]) + b_dec1[...]
    sig = jax.nn.sigmoid(pre)
    hidden = (pre * sig).astype(BF).astype(F32)
    wout = w_dec2[...].astype(F32)
    logit = jnp.sum(hidden * wout, axis=1, keepdims=True)
    dlogit = jax.nn.sigmoid(logit) - target
    d_pre = (dlogit * wout * (sig * (1.0 + pre * (1.0 - sig)))).astype(BF)
    dz = nt(d_pre, wdec1[...])
    gpair[:queries, :] = (dz * tail).astype(BF)
    gpair[queries:, :] = (dz * head).astype(BF)

    @pl.loop(0, slots // gtile)
    def _(i):
        at = pl.ds(pl.multiple_of(i * gtile, gtile), gtile)
        block = nn(hot_et[at, :], gpair[...]).astype(BF)
        gra_s[pl.ds(i * per, per)] = block.reshape(per, SLOTS, width)

    both_ways(8, gra_s, gra_a, gra_b, gra_r)

    grad1 = tn(zprod, d_pre)
    gb1 = jnp.sum(d_pre.astype(F32), axis=0, keepdims=True)
    gd2 = jnp.sum(hidden * dlogit, axis=0, keepdims=True)
    vrow = iota((8, width), 0)
    vecs = jnp.where(vrow == 0, gb1, jnp.where(vrow == 1, gd2, 0.0))
    crows = width // 2
    zrows = crows // n_z
    for h in range(2):
        dc_s[h, :crows] = grad1[h * crows : (h + 1) * crows]
        dc_s[h, crows:] = vecs
    other = 1 - core
    pair = pltpu.make_async_remote_copy(
        src_ref=dc_s.at[other], dst_ref=dc_r, send_sem=ssem.at[12], recv_sem=rsem.at[12],
        device_id={"dom": y * n_zc + 2 * z + other}, device_id_type=MESH,
    )
    pair.start()

    def along_z(index, source, goal):
        def body(k, carry):
            peer = lax.rem(z + k, n_z)
            pltpu.make_async_remote_copy(
                src_ref=source(peer), dst_ref=goal(z), send_sem=ssem.at[index], recv_sem=rsem.at[index],
                device_id={"dom": y * n_zc + 2 * peer + core}, device_id_type=MESH,
            ).start()
            return carry

        lax.fori_loop(1, n_z, body, 0)
        pltpu.make_async_copy(source(z), goal(z), rsem.at[index]).start()

    pair.wait_recv()
    for j in range(n_z):
        dz_s[j, :zrows] = dc_s[core, j * zrows : (j + 1) * zrows] + dc_r[j * zrows : (j + 1) * zrows]
        dz_s[j, zrows:] = dc_s[core, crows:] + dc_r[crows:]
    along_z(13, lambda p: dz_s.at[p], lambda m: dz_r.at[m])

    both_ways_on(8, gra_a, gra_b, gra_r)

    copies(dz_r, rsem.at[13]).wait()
    total = dz_r[0]
    for j in range(1, n_z):
        total = total + dz_r[j]
    zbuf[...] = total
    along_y(14, lambda p: zbuf, lambda m: dy_r.at[m])

    copies(dy_r, rsem.at[14]).wait()
    total = dy_r[0]
    for j in range(1, n_y):
        total = total + dy_r[j]
    dbuf[...] = total
    for k in range(1, n_x):
        pltpu.make_async_remote_copy(
            src_ref=dbuf, dst_ref=dx_r.at[rep], send_sem=ssem.at[15], recv_sem=rsem.at[15],
            device_id={"rep": lax.rem(rep + k, n_x)}, device_id_type=MESH,
        ).start()
    pltpu.make_async_copy(dbuf, dx_r.at[rep], rsem.at[15]).start()

    flip = rep + 1 - 2 * lax.rem(rep, 2)
    wrap = 3 - rep
    wflip = wrap + 1 - 2 * lax.rem(wrap, 2)
    quarter = nodes // n_x
    jtile = min(64, quarter)

    def local_sum(q, cols):
        at = pl.ds(pl.multiple_of(q * quarter, quarter), quarter)
        return nn(hot_gt[at, :], gra_r[cols].reshape(slots, half))

    def trade(index, source, goal, partner):
        copy = pltpu.make_async_remote_copy(
            src_ref=source, dst_ref=goal, send_sem=ssem.at[index], recv_sem=rsem.at[index],
            device_id={"rep": partner}, device_id_type=MESH,
        )
        copy.start()
        return copy

    def joined(way, part):
        @pl.loop(0, quarter // jtile)
        def _(i):
            at = pl.ds(pl.multiple_of(i * jtile, jtile), jtile)
            xs2[way, at, :] = (xk[part, at, :] + xr1[way, 1, at, :].astype(F32)).astype(BF)

    copies(gra_r.at[0], rsem.at[10]).wait()
    xs1[0, 0] = local_sum(flip, 0).astype(BF)
    xs1[0, 1] = local_sum(wflip, 0).astype(BF)
    one = trade(16, xs1.at[0], xr1.at[0], flip)
    copies(gra_r.at[1], rsem.at[11]).wait()
    xs1[1, 0] = local_sum(wrap, 1).astype(BF)
    xs1[1, 1] = local_sum(wflip, 1).astype(BF)
    two = trade(17, xs1.at[1], xr1.at[1], wrap)
    xk[0] = local_sum(rep, 0)
    xk[1] = local_sum(rep, 1)
    xk[2] = local_sum(wrap, 0)
    xk[3] = local_sum(flip, 1)
    one.wait_recv()
    joined(0, 2)
    three = trade(18, xs2.at[0], xr2.at[0], wrap)
    two.wait_recv()
    joined(1, 3)
    four = trade(19, xs2.at[1], xr2.at[1], flip)

    copies(dx_r, rsem.at[15]).wait()
    total = dx_r[0]
    for j in range(1, n_x):
        total = total + dx_r[j]
    zbuf2 = total[:zrows]
    gv_o[...] = total[zrows:]
    dc_r[:zrows] = zbuf2
    along_z(20, lambda p: dc_r.at[pl.ds(0, zrows)], lambda m: dg_r.at[core, m])

    three.wait_recv()
    ge_o[:, :half] = xk[0] + xr1[0, 0].astype(F32) + xr2[0].astype(F32)
    four.wait_recv()
    ge_o[:, half:] = xk[1] + xr1[1, 0].astype(F32) + xr2[1].astype(F32)

    copies(dg_r.at[0], rsem.at[20]).wait()
    last = pltpu.make_async_remote_copy(
        src_ref=dg_r.at[core], dst_ref=dg_r.at[core], send_sem=ssem.at[21], recv_sem=rsem.at[21],
        device_id={"dom": y * n_zc + 2 * z + other}, device_id_type=MESH,
    )
    last.start()

    copies(ids_s.at[pl.ds(0, n_zc - 1)], ssem.at[0]).wait()
    copies(ids_t.at[pl.ds(0, n_y - 1)], ssem.at[1]).wait()
    copies(hal_s.at[pl.ds(0, n_zc - 1)], ssem.at[2]).wait()
    copies(hal_t.at[pl.ds(0, n_y - 1)], ssem.at[3]).wait()
    for base, mid_a, mid_b in ((4, fet_a, fet_b), (8, gra_a, gra_b)):
        copies(mid_a.at[pl.ds(0, n_zc - 1)], ssem.at[base]).wait()
        copies(mid_b.at[pl.ds(0, n_y - 1)], ssem.at[base + 1]).wait()
        copies(mid_b.at[pl.ds(0, n_y - 1)], ssem.at[base + 2]).wait()
        copies(mid_a.at[pl.ds(0, n_zc - 1)], ssem.at[base + 3]).wait()
    pair.wait_send()
    copies(dz_s.at[pl.ds(0, n_z - 1)], ssem.at[13]).wait()
    copies(dy_r.at[pl.ds(0, n_y - 1)], ssem.at[14]).wait()
    copies(dx_r.at[pl.ds(0, n_x - 1)], ssem.at[15]).wait()
    for copy in (one, two, three, four):
        copy.wait_send()
    copies(dg_r.at[0, pl.ds(0, n_z - 1)], ssem.at[20]).wait()
    last.wait()
    gd_o[...] = dg_r[...].reshape(width, width)


def per_device(
    feats, history, adj_inner, adj_halo, halo_rows, w_self, w_nbr, b_enc,
    edge_owner, edge_rows, labels, w_dec1, b_dec1, w_dec2,
):
    n_dom, n_x = lax.axis_size("dom"), lax.axis_size("rep")
    n_zc = 16 if n_dom == 128 else 4
    n_y = n_dom // n_zc
    nodes, width = feats.shape
    halos = adj_halo.shape[1]
    queries = edge_owner.shape[0]
    ends = 2 * queries
    slots = n_dom * SLOTS
    half = width // 2
    n_z = n_zc // 2
    quarter = nodes // n_x
    crows = width // 2
    zrows = crows // n_z
    vmem = pl.BlockSpec(memory_space=pltpu.VMEM)
    any_ = pl.BlockSpec(memory_space=pl.ANY)
    V = pltpu.VMEM
    outs = pl.pallas_call(
        functools.partial(kernel, n_y, n_zc, n_x),
        out_shape=(
            jax.ShapeDtypeStruct((nodes, width), BF),
            jax.ShapeDtypeStruct((quarter, width), F32),
            jax.ShapeDtypeStruct((width, width), F32),
            jax.ShapeDtypeStruct((8, width), F32),
        ),
        in_specs=[vmem] * 7 + [any_] * 7,
        out_specs=(vmem,) * 4,
        scratch_shapes=[
            V((nodes, width), BF), V((nodes, width), BF), V((nodes, nodes), BF), V((nodes, halos), BF),
            V((width, width), BF), V((width, width), BF), V((width, width), BF),
            V((n_zc, n_y, LANES), BF), V((n_zc, n_y, LANES), BF), V((n_y, n_zc, LANES), BF), V((n_y, n_zc, LANES), BF),
            V((n_zc, 2, n_y, width), BF), V((n_zc, 2, n_y, width), BF), V((n_y, 2 * n_zc, width), BF),
            V((n_y, 2 * n_zc, width), BF), V((nodes, halos), BF),
            V((nodes, width), F32), V((nodes, width), F32), V((8, ends), F32),
            V((ends, slots), BF), V((slots, ends), BF), V((slots, nodes), BF), V((nodes, slots), BF),
            V((n_dom, SLOTS, width), BF), V((n_zc, n_y, SLOTS, half), BF), V((n_y, n_zc, SLOTS, half), BF),
            V((2, n_y, n_zc, SLOTS, half), BF),
            V((n_dom, SLOTS, width), BF), V((n_zc, n_y, SLOTS, half), BF), V((n_y, n_zc, SLOTS, half), BF),
            V((2, n_y, n_zc, SLOTS, half), BF), V((ends, width), BF),
            V((zrows + 8, width), F32), V((zrows + 8, width), F32),
            V((2, 2, quarter, half), BF), V((2, 2, quarter, half), BF), V((2, quarter, half), BF),
            V((2, quarter, half), BF), V((4, quarter, half), F32),
            V((2, crows + 8, width), F32), V((crows + 8, width), F32),
            V((n_z, zrows + 8, width), F32), V((n_z, zrows + 8, width), F32),
            V((n_y, zrows + 8, width), F32), V((n_x, zrows + 8, width), F32), V((2, n_z, zrows, width), F32),
            pltpu.SemaphoreType.DMA((7,)), pltpu.SemaphoreType.DMA((4,)),
            pltpu.SemaphoreType.DMA((22,)), pltpu.SemaphoreType.DMA((22,)),
        ],
        compiler_params=pltpu.CompilerParams(
            collective_id=0, has_side_effects=True, vmem_limit_bytes=60 * 1024 * 1024
        ),
        name="encode_decode",
    )(
        edge_owner.T, edge_rows.T, halo_rows.T, labels.reshape(1, -1), b_enc.reshape(1, -1), b_dec1.reshape(1, -1),
        w_dec2.reshape(1, -1), feats, history, adj_inner, adj_halo, w_self, w_nbr, w_dec1,
    )
    embed, grad_embed, grad_dec1, vecs = outs
    return embed, grad_embed, grad_dec1, vecs[0], vecs[1]


def solution(mesh):
    placed = (
        P("dom", None), P("dom", None), P("dom", None), P("dom", None), P("dom", None), P(), P(), P(),
        P(("dom", "rep"), None), P(("dom", "rep"), None), P(("dom", "rep")), P(), P(), P(),
    )
    return jax.shard_map(
        per_device,
        mesh=mesh,
        in_specs=placed,
        out_specs=(P("dom", None), P(("dom", "rep"), None), P(), P(), P()),
        check_vma=False,
    )
```

```python
import functools

import jax
import jax.numpy as jnp
from jax import lax
from jax.experimental import pallas as pl
from jax.experimental.pallas import tpu as pltpu
from jax.sharding import PartitionSpec as P

BF = jnp.bfloat16
F32 = jnp.float32
I32 = jnp.int32
MESH = pl.DeviceIdType.MESH
SLOTS = 8
LANES = 128


def log2(value):
    return value.bit_length() - 1


def iota(shape, dim):
    return lax.broadcasted_iota(I32, shape, dim)


def nn(a, b):
    return lax.dot_general(a, b, (((1,), (0,)), ((), ())), preferred_element_type=F32)


def nt(a, b):
    return lax.dot_general(a, b, (((1,), (1,)), ((), ())), preferred_element_type=F32)


def tn(a, b):
    return lax.dot_general(a, b, (((0,), (0,)), ((), ())), preferred_element_type=F32)


def hot(cond):
    return jnp.where(cond, 1.0, 0.0).astype(BF)


def column_of(row):
    n = row.shape[1]
    return jnp.sum(jnp.where(iota((n, n), 0) == iota((n, n), 1), row, 0.0), axis=1, keepdims=True)


def row_of(column):
    n = column.shape[0]
    return jnp.sum(jnp.where(iota((n, n), 0) == iota((n, n), 1), column, 0.0), axis=0, keepdims=True)


def copies(ref, sem):
    return pltpu.make_async_copy(ref, ref, sem)


def kernel(
    n_y, n_zc, n_x,
    eo, er, hr, lab, b_enc, b_dec1, w_dec2,
    feats_h, hist_h, adji_h, adjh_h, wself_h, wnbr_h, wdec1_h,
    emb_o, ge_o, gd_o, gv_o,
    feats, hist, adji, adjh, wself, wnbr, wdec1,
    ids_s, ids_r1, ids_t, ids_r2,
    hal_s, hal_r1, hal_t, hal_r2, adjp,
    inner, selfp, place,
    hot_e, hot_et, hot_g, hot_gt,
    fet_s, fet_a, fet_b, fet_r,
    gra_s, gra_a, gra_b, gra_r, gpair,
    zbuf, dbuf,
    xs1, xr1, xs2, xr2, xk,
    dc_s, dc_r, dz_s, dz_r, dy_r, dx_r, dg_r,
    load_sem, out_sem,
    ssem, rsem,
):
    n_dom = n_y * n_zc
    nodes, width = feats.shape
    half = width // 2
    queries = eo.shape[1]
    ends = 2 * queries
    slots = n_dom * SLOTS
    halos = 2 * n_dom
    n_z = n_zc // 2
    ly, lzc = log2(n_y), log2(n_zc)
    me = lax.axis_index("dom")
    rep = lax.axis_index("rep")
    y = lax.div(me, n_zc)
    zc = lax.rem(me, n_zc)
    z = lax.div(zc, 2)
    core = lax.rem(zc, 2)

    loads = [
        pltpu.make_async_copy(src, dst, load_sem.at[i])
        for i, (src, dst) in enumerate(
            ((feats_h, feats), (adji_h, adji), (wself_h, wself), (adjh_h, adjh), (hist_h, hist), (wnbr_h, wnbr), (wdec1_h, wdec1))
        )
    ]
    for load in loads:
        load.start()

    barrier = pltpu.get_barrier_semaphore()

    def zc_peer(k):
        return lax.rem(zc + k, n_zc)

    def y_peer(k):
        return lax.rem(y + k, n_y)

    def greet_zc(k, carry):
        pl.semaphore_signal(barrier, inc=1, device_id={"dom": y * n_zc + zc_peer(k)}, device_id_type=MESH)
        return carry

    def greet_y(k, carry):
        pl.semaphore_signal(barrier, inc=1, device_id={"dom": y_peer(k) * n_zc + zc}, device_id_type=MESH)
        return carry

    lax.fori_loop(1, n_zc, greet_zc, 0)
    lax.fori_loop(1, n_y, greet_y, 0)
    for k in range(1, n_x):
        pl.semaphore_signal(barrier, inc=1, device_id={"rep": lax.rem(rep + k, n_x)}, device_id_type=MESH)

    sent = []

    def drain():
        for index, size in sent:
            copies(size, ssem.at[index]).wait()

    def along_zc(index, source, target, sent_size):
        def body(k, carry):
            peer = zc_peer(k)
            pltpu.make_async_remote_copy(
                src_ref=source(peer), dst_ref=target(zc), send_sem=ssem.at[index], recv_sem=rsem.at[index],
                device_id={"dom": y * n_zc + peer}, device_id_type=MESH,
            ).start()
            return carry

        lax.fori_loop(1, n_zc, body, 0)
        pltpu.make_async_copy(source(zc), target(zc), rsem.at[index]).start()
        sent.append((index, sent_size))

    def along_y(index, source, target, sent_size):
        def body(k, carry):
            peer = y_peer(k)
            pltpu.make_async_remote_copy(
                src_ref=source(peer), dst_ref=target(y), send_sem=ssem.at[index], recv_sem=rsem.at[index],
                device_id={"dom": peer * n_zc + zc}, device_id_type=MESH,
            ).start()
            return carry

        lax.fori_loop(1, n_y, body, 0)
        pltpu.make_async_copy(source(y), target(y), rsem.at[index]).start()
        sent.append((index, sent_size))

    owner = jnp.concatenate([eo[0:1, :], eo[1:2, :]], axis=1)
    local = jnp.concatenate([er[0:1, :], er[1:2, :]], axis=1)
    rows = iota((n_dom, ends), 0)
    turned = ((rows & (n_y - 1)) << lzc) + (rows >> ly)
    match = owner == turned
    match_hot = hot(match)
    before = hot(iota((ends, ends), 0) < iota((ends, ends), 1))
    rank = nn(match_hot, before)
    slot = jnp.sum(jnp.where(match, rank, 0.0), axis=0, keepdims=True)
    place[...] = jnp.broadcast_to(owner.astype(F32) * float(SLOTS) + slot, place.shape)

    def lane_rows(at, value):
        lane = iota((LANES, value.shape[1]), 0)
        part = jnp.where(lane < 16, value >> 5, value & 31)
        return jnp.where(at & (lane < 32), part.astype(F32), 0.0).astype(BF)

    wanted = lane_rows(slot == (iota((LANES, ends), 0) & 15).astype(F32), local)
    lane = iota((LANES, n_dom), 0) & 15
    halo_ids = jnp.where(lane == SLOTS, hr[0:1, :], hr[1:2, :])
    halo_wanted = lane_rows((lane == SLOTS) | (lane == SLOTS + 1), halo_ids)
    prow, pcol = iota((n_dom, n_dom), 0), iota((n_dom, n_dom), 1)
    to_zc_y = hot(pcol == ((prow & (n_y - 1)) << lzc) + (prow >> ly))
    to_y_zc = hot(pcol == ((prow & (n_zc - 1)) << ly) + (prow >> lzc))
    requests = nt(match_hot, wanted) + nt(to_zc_y, halo_wanted)
    ids_s[...] = requests.astype(BF).reshape(n_zc, n_y, LANES)

    pl.semaphore_wait(barrier, (n_zc - 1) + (n_y - 1) + (n_x - 1))
    along_zc(0, lambda p: ids_s.at[p], lambda m: ids_r1.at[m], ids_s.at[pl.ds(0, n_zc - 1)])

    tile = min(256, nodes)
    loads[0].wait()
    loads[1].wait()

    @pl.loop(0, nodes // tile)
    def _(i):
        at = pl.ds(pl.multiple_of(i * tile, tile), tile)
        inner[at, :] = nn(adji[at, :], feats[...])

    copies(ids_r1, rsem.at[0]).wait()
    ids_t[...] = nn(to_y_zc, ids_r1[...].reshape(n_dom, LANES)).astype(BF).reshape(n_y, n_zc, LANES)
    along_y(1, lambda p: ids_t.at[p], lambda m: ids_r2.at[m], ids_t.at[pl.ds(0, n_y - 1)])

    loads[2].wait()
    loads[3].wait()

    @pl.loop(0, nodes // tile)
    def _(i):
        at = pl.ds(pl.multiple_of(i * tile, tile), tile)
        selfp[at, :] = nn(feats[at, :], wself[...]) + b_enc[...]

    ko, jo = iota((halos, halos), 0), iota((halos, halos), 1)
    std = ((((jo >> (lzc + 1)) << lzc) + (jo & (n_zc - 1))) << 1) + ((jo >> lzc) & 1)
    adjp[...] = nn(adjh[...], hot(ko == std)).astype(BF)

    for i in (4, 5, 6):
        loads[i].wait()

    place_col = column_of(place[0:1, :])
    etile = min(256, ends)
    for i in range(ends // etile):
        hot_e[i * etile : (i + 1) * etile, :] = hot(
            place_col[i * etile : (i + 1) * etile, :] == iota((etile, slots), 1).astype(F32)
        )

    copies(ids_r2, rsem.at[1]).wait()
    asked = nn(to_zc_y, ids_r2[...].reshape(n_dom, LANES))
    for c in range(2):
        at = SLOTS + c
        asked_c = 32.0 * asked[:, at : at + 1] + asked[:, at + 16 : at + 17]
        pick = hot(asked_c == iota((n_dom, nodes), 1).astype(F32))
        hal_s[:, c] = nn(pick, hist[...]).astype(BF).reshape(n_zc, n_y, width)
    along_zc(2, lambda p: hal_s.at[p], lambda m: hal_r1.at[m], hal_s.at[pl.ds(0, n_zc - 1)])

    gtile = min(256, slots)
    per = gtile // SLOTS
    id_rows = []
    for i in range(slots // gtile):
        asked = ids_r2[...].reshape(n_dom, LANES)[i * per : (i + 1) * per].astype(F32)
        spread = jnp.broadcast_to(asked[:, None, :], (per, SLOTS, LANES)).reshape(gtile, LANES)
        lane, mine = iota((gtile, LANES), 1), iota((gtile, LANES), 0) & (SLOTS - 1)
        weight = jnp.where(lane == mine, 32.0, jnp.where(lane == mine + 16, 1.0, 0.0))
        id_col = jnp.sum(spread * weight, axis=1, keepdims=True)
        hot_g[i * gtile : (i + 1) * gtile, :] = hot(id_col == iota((gtile, nodes), 1).astype(F32))
        id_rows.append(row_of(id_col))
    id_row = jnp.concatenate(id_rows, axis=1)

    copies(hal_r1, rsem.at[2]).wait()
    io, oo = iota((halos, halos), 1), iota((halos, halos), 0)
    into = ((oo & (n_zc - 1)) << (ly + 1)) + (((oo >> lzc) & 1) << ly) + (oo >> (lzc + 1))
    hal_t[...] = nn(hot(io == into), hal_r1[...].reshape(halos, width)).astype(BF).reshape(n_y, 2 * n_zc, width)
    along_y(3, lambda p: hal_t.at[p], lambda m: hal_r2.at[m], hal_t.at[pl.ds(0, n_y - 1)])

    @pl.loop(0, nodes // tile)
    def _(i):
        at = pl.ds(pl.multiple_of(i * tile, tile), tile)
        hot_gt[at, :] = hot((iota((tile, slots), 0) + i * tile).astype(F32) == id_row)

    @pl.loop(0, slots // gtile)
    def _(i):
        at = pl.ds(pl.multiple_of(i * gtile, gtile), gtile)
        hot_et[at, :] = hot((iota((gtile, ends), 0) + i * gtile).astype(F32) == place[0:1, :])

    target = column_of(lab[...].astype(F32))

    copies(hal_r2, rsem.at[3]).wait()

    @pl.loop(0, nodes // tile)
    def _(i):
        at = pl.ds(pl.multiple_of(i * tile, tile), tile)
        agg = (inner[at, :] + nn(adjp[at, :], hal_r2[...].reshape(halos, width))).astype(BF)
        emb_o[at, :] = jnp.maximum(selfp[at, :] + nn(agg, wnbr[...]), 0.0).astype(BF)

    @pl.loop(0, slots // gtile)
    def _(i):
        at = pl.ds(pl.multiple_of(i * gtile, gtile), gtile)
        block = nn(hot_g[at, :], emb_o[...]).astype(BF)
        fet_s[pl.ds(i * per, per)] = block.reshape(per, SLOTS, width)

    left, right = pl.ds(0, half), pl.ds(half, half)

    def both_ways(base, send, mid_a, mid_b, recv):
        send4 = send.reshape(n_y, n_zc, SLOTS, width)
        along_zc(base, lambda p: send4.at[:, p, :, left], lambda m: mid_a.at[m], mid_a.at[pl.ds(0, n_zc - 1)])
        along_y(base + 1, lambda p: send4.at[p, :, :, right], lambda m: mid_b.at[m], mid_b.at[pl.ds(0, n_y - 1)])

    def both_ways_on(base, mid_a, mid_b, recv):
        copies(mid_a, rsem.at[base]).wait()
        along_y(base + 2, lambda p: mid_a.at[:, p], lambda m: recv.at[0, m], mid_b.at[pl.ds(0, n_y - 1)])
        copies(mid_b, rsem.at[base + 1]).wait()
        along_zc(base + 3, lambda p: mid_b.at[:, p], lambda m: recv.at[1, :, m], mid_a.at[pl.ds(0, n_zc - 1)])

    both_ways(4, fet_s, fet_a, fet_b, fet_r)
    both_ways_on(4, fet_a, fet_b, fet_r)
    copies(fet_r.at[0], rsem.at[6]).wait()
    copies(fet_r.at[1], rsem.at[7]).wait()

    both = [nn(hot_e[...], fet_r[h].reshape(slots, half)) for h in range(2)]
    head = jnp.concatenate([part[:queries] for part in both], axis=1)
    tail = jnp.concatenate([part[queries:] for part in both], axis=1)
    zprod = (head * tail).astype(BF)
    pre = nn(zprod, wdec1[...]) + b_dec1[...]
    sig = jax.nn.sigmoid(pre)
    hidden = (pre * sig).astype(BF).astype(F32)
    wout = w_dec2[...].astype(F32).reshape(1, width)
    logit = jnp.sum(hidden * wout, axis=1, keepdims=True)
    dlogit = jax.nn.sigmoid(logit) - target
    d_pre = (dlogit * wout * (sig * (1.0 + pre * (1.0 - sig)))).astype(BF)
    dz = nt(d_pre, wdec1[...])
    gpair[:queries, :] = (dz * tail).astype(BF)
    gpair[queries:, :] = (dz * head).astype(BF)

    @pl.loop(0, slots // gtile)
    def _(i):
        at = pl.ds(pl.multiple_of(i * gtile, gtile), gtile)
        block = nn(hot_et[at, :], gpair[...]).astype(BF)
        gra_s[pl.ds(i * per, per)] = block.reshape(per, SLOTS, width)

    both_ways(8, gra_s, gra_a, gra_b, gra_r)

    grad1 = tn(zprod, d_pre)
    gb1 = jnp.sum(d_pre.astype(F32), axis=0, keepdims=True)
    gd2 = jnp.sum(hidden * dlogit, axis=0, keepdims=True)
    vrow = iota((8, width), 0)
    vecs = jnp.where(vrow == 0, gb1, jnp.where(vrow == 1, gd2, 0.0))
    crows = width // 2
    zrows = crows // n_z
    for h in range(2):
        dc_s[h, :crows] = grad1[h * crows : (h + 1) * crows]
        dc_s[h, crows:] = vecs
    other = 1 - core
    pair = pltpu.make_async_remote_copy(
        src_ref=dc_s.at[other], dst_ref=dc_r, send_sem=ssem.at[12], recv_sem=rsem.at[12],
        device_id={"dom": y * n_zc + 2 * z + other}, device_id_type=MESH,
    )
    pair.start()

    def along_z(index, source, goal, sent_size):
        def body(k, carry):
            peer = lax.rem(z + k, n_z)
            pltpu.make_async_remote_copy(
                src_ref=source(peer), dst_ref=goal(z), send_sem=ssem.at[index], recv_sem=rsem.at[index],
                device_id={"dom": y * n_zc + 2 * peer + core}, device_id_type=MESH,
            ).start()
            return carry

        lax.fori_loop(1, n_z, body, 0)
        pltpu.make_async_copy(source(z), goal(z), rsem.at[index]).start()
        sent.append((index, sent_size))

    pair.wait_recv()
    for j in range(n_z):
        dz_s[j, :zrows] = dc_s[core, j * zrows : (j + 1) * zrows] + dc_r[j * zrows : (j + 1) * zrows]
        dz_s[j, zrows:] = dc_s[core, crows:] + dc_r[crows:]
    along_z(13, lambda p: dz_s.at[p], lambda m: dz_r.at[m], dz_s.at[pl.ds(0, n_z - 1)])

    both_ways_on(8, gra_a, gra_b, gra_r)

    copies(dz_r, rsem.at[13]).wait()
    total = dz_r[0]
    for j in range(1, n_z):
        total = total + dz_r[j]
    zbuf[...] = total
    along_y(14, lambda p: zbuf, lambda m: dy_r.at[m], dy_r.at[pl.ds(0, n_y - 1)])

    copies(dy_r, rsem.at[14]).wait()
    total = dy_r[0]
    for j in range(1, n_y):
        total = total + dy_r[j]
    dbuf[...] = total
    for k in range(1, n_x):
        pltpu.make_async_remote_copy(
            src_ref=dbuf, dst_ref=dx_r.at[rep], send_sem=ssem.at[15], recv_sem=rsem.at[15],
            device_id={"rep": lax.rem(rep + k, n_x)}, device_id_type=MESH,
        ).start()
    pltpu.make_async_copy(dbuf, dx_r.at[rep], rsem.at[15]).start()
    sent.append((15, dx_r.at[pl.ds(0, n_x - 1)]))

    flip = rep + 1 - 2 * lax.rem(rep, 2)
    wrap = 3 - rep
    wflip = wrap + 1 - 2 * lax.rem(wrap, 2)
    quarter = nodes // n_x
    jtile = min(64, quarter)

    def local_sum(q, cols):
        at = pl.ds(pl.multiple_of(q * quarter, quarter), quarter)
        return nn(hot_gt[at, :], gra_r[cols].reshape(slots, half))

    def trade(index, source, goal, partner):
        copy = pltpu.make_async_remote_copy(
            src_ref=source, dst_ref=goal, send_sem=ssem.at[index], recv_sem=rsem.at[index],
            device_id={"rep": partner}, device_id_type=MESH,
        )
        copy.start()
        return copy

    def joined(way, part):
        @pl.loop(0, quarter // jtile)
        def _(i):
            at = pl.ds(pl.multiple_of(i * jtile, jtile), jtile)
            xs2[way, at, :] = (xk[part, at, :] + xr1[way, 1, at, :].astype(F32)).astype(BF)

    copies(gra_r.at[0], rsem.at[10]).wait()
    xs1[0, 0] = local_sum(flip, 0).astype(BF)
    xs1[0, 1] = local_sum(wflip, 0).astype(BF)
    one = trade(16, xs1.at[0], xr1.at[0], flip)
    copies(gra_r.at[1], rsem.at[11]).wait()
    xs1[1, 0] = local_sum(wrap, 1).astype(BF)
    xs1[1, 1] = local_sum(wflip, 1).astype(BF)
    two = trade(17, xs1.at[1], xr1.at[1], wrap)
    xk[0] = local_sum(rep, 0)
    xk[1] = local_sum(rep, 1)
    xk[2] = local_sum(wrap, 0)
    xk[3] = local_sum(flip, 1)
    one.wait_recv()
    joined(0, 2)
    three = trade(18, xs2.at[0], xr2.at[0], wrap)
    two.wait_recv()
    joined(1, 3)
    four = trade(19, xs2.at[1], xr2.at[1], flip)

    copies(dx_r, rsem.at[15]).wait()
    total = dx_r[0]
    for j in range(1, n_x):
        total = total + dx_r[j]
    zbuf2 = total[:zrows]
    gv_o[...] = total[zrows:]
    dc_r[:zrows] = zbuf2
    along_z(20, lambda p: dc_r.at[pl.ds(0, zrows)], lambda m: dg_r.at[core, m], dg_r.at[0, pl.ds(0, n_z - 1)])

    three.wait_recv()
    ge_o[:, :half] = xk[0] + xr1[0, 0].astype(F32) + xr2[0].astype(F32)
    four.wait_recv()
    ge_o[:, half:] = xk[1] + xr1[1, 0].astype(F32) + xr2[1].astype(F32)

    copies(dg_r.at[0], rsem.at[20]).wait()
    last = pltpu.make_async_remote_copy(
        src_ref=dg_r.at[core], dst_ref=dg_r.at[core], send_sem=ssem.at[21], recv_sem=rsem.at[21],
        device_id={"dom": y * n_zc + 2 * z + other}, device_id_type=MESH,
    )
    last.start()

    drain()
    pair.wait_send()
    for copy in (one, two, three, four):
        copy.wait_send()
    last.wait()
    gd_o[...] = dg_r[...].reshape(width, width)


def put_out(emb, ge, gd, gv, emb_h, ge_h, gd_h, gb_h, g2_h, sem):
    pairs = ((emb, emb_h), (ge, ge_h), (gd, gd_h), (gv.at[pl.ds(0, 1)], gb_h), (gv.at[pl.ds(1, 1)], g2_h))
    copies_out = [pltpu.make_async_copy(src, dst, sem.at[i]) for i, (src, dst) in enumerate(pairs)]
    for copy in copies_out:
        copy.start()
    for copy in copies_out:
        copy.wait()


def per_device(
    feats, history, adj_inner, adj_halo, halo_rows, w_self, w_nbr, b_enc,
    edge_owner, edge_rows, labels, w_dec1, b_dec1, w_dec2,
):
    n_dom, n_x = lax.axis_size("dom"), lax.axis_size("rep")
    n_zc = 16 if n_dom == 128 else 4
    n_y = n_dom // n_zc
    nodes, width = feats.shape
    halos = adj_halo.shape[1]
    queries = edge_owner.shape[0]
    ends = 2 * queries
    slots = n_dom * SLOTS
    half = width // 2
    n_z = n_zc // 2
    quarter = nodes // n_x
    crows = width // 2
    zrows = crows // n_z
    vmem = pl.BlockSpec(memory_space=pltpu.VMEM)
    any_ = pl.BlockSpec(memory_space=pl.ANY)
    V = pltpu.VMEM
    outs = pl.pallas_call(
        functools.partial(kernel, n_y, n_zc, n_x),
        out_shape=(
            V((nodes, width), BF),
            V((quarter, width), F32),
            V((width, width), F32),
            V((8, width), F32),
        ),
        in_specs=[vmem] * 7 + [any_] * 7,
        out_specs=(vmem,) * 4,
        scratch_shapes=[
            V((nodes, width), BF), V((nodes, width), BF), V((nodes, nodes), BF), V((nodes, halos), BF),
            V((width, width), BF), V((width, width), BF), V((width, width), BF),
            V((n_zc, n_y, LANES), BF), V((n_zc, n_y, LANES), BF), V((n_y, n_zc, LANES), BF), V((n_y, n_zc, LANES), BF),
            V((n_zc, 2, n_y, width), BF), V((n_zc, 2, n_y, width), BF), V((n_y, 2 * n_zc, width), BF),
            V((n_y, 2 * n_zc, width), BF), V((nodes, halos), BF),
            V((nodes, width), F32), V((nodes, width), F32), V((8, ends), F32),
            V((ends, slots), BF), V((slots, ends), BF), V((slots, nodes), BF), V((nodes, slots), BF),
            V((n_dom, SLOTS, width), BF), V((n_zc, n_y, SLOTS, half), BF), V((n_y, n_zc, SLOTS, half), BF),
            V((2, n_y, n_zc, SLOTS, half), BF),
            V((n_dom, SLOTS, width), BF), V((n_zc, n_y, SLOTS, half), BF), V((n_y, n_zc, SLOTS, half), BF),
            V((2, n_y, n_zc, SLOTS, half), BF), V((ends, width), BF),
            V((zrows + 8, width), F32), V((zrows + 8, width), F32),
            V((2, 2, quarter, half), BF), V((2, 2, quarter, half), BF), V((2, quarter, half), BF),
            V((2, quarter, half), BF), V((4, quarter, half), F32),
            V((2, crows + 8, width), F32), V((crows + 8, width), F32),
            V((n_z, zrows + 8, width), F32), V((n_z, zrows + 8, width), F32),
            V((n_y, zrows + 8, width), F32), V((n_x, zrows + 8, width), F32), V((2, n_z, zrows, width), F32),
            pltpu.SemaphoreType.DMA((7,)), pltpu.SemaphoreType.DMA((4,)),
            pltpu.SemaphoreType.DMA((22,)), pltpu.SemaphoreType.DMA((22,)),
        ],
        compiler_params=pltpu.CompilerParams(
            collective_id=0, has_side_effects=True, vmem_limit_bytes=60 * 1024 * 1024
        ),
        name="encode_decode",
    )(
        edge_owner.T, edge_rows.T, halo_rows.T, labels.reshape(1, -1), b_enc.reshape(1, -1), b_dec1.reshape(1, -1),
        w_dec2, feats, history, adj_inner, adj_halo, w_self, w_nbr, w_dec1,
    )
    shapes = ((nodes, width, BF), (quarter, width, F32), (width, width, F32), (1, width, F32), (1, width, F32))
    embed, grad_embed, grad_dec1, bias1, dec2 = pl.pallas_call(
        put_out,
        out_shape=tuple(jax.ShapeDtypeStruct(shape[:2], shape[2]) for shape in shapes),
        in_specs=[vmem] * 4,
        out_specs=(any_,) * 5,
        scratch_shapes=[pltpu.SemaphoreType.DMA((5,))],
        name="put_out",
    )(*[pltpu.with_memory_space_constraint(out, pltpu.VMEM) for out in outs])
    return embed, grad_embed, grad_dec1, bias1.reshape(-1), dec2.reshape(-1)


def solution(mesh):
    placed = (
        P("dom", None), P("dom", None), P("dom", None), P("dom", None), P("dom", None), P(), P(), P(),
        P(("dom", "rep"), None), P(("dom", "rep"), None), P(("dom", "rep")), P(), P(), P(),
    )
    return jax.shard_map(
        per_device,
        mesh=mesh,
        in_specs=placed,
        out_specs=(P("dom", None), P(("dom", "rep"), None), P(), P(), P()),
        check_vma=False,
    )
```

```python
import functools

import jax
import jax.numpy as jnp
from jax import lax
from jax.experimental import pallas as pl
from jax.experimental.pallas import tpu as pltpu
from jax.sharding import PartitionSpec as P

BF = jnp.bfloat16
F32 = jnp.float32
I32 = jnp.int32
MESH = pl.DeviceIdType.MESH
SLOTS = 8
LANES = 128


def log2(value):
    return value.bit_length() - 1


def iota(shape, dim):
    return lax.broadcasted_iota(I32, shape, dim)


def nn(a, b):
    return lax.dot_general(a, b, (((1,), (0,)), ((), ())), preferred_element_type=F32)


def nt(a, b):
    return lax.dot_general(a, b, (((1,), (1,)), ((), ())), preferred_element_type=F32)


def tn(a, b):
    return lax.dot_general(a, b, (((0,), (0,)), ((), ())), preferred_element_type=F32)


def hot(cond):
    return jnp.where(cond, 1.0, 0.0).astype(BF)


def column_of(row):
    n = row.shape[1]
    return jnp.sum(jnp.where(iota((n, n), 0) == iota((n, n), 1), row, 0.0), axis=1, keepdims=True)


def row_of(column):
    n = column.shape[0]
    return jnp.sum(jnp.where(iota((n, n), 0) == iota((n, n), 1), column, 0.0), axis=0, keepdims=True)


def copies(ref, sem):
    return pltpu.make_async_copy(ref, ref, sem)


def kernel(
    n_y, n_zc, n_x,
    eo, er, hr, lab, b_enc, b_dec1, w_dec2,
    feats_h, hist_h, adji_h, adjh_h, wself_h, wnbr_h, wdec1_h,
    emb_o, ge_o, gd_o, gv_o,
    feats, hist, adji, adjh, wself, wnbr, wdec1,
    ids_s, ids_r1, ids_t, ids_r2,
    hal_s, hal_r1, hal_t, hal_r2, hal_m, hal_u, hal_v, hal_w, halo, adjp,
    inner, selfp, place,
    hot_e, hot_et, hot_g, hot_gt,
    fet_s, fet_a, fet_b, fet_r,
    gra_s, gra_a, gra_b, gra_r, gpair,
    zbuf, dbuf,
    xs1, xr1, xs2, xr2, xk,
    dc_s, dc_r, dz_s, dz_r, dy_r, dx_r, dg_r,
    load_sem, out_sem,
    ssem, rsem,
):
    n_dom = n_y * n_zc
    nodes, width = feats.shape
    half = width // 2
    queries = eo.shape[1]
    ends = 2 * queries
    slots = n_dom * SLOTS
    halos = 2 * n_dom
    n_z = n_zc // 2
    ly, lzc = log2(n_y), log2(n_zc)
    me = lax.axis_index("dom")
    rep = lax.axis_index("rep")
    y = lax.div(me, n_zc)
    zc = lax.rem(me, n_zc)
    z = lax.div(zc, 2)
    core = lax.rem(zc, 2)

    loads = [
        pltpu.make_async_copy(src, dst, load_sem.at[i])
        for i, (src, dst) in enumerate(
            ((feats_h, feats), (adji_h, adji), (wself_h, wself), (adjh_h, adjh), (hist_h, hist), (wnbr_h, wnbr), (wdec1_h, wdec1))
        )
    ]
    for load in loads:
        load.start()

    barrier = pltpu.get_barrier_semaphore()

    def zc_peer(k):
        return lax.rem(zc + k, n_zc)

    def y_peer(k):
        return lax.rem(y + k, n_y)

    def greet_zc(k, carry):
        pl.semaphore_signal(barrier, inc=1, device_id={"dom": y * n_zc + zc_peer(k)}, device_id_type=MESH)
        return carry

    def greet_y(k, carry):
        pl.semaphore_signal(barrier, inc=1, device_id={"dom": y_peer(k) * n_zc + zc}, device_id_type=MESH)
        return carry

    lax.fori_loop(1, n_zc, greet_zc, 0)
    lax.fori_loop(1, n_y, greet_y, 0)
    for k in range(1, n_x):
        pl.semaphore_signal(barrier, inc=1, device_id={"rep": lax.rem(rep + k, n_x)}, device_id_type=MESH)

    sent = []

    def drain():
        for index, size in sent:
            copies(size, ssem.at[index]).wait()

    def along_zc(index, source, target, sent_size):
        def body(k, carry):
            peer = zc_peer(k)
            pltpu.make_async_remote_copy(
                src_ref=source(peer), dst_ref=target(zc), send_sem=ssem.at[index], recv_sem=rsem.at[index],
                device_id={"dom": y * n_zc + peer}, device_id_type=MESH,
            ).start()
            return carry

        lax.fori_loop(1, n_zc, body, 0)
        pltpu.make_async_copy(source(zc), target(zc), rsem.at[index]).start()
        sent.append((index, sent_size))

    def along_y(index, source, target, sent_size):
        def body(k, carry):
            peer = y_peer(k)
            pltpu.make_async_remote_copy(
                src_ref=source(peer), dst_ref=target(y), send_sem=ssem.at[index], recv_sem=rsem.at[index],
                device_id={"dom": peer * n_zc + zc}, device_id_type=MESH,
            ).start()
            return carry

        lax.fori_loop(1, n_y, body, 0)
        pltpu.make_async_copy(source(y), target(y), rsem.at[index]).start()
        sent.append((index, sent_size))

    owner = jnp.concatenate([eo[0:1, :], eo[1:2, :]], axis=1)
    local = jnp.concatenate([er[0:1, :], er[1:2, :]], axis=1)
    rows = iota((n_dom, ends), 0)
    turned = ((rows & (n_y - 1)) << lzc) + (rows >> ly)
    match = owner == turned
    match_hot = hot(match)
    before = hot(iota((ends, ends), 0) < iota((ends, ends), 1))
    rank = nn(match_hot, before)
    slot = jnp.sum(jnp.where(match, rank, 0.0), axis=0, keepdims=True)
    place[...] = jnp.broadcast_to(owner.astype(F32) * float(SLOTS) + slot, place.shape)

    def lane_rows(at, value):
        lane = iota((LANES, value.shape[1]), 0)
        part = jnp.where(lane < 16, value >> 5, value & 31)
        return jnp.where(at & (lane < 32), part.astype(F32), 0.0).astype(BF)

    wanted = lane_rows(slot == (iota((LANES, ends), 0) & 15).astype(F32), local)
    lane = iota((LANES, n_dom), 0) & 15
    halo_ids = jnp.where(lane == SLOTS, hr[0:1, :], hr[1:2, :])
    halo_wanted = lane_rows((lane == SLOTS) | (lane == SLOTS + 1), halo_ids)
    prow, pcol = iota((n_dom, n_dom), 0), iota((n_dom, n_dom), 1)
    to_zc_y = hot(pcol == ((prow & (n_y - 1)) << lzc) + (prow >> ly))
    to_y_zc = hot(pcol == ((prow & (n_zc - 1)) << ly) + (prow >> lzc))
    requests = nt(match_hot, wanted) + nt(to_zc_y, halo_wanted)
    ids_s[...] = requests.astype(BF).reshape(n_zc, n_y, LANES)

    pl.semaphore_wait(barrier, (n_zc - 1) + (n_y - 1) + (n_x - 1))
    along_zc(0, lambda p: ids_s.at[p], lambda m: ids_r1.at[m], ids_s.at[pl.ds(0, n_zc - 1)])

    tile = min(256, nodes)
    loads[0].wait()
    loads[1].wait()

    @pl.loop(0, nodes // tile)
    def _(i):
        at = pl.ds(pl.multiple_of(i * tile, tile), tile)
        inner[at, :] = nn(adji[at, :], feats[...])

    copies(ids_r1, rsem.at[0]).wait()
    ids_t[...] = nn(to_y_zc, ids_r1[...].reshape(n_dom, LANES)).astype(BF).reshape(n_y, n_zc, LANES)
    along_y(1, lambda p: ids_t.at[p], lambda m: ids_r2.at[m], ids_t.at[pl.ds(0, n_y - 1)])

    loads[2].wait()
    loads[3].wait()

    @pl.loop(0, nodes // tile)
    def _(i):
        at = pl.ds(pl.multiple_of(i * tile, tile), tile)
        selfp[at, :] = nn(feats[at, :], wself[...]) + b_enc[...]

    ko, jo = iota((halos, halos), 0), iota((halos, halos), 1)
    std = ((((jo >> (lzc + 1)) << lzc) + (jo & (n_zc - 1))) << 1) + ((jo >> lzc) & 1)
    adjp[...] = nn(adjh[...], hot(ko == std)).astype(BF)

    for i in (4, 5, 6):
        loads[i].wait()

    place_col = column_of(place[0:1, :])
    etile = min(256, ends)
    for i in range(ends // etile):
        hot_e[i * etile : (i + 1) * etile, :] = hot(
            place_col[i * etile : (i + 1) * etile, :] == iota((etile, slots), 1).astype(F32)
        )

    copies(ids_r2, rsem.at[1]).wait()
    asked = nn(to_zc_y, ids_r2[...].reshape(n_dom, LANES))
    for c in range(2):
        at = SLOTS + c
        asked_c = 32.0 * asked[:, at : at + 1] + asked[:, at + 16 : at + 17]
        pick = hot(asked_c == iota((n_dom, nodes), 1).astype(F32))
        picked = nn(pick, hist[...]).astype(BF)
        hal_s[:, c] = picked[:, :half].reshape(n_zc, n_y, half)
        hal_m[:, c] = picked[:, half:].reshape(n_zc, n_y, half)
    along_zc(2, lambda p: hal_s.at[p], lambda m: hal_r1.at[m], hal_s.at[pl.ds(0, n_zc - 1)])
    io, oo = iota((halos, halos), 1), iota((halos, halos), 0)
    turn = hot(io == ((oo & (n_zc - 1)) << (ly + 1)) + (((oo >> lzc) & 1) << ly) + (oo >> (lzc + 1)))
    back = hot(io == ((oo & (n_y - 1)) << (lzc + 1)) + (((oo >> ly) & 1) << lzc) + (oo >> (ly + 1)))
    hal_u[...] = nn(turn, hal_m[...].reshape(halos, half)).astype(BF).reshape(n_y, 2 * n_zc, half)
    along_y(22, lambda p: hal_u.at[p], lambda m: hal_v.at[m], hal_u.at[pl.ds(0, n_y - 1)])

    gtile = min(256, slots)
    per = gtile // SLOTS
    id_rows = []
    for i in range(slots // gtile):
        asked = ids_r2[...].reshape(n_dom, LANES)[i * per : (i + 1) * per].astype(F32)
        spread = jnp.broadcast_to(asked[:, None, :], (per, SLOTS, LANES)).reshape(gtile, LANES)
        lane, mine = iota((gtile, LANES), 1), iota((gtile, LANES), 0) & (SLOTS - 1)
        weight = jnp.where(lane == mine, 32.0, jnp.where(lane == mine + 16, 1.0, 0.0))
        id_col = jnp.sum(spread * weight, axis=1, keepdims=True)
        hot_g[i * gtile : (i + 1) * gtile, :] = hot(id_col == iota((gtile, nodes), 1).astype(F32))
        id_rows.append(row_of(id_col))
    id_row = jnp.concatenate(id_rows, axis=1)

    copies(hal_r1, rsem.at[2]).wait()
    hal_t[...] = nn(turn, hal_r1[...].reshape(halos, half)).astype(BF).reshape(n_y, 2 * n_zc, half)
    along_y(3, lambda p: hal_t.at[p], lambda m: hal_r2.at[m], hal_t.at[pl.ds(0, n_y - 1)])
    copies(hal_v, rsem.at[22]).wait()
    hal_m[...] = nn(back, hal_v[...].reshape(halos, half)).astype(BF).reshape(n_zc, 2, n_y, half)
    along_zc(23, lambda p: hal_m.at[p], lambda m: hal_w.at[m], hal_m.at[pl.ds(0, n_zc - 1)])

    @pl.loop(0, nodes // tile)
    def _(i):
        at = pl.ds(pl.multiple_of(i * tile, tile), tile)
        hot_gt[at, :] = hot((iota((tile, slots), 0) + i * tile).astype(F32) == id_row)

    @pl.loop(0, slots // gtile)
    def _(i):
        at = pl.ds(pl.multiple_of(i * gtile, gtile), gtile)
        hot_et[at, :] = hot((iota((gtile, ends), 0) + i * gtile).astype(F32) == place[0:1, :])

    target = column_of(lab[...].astype(F32))

    copies(hal_r2, rsem.at[3]).wait()
    copies(hal_w, rsem.at[23]).wait()
    halo[:, :half] = hal_r2[...].reshape(halos, half)
    halo[:, half:] = nn(turn, hal_w[...].reshape(halos, half)).astype(BF)

    @pl.loop(0, nodes // tile)
    def _(i):
        at = pl.ds(pl.multiple_of(i * tile, tile), tile)
        agg = (inner[at, :] + nn(adjp[at, :], halo[...])).astype(BF)
        emb_o[at, :] = jnp.maximum(selfp[at, :] + nn(agg, wnbr[...]), 0.0).astype(BF)

    @pl.loop(0, slots // gtile)
    def _(i):
        at = pl.ds(pl.multiple_of(i * gtile, gtile), gtile)
        block = nn(hot_g[at, :], emb_o[...]).astype(BF)
        fet_s[pl.ds(i * per, per)] = block.reshape(per, SLOTS, width)

    left, right = pl.ds(0, half), pl.ds(half, half)

    def both_ways(base, send, mid_a, mid_b, recv):
        send4 = send.reshape(n_y, n_zc, SLOTS, width)
        along_zc(base, lambda p: send4.at[:, p, :, left], lambda m: mid_a.at[m], mid_a.at[pl.ds(0, n_zc - 1)])
        along_y(base + 1, lambda p: send4.at[p, :, :, right], lambda m: mid_b.at[m], mid_b.at[pl.ds(0, n_y - 1)])

    def both_ways_on(base, mid_a, mid_b, recv):
        copies(mid_a, rsem.at[base]).wait()
        along_y(base + 2, lambda p: mid_a.at[:, p], lambda m: recv.at[m, :, :, left], mid_b.at[pl.ds(0, n_y - 1)])
        copies(mid_b, rsem.at[base + 1]).wait()
        along_zc(base + 3, lambda p: mid_b.at[:, p], lambda m: recv.at[:, m, :, right], mid_a.at[pl.ds(0, n_zc - 1)])

    both_ways(4, fet_s, fet_a, fet_b, fet_r)
    both_ways_on(4, fet_a, fet_b, fet_r)
    copies(fet_r.at[:, :, :, left], rsem.at[6]).wait()
    copies(fet_r.at[:, :, :, right], rsem.at[7]).wait()

    got = fet_r[...].reshape(slots, width)
    head = nn(hot_e[:queries, :], got)
    tail = nn(hot_e[queries:, :], got)
    zprod = (head * tail).astype(BF)
    pre = nn(zprod, wdec1[...]) + b_dec1[...]
    sig = jax.nn.sigmoid(pre)
    hidden = (pre * sig).astype(BF).astype(F32)
    wout = w_dec2[...].astype(F32).reshape(1, width)
    logit = jnp.sum(hidden * wout, axis=1, keepdims=True)
    dlogit = jax.nn.sigmoid(logit) - target
    d_pre = (dlogit * wout * (sig * (1.0 + pre * (1.0 - sig)))).astype(BF)
    grad1 = tn(zprod, d_pre)
    gb1 = jnp.sum(d_pre.astype(F32), axis=0, keepdims=True)
    gd2 = jnp.sum(hidden * dlogit, axis=0, keepdims=True)
    vrow = iota((8, width), 0)
    vecs = jnp.where(vrow == 0, gb1, jnp.where(vrow == 1, gd2, 0.0))
    crows = width // 2
    zrows = crows // n_z
    for h in range(2):
        dc_s[h, :crows] = grad1[h * crows : (h + 1) * crows]
        dc_s[h, crows:] = vecs
    other = 1 - core
    pair = pltpu.make_async_remote_copy(
        src_ref=dc_s.at[other], dst_ref=dc_r, send_sem=ssem.at[12], recv_sem=rsem.at[12],
        device_id={"dom": y * n_zc + 2 * z + other}, device_id_type=MESH,
    )
    pair.start()

    def along_z(index, source, goal, sent_size):
        def body(k, carry):
            peer = lax.rem(z + k, n_z)
            pltpu.make_async_remote_copy(
                src_ref=source(peer), dst_ref=goal(z), send_sem=ssem.at[index], recv_sem=rsem.at[index],
                device_id={"dom": y * n_zc + 2 * peer + core}, device_id_type=MESH,
            ).start()
            return carry

        lax.fori_loop(1, n_z, body, 0)
        pltpu.make_async_copy(source(z), goal(z), rsem.at[index]).start()
        sent.append((index, sent_size))

    dz = nt(d_pre, wdec1[...])
    gpair[:queries, :] = (dz * tail).astype(BF)
    gpair[queries:, :] = (dz * head).astype(BF)

    @pl.loop(0, slots // gtile)
    def _(i):
        at = pl.ds(pl.multiple_of(i * gtile, gtile), gtile)
        block = nn(hot_et[at, :], gpair[...]).astype(BF)
        gra_s[pl.ds(i * per, per)] = block.reshape(per, SLOTS, width)

    gra_s4 = gra_s.reshape(n_y, n_zc, SLOTS, width)
    along_y(9, lambda p: gra_s4.at[p, :, :, right], lambda m: gra_b.at[m], gra_b.at[pl.ds(0, n_y - 1)])

    pair.wait_recv()
    for j in range(n_z):
        dz_s[j, :zrows] = (dc_s[core, j * zrows : (j + 1) * zrows] + dc_r[j * zrows : (j + 1) * zrows]).astype(BF)
        dz_s[j, zrows:] = (dc_s[core, crows:] + dc_r[crows:]).astype(BF)
    along_z(13, lambda p: dz_s.at[p], lambda m: dz_r.at[m], dz_s.at[pl.ds(0, n_z - 1)])

    along_zc(8, lambda p: gra_s4.at[:, p, :, left], lambda m: gra_a.at[m], gra_a.at[pl.ds(0, n_zc - 1)])

    copies(dz_r, rsem.at[13]).wait()
    total = dz_r[0].astype(F32)
    for j in range(1, n_z):
        total = total + dz_r[j].astype(F32)
    zbuf[...] = total.astype(BF)
    along_y(14, lambda p: zbuf, lambda m: dy_r.at[m], dy_r.at[pl.ds(0, n_y - 1)])

    both_ways_on(8, gra_a, gra_b, gra_r)

    copies(dy_r, rsem.at[14]).wait()
    total = dy_r[0].astype(F32)
    for j in range(1, n_y):
        total = total + dy_r[j].astype(F32)
    dbuf[...] = total
    for k in range(1, n_x):
        pltpu.make_async_remote_copy(
            src_ref=dbuf, dst_ref=dx_r.at[rep], send_sem=ssem.at[15], recv_sem=rsem.at[15],
            device_id={"rep": lax.rem(rep + k, n_x)}, device_id_type=MESH,
        ).start()
    pltpu.make_async_copy(dbuf, dx_r.at[rep], rsem.at[15]).start()
    sent.append((15, dx_r.at[pl.ds(0, n_x - 1)]))

    copies(dx_r, rsem.at[15]).wait()
    total = dx_r[0]
    for j in range(1, n_x):
        total = total + dx_r[j]
    gv_o[...] = total[zrows:]
    dc_r[:zrows] = total[:zrows]
    along_z(20, lambda p: dc_r.at[pl.ds(0, zrows)], lambda m: dg_r.at[core, m], dg_r.at[0, pl.ds(0, n_z - 1)])

    flip = rep + 1 - 2 * lax.rem(rep, 2)
    wrap = 3 - rep
    wflip = wrap + 1 - 2 * lax.rem(wrap, 2)
    quarter = nodes // n_x
    jtile = min(64, quarter)

    def local_sum(q):
        at = pl.ds(pl.multiple_of(q * quarter, quarter), quarter)
        return nn(hot_gt[at, :], gra_r[...].reshape(slots, width))

    def trade(index, source, goal, partner):
        copy = pltpu.make_async_remote_copy(
            src_ref=source, dst_ref=goal, send_sem=ssem.at[index], recv_sem=rsem.at[index],
            device_id={"rep": partner}, device_id_type=MESH,
        )
        copy.start()
        return copy

    def joined(way, part):
        @pl.loop(0, quarter // jtile)
        def _(i):
            at = pl.ds(pl.multiple_of(i * jtile, jtile), jtile)
            xs2[way, at, :] = (xk[part, at, :] + xr1[way, 1, at, :].astype(F32)).astype(BF)

    copies(gra_r.at[:, :, :, left], rsem.at[10]).wait()
    copies(gra_r.at[:, :, :, right], rsem.at[11]).wait()
    part = local_sum(wflip)
    xs1[0, 1] = part[:, :half].astype(BF)
    xs1[1, 1] = part[:, half:].astype(BF)
    part = local_sum(flip)
    xs1[0, 0] = part[:, :half].astype(BF)
    one = trade(16, xs1.at[0], xr1.at[0], flip)
    xk[3] = part[:, half:]
    part = local_sum(wrap)
    xs1[1, 0] = part[:, half:].astype(BF)
    two = trade(17, xs1.at[1], xr1.at[1], wrap)
    xk[2] = part[:, :half]
    part = local_sum(rep)
    xk[0] = part[:, :half]
    xk[1] = part[:, half:]
    one.wait_recv()
    joined(0, 2)
    three = trade(18, xs2.at[0], xr2.at[0], wrap)
    two.wait_recv()
    joined(1, 3)
    four = trade(19, xs2.at[1], xr2.at[1], flip)

    three.wait_recv()
    ge_o[:, :half] = xk[0] + xr1[0, 0].astype(F32) + xr2[0].astype(F32)
    four.wait_recv()
    ge_o[:, half:] = xk[1] + xr1[1, 0].astype(F32) + xr2[1].astype(F32)

    copies(dg_r.at[0], rsem.at[20]).wait()
    last = pltpu.make_async_remote_copy(
        src_ref=dg_r.at[core], dst_ref=dg_r.at[core], send_sem=ssem.at[21], recv_sem=rsem.at[21],
        device_id={"dom": y * n_zc + 2 * z + other}, device_id_type=MESH,
    )
    last.start()

    drain()
    pair.wait_send()
    for copy in (one, two, three, four):
        copy.wait_send()
    last.wait()
    gd_o[...] = dg_r[...].reshape(width, width)


def put_out(emb, ge, gd, gv, emb_h, ge_h, gd_h, gb_h, g2_h, sem):
    pairs = ((emb, emb_h), (ge, ge_h), (gd, gd_h), (gv.at[pl.ds(0, 1)], gb_h), (gv.at[pl.ds(1, 1)], g2_h))
    copies_out = [pltpu.make_async_copy(src, dst, sem.at[i]) for i, (src, dst) in enumerate(pairs)]
    for copy in copies_out:
        copy.start()
    for copy in copies_out:
        copy.wait()


def per_device(
    feats, history, adj_inner, adj_halo, halo_rows, w_self, w_nbr, b_enc,
    edge_owner, edge_rows, labels, w_dec1, b_dec1, w_dec2,
):
    n_dom, n_x = lax.axis_size("dom"), lax.axis_size("rep")
    n_zc = 16 if n_dom == 128 else 4
    n_y = n_dom // n_zc
    nodes, width = feats.shape
    halos = adj_halo.shape[1]
    queries = edge_owner.shape[0]
    ends = 2 * queries
    slots = n_dom * SLOTS
    half = width // 2
    n_z = n_zc // 2
    quarter = nodes // n_x
    crows = width // 2
    zrows = crows // n_z
    vmem = pl.BlockSpec(memory_space=pltpu.VMEM)
    any_ = pl.BlockSpec(memory_space=pl.ANY)
    V = pltpu.VMEM
    outs = pl.pallas_call(
        functools.partial(kernel, n_y, n_zc, n_x),
        out_shape=(
            V((nodes, width), BF),
            V((quarter, width), F32),
            V((width, width), F32),
            V((8, width), F32),
        ),
        in_specs=[vmem] * 7 + [any_] * 7,
        out_specs=(vmem,) * 4,
        scratch_shapes=[
            V((nodes, width), BF), V((nodes, width), BF), V((nodes, nodes), BF), V((nodes, halos), BF),
            V((width, width), BF), V((width, width), BF), V((width, width), BF),
            V((n_zc, n_y, LANES), BF), V((n_zc, n_y, LANES), BF), V((n_y, n_zc, LANES), BF), V((n_y, n_zc, LANES), BF),
            V((n_zc, 2, n_y, half), BF), V((n_zc, 2, n_y, half), BF), V((n_y, 2 * n_zc, half), BF),
            V((n_y, 2 * n_zc, half), BF), V((n_zc, 2, n_y, half), BF), V((n_y, 2 * n_zc, half), BF),
            V((n_y, 2 * n_zc, half), BF), V((n_zc, 2, n_y, half), BF), V((halos, width), BF), V((nodes, halos), BF),
            V((nodes, width), F32), V((nodes, width), F32), V((8, ends), F32),
            V((ends, slots), BF), V((slots, ends), BF), V((slots, nodes), BF), V((nodes, slots), BF),
            V((n_dom, SLOTS, width), BF), V((n_zc, n_y, SLOTS, half), BF), V((n_y, n_zc, SLOTS, half), BF),
            V((n_y, n_zc, SLOTS, width), BF),
            V((n_dom, SLOTS, width), BF), V((n_zc, n_y, SLOTS, half), BF), V((n_y, n_zc, SLOTS, half), BF),
            V((n_y, n_zc, SLOTS, width), BF), V((ends, width), BF),
            V((zrows + 8, width), BF), V((zrows + 8, width), F32),
            V((2, 2, quarter, half), BF), V((2, 2, quarter, half), BF), V((2, quarter, half), BF),
            V((2, quarter, half), BF), V((4, quarter, half), F32),
            V((2, crows + 8, width), F32), V((crows + 8, width), F32),
            V((n_z, zrows + 8, width), BF), V((n_z, zrows + 8, width), BF),
            V((n_y, zrows + 8, width), BF), V((n_x, zrows + 8, width), F32), V((2, n_z, zrows, width), F32),
            pltpu.SemaphoreType.DMA((7,)), pltpu.SemaphoreType.DMA((4,)),
            pltpu.SemaphoreType.DMA((24,)), pltpu.SemaphoreType.DMA((24,)),
        ],
        compiler_params=pltpu.CompilerParams(
            collective_id=0, has_side_effects=True, vmem_limit_bytes=60 * 1024 * 1024
        ),
        name="encode_decode",
    )(
        edge_owner.T, edge_rows.T, halo_rows.T, labels.reshape(1, -1), b_enc.reshape(1, -1), b_dec1.reshape(1, -1),
        w_dec2, feats, history, adj_inner, adj_halo, w_self, w_nbr, w_dec1,
    )
    shapes = ((nodes, width, BF), (quarter, width, F32), (width, width, F32), (1, width, F32), (1, width, F32))
    embed, grad_embed, grad_dec1, bias1, dec2 = pl.pallas_call(
        put_out,
        out_shape=tuple(jax.ShapeDtypeStruct(shape[:2], shape[2]) for shape in shapes),
        in_specs=[vmem] * 4,
        out_specs=(any_,) * 5,
        scratch_shapes=[pltpu.SemaphoreType.DMA((5,))],
        name="put_out",
    )(*[pltpu.with_memory_space_constraint(out, pltpu.VMEM) for out in outs])
    return embed, grad_embed, grad_dec1, bias1.reshape(-1), dec2.reshape(-1)


def solution(mesh):
    placed = (
        P("dom", None), P("dom", None), P("dom", None), P("dom", None), P("dom", None), P(), P(), P(),
        P(("dom", "rep"), None), P(("dom", "rep"), None), P(("dom", "rep")), P(), P(), P(),
    )
    return jax.shard_map(
        per_device,
        mesh=mesh,
        in_specs=placed,
        out_specs=(P("dom", None), P(("dom", "rep"), None), P(), P(), P()),
        check_vma=False,
    )
```

```python
import functools

import jax
import jax.numpy as jnp
from jax import lax
from jax.experimental import pallas as pl
from jax.experimental.pallas import tpu as pltpu
from jax.sharding import PartitionSpec as P

BF = jnp.bfloat16
F32 = jnp.float32
I32 = jnp.int32
MESH = pl.DeviceIdType.MESH
SLOTS = 8
LANES = 128


def log2(value):
    return value.bit_length() - 1


def iota(shape, dim):
    return lax.broadcasted_iota(I32, shape, dim)


def nn(a, b):
    return lax.dot_general(a, b, (((1,), (0,)), ((), ())), preferred_element_type=F32)


def nt(a, b):
    return lax.dot_general(a, b, (((1,), (1,)), ((), ())), preferred_element_type=F32)


def tn(a, b):
    return lax.dot_general(a, b, (((0,), (0,)), ((), ())), preferred_element_type=F32)


def hot(cond):
    return jnp.where(cond, 1.0, 0.0).astype(BF)


def column_of(row):
    n = row.shape[1]
    return jnp.sum(jnp.where(iota((n, n), 0) == iota((n, n), 1), row, 0.0), axis=1, keepdims=True)


def row_of(column):
    n = column.shape[0]
    return jnp.sum(jnp.where(iota((n, n), 0) == iota((n, n), 1), column, 0.0), axis=0, keepdims=True)


def far_first(n):
    return sorted(range(1, n), key=lambda k: -min(k, n - k))


def copies(ref, sem):
    return pltpu.make_async_copy(ref, ref, sem)


def kernel(
    n_y, n_zc, n_x,
    eo_h, er_h, hr_h, lab_h, b_enc_h, b_dec1_h, w_dec2_h,
    feats_h, hist_h, adji_h, adjh_h, wself_h, wnbr_h, wdec1_h,
    emb_o, ge_o, gd_o, gv_o,
    eo, er, hr, lab, b_enc, b_dec1, w_dec2,
    feats, hist, adji, adjh, wself, wnbr, wdec1,
    ids_s, ids_r1, ids_t, ids_r2,
    hal_s, hal_r1, hal_t, hal_r2, hal_m, hal_u, hal_v, hal_w, halo, adjp,
    inner, selfp, place,
    hot_e, hot_et, hot_g, hot_gt,
    fet_s, fet_a, fet_b, fet_r,
    gra_s, gra_a, gra_b, gra_r, gpair,
    zbuf, dbuf,
    xs1, xr1, xs2, xr2, xk,
    dc_s, dc_r, dz_s, dz_r, dy_r, dx_r, dg_r,
    small_sem, load_sem,
    ssem, rsem,
):
    n_dom = n_y * n_zc
    nodes, width = feats.shape
    half = width // 2
    queries = eo.shape[1]
    ends = 2 * queries
    slots = n_dom * SLOTS
    halos = 2 * n_dom
    n_z = n_zc // 2
    ly, lzc = log2(n_y), log2(n_zc)
    me = lax.axis_index("dom")
    rep = lax.axis_index("rep")
    y = lax.div(me, n_zc)
    zc = lax.rem(me, n_zc)
    z = lax.div(zc, 2)
    core = lax.rem(zc, 2)

    small = [
        pltpu.make_async_copy(src, dst, small_sem.at[i])
        for i, (src, dst) in enumerate(
            ((eo_h, eo), (er_h, er), (hr_h, hr), (lab_h, lab), (b_enc_h, b_enc), (b_dec1_h, b_dec1), (w_dec2_h, w_dec2))
        )
    ]
    loads = [
        pltpu.make_async_copy(src, dst, load_sem.at[i])
        for i, (src, dst) in enumerate(
            ((feats_h, feats), (adji_h, adji), (wself_h, wself), (adjh_h, adjh), (hist_h, hist), (wnbr_h, wnbr), (wdec1_h, wdec1))
        )
    ]
    barrier = pltpu.get_barrier_semaphore()

    def zc_peer(k):
        return lax.rem(zc + k, n_zc)

    def y_peer(k):
        return lax.rem(y + k, n_y)

    for k in far_first(n_zc):
        pl.semaphore_signal(barrier, inc=1, device_id={"dom": y * n_zc + zc_peer(k)}, device_id_type=MESH)
    for k in far_first(n_y):
        pl.semaphore_signal(barrier, inc=1, device_id={"dom": y_peer(k) * n_zc + zc}, device_id_type=MESH)
    for k in range(1, n_x):
        pl.semaphore_signal(barrier, inc=1, device_id={"rep": lax.rem(rep + k, n_x)}, device_id_type=MESH)

    sent = []

    def drain():
        for index, size in sent:
            copies(size, ssem.at[index]).wait()

    def along_zc(index, source, target, sent_size):
        for k in far_first(n_zc):
            peer = zc_peer(k)
            pltpu.make_async_remote_copy(
                src_ref=source(peer), dst_ref=target(zc), send_sem=ssem.at[index], recv_sem=rsem.at[index],
                device_id={"dom": y * n_zc + peer}, device_id_type=MESH,
            ).start()
        pltpu.make_async_copy(source(zc), target(zc), rsem.at[index]).start()
        sent.append((index, sent_size))

    def along_y(index, source, target, sent_size):
        for k in far_first(n_y):
            peer = y_peer(k)
            pltpu.make_async_remote_copy(
                src_ref=source(peer), dst_ref=target(y), send_sem=ssem.at[index], recv_sem=rsem.at[index],
                device_id={"dom": peer * n_zc + zc}, device_id_type=MESH,
            ).start()
        pltpu.make_async_copy(source(y), target(y), rsem.at[index]).start()
        sent.append((index, sent_size))

    for load in small + loads:
        load.start()
    for load in small:
        load.wait()

    owner = jnp.concatenate([eo[0:1, :], eo[1:2, :]], axis=1)
    local = jnp.concatenate([er[0:1, :], er[1:2, :]], axis=1)
    rows = iota((n_dom, ends), 0)
    turned = ((rows & (n_y - 1)) << lzc) + (rows >> ly)
    match = owner == turned
    match_hot = hot(match)
    before = hot(iota((ends, ends), 0) < iota((ends, ends), 1))
    rank = nn(match_hot, before)
    slot = jnp.sum(jnp.where(match, rank, 0.0), axis=0, keepdims=True)
    place[...] = jnp.broadcast_to(owner.astype(F32) * float(SLOTS) + slot, place.shape)

    def lane_rows(at, value):
        lane = iota((LANES, value.shape[1]), 0)
        part = jnp.where(lane < 16, value >> 5, value & 31)
        return jnp.where(at & (lane < 32), part.astype(F32), 0.0).astype(BF)

    wanted = lane_rows(slot == (iota((LANES, ends), 0) & 15).astype(F32), local)
    lane = iota((LANES, n_dom), 0) & 15
    halo_ids = jnp.where(lane == SLOTS, hr[0:1, :], hr[1:2, :])
    halo_wanted = lane_rows((lane == SLOTS) | (lane == SLOTS + 1), halo_ids)
    prow, pcol = iota((n_dom, n_dom), 0), iota((n_dom, n_dom), 1)
    to_zc_y = hot(pcol == ((prow & (n_y - 1)) << lzc) + (prow >> ly))
    to_y_zc = hot(pcol == ((prow & (n_zc - 1)) << ly) + (prow >> lzc))
    requests = nt(match_hot, wanted) + nt(to_zc_y, halo_wanted)
    ids_s[...] = requests.astype(BF).reshape(n_zc, n_y, LANES)

    pl.semaphore_wait(barrier, (n_zc - 1) + (n_y - 1) + (n_x - 1))
    along_zc(0, lambda p: ids_s.at[p], lambda m: ids_r1.at[m], ids_s.at[pl.ds(0, n_zc - 1)])

    tile = min(256, nodes)
    loads[0].wait()
    loads[1].wait()

    @pl.loop(0, nodes // tile)
    def _(i):
        at = pl.ds(pl.multiple_of(i * tile, tile), tile)
        inner[at, :] = nn(adji[at, :], feats[...])

    copies(ids_r1, rsem.at[0]).wait()
    ids_t[...] = nn(to_y_zc, ids_r1[...].reshape(n_dom, LANES)).astype(BF).reshape(n_y, n_zc, LANES)
    along_y(1, lambda p: ids_t.at[p], lambda m: ids_r2.at[m], ids_t.at[pl.ds(0, n_y - 1)])

    loads[2].wait()
    loads[3].wait()

    @pl.loop(0, nodes // tile)
    def _(i):
        at = pl.ds(pl.multiple_of(i * tile, tile), tile)
        selfp[at, :] = nn(feats[at, :], wself[...]) + b_enc[...]

    ko, jo = iota((halos, halos), 0), iota((halos, halos), 1)
    std = ((((jo >> (lzc + 1)) << lzc) + (jo & (n_zc - 1))) << 1) + ((jo >> lzc) & 1)
    adjp[...] = nn(adjh[...], hot(ko == std)).astype(BF)

    for i in (4, 5, 6):
        loads[i].wait()

    copies(ids_r2, rsem.at[1]).wait()
    asked = nn(to_zc_y, ids_r2[...].reshape(n_dom, LANES))
    asked_c = [32.0 * asked[:, at : at + 1] + asked[:, at + 16 : at + 17] for at in (SLOTS, SLOTS + 1)]
    pick = hot(jnp.concatenate(asked_c, axis=0) == iota((halos, nodes), 1).astype(F32))
    picked = nn(pick, hist[...]).astype(BF)
    for c in range(2):
        hal_s[:, c] = picked[c * n_dom : (c + 1) * n_dom, :half].reshape(n_zc, n_y, half)
        hal_m[:, c] = picked[c * n_dom : (c + 1) * n_dom, half:].reshape(n_zc, n_y, half)
    along_zc(2, lambda p: hal_s.at[p], lambda m: hal_r1.at[m], hal_s.at[pl.ds(0, n_zc - 1)])
    io, oo = iota((halos, halos), 1), iota((halos, halos), 0)
    turn = hot(io == ((oo & (n_zc - 1)) << (ly + 1)) + (((oo >> lzc) & 1) << ly) + (oo >> (lzc + 1)))
    back = hot(io == ((oo & (n_y - 1)) << (lzc + 1)) + (((oo >> ly) & 1) << lzc) + (oo >> (ly + 1)))
    hal_u[...] = nn(turn, hal_m[...].reshape(halos, half)).astype(BF).reshape(n_y, 2 * n_zc, half)
    along_y(22, lambda p: hal_u.at[p], lambda m: hal_v.at[m], hal_u.at[pl.ds(0, n_y - 1)])

    gtile = min(256, slots)
    per = gtile // SLOTS
    id_rows = []
    for i in range(slots // gtile):
        asked = ids_r2[...].reshape(n_dom, LANES)[i * per : (i + 1) * per].astype(F32)
        spread = jnp.broadcast_to(asked[:, None, :], (per, SLOTS, LANES)).reshape(gtile, LANES)
        lane, mine = iota((gtile, LANES), 1), iota((gtile, LANES), 0) & (SLOTS - 1)
        weight = jnp.where(lane == mine, 32.0, jnp.where(lane == mine + 16, 1.0, 0.0))
        id_col = jnp.sum(spread * weight, axis=1, keepdims=True)
        hot_g[i * gtile : (i + 1) * gtile, :] = hot(id_col == iota((gtile, nodes), 1).astype(F32))
        id_rows.append(row_of(id_col))
    id_row = jnp.concatenate(id_rows, axis=1)

    copies(hal_r1, rsem.at[2]).wait()
    hal_t[...] = nn(turn, hal_r1[...].reshape(halos, half)).astype(BF).reshape(n_y, 2 * n_zc, half)
    along_y(3, lambda p: hal_t.at[p], lambda m: hal_r2.at[m], hal_t.at[pl.ds(0, n_y - 1)])
    copies(hal_v, rsem.at[22]).wait()
    hal_m[...] = nn(back, hal_v[...].reshape(halos, half)).astype(BF).reshape(n_zc, 2, n_y, half)
    along_zc(23, lambda p: hal_m.at[p], lambda m: hal_w.at[m], hal_m.at[pl.ds(0, n_zc - 1)])

    copies(hal_r2, rsem.at[3]).wait()
    copies(hal_w, rsem.at[23]).wait()
    halo[:, :half] = hal_r2[...].reshape(halos, half)
    halo[:, half:] = nn(turn, hal_w[...].reshape(halos, half)).astype(BF)

    @pl.loop(0, nodes // tile)
    def _(i):
        at = pl.ds(pl.multiple_of(i * tile, tile), tile)
        agg = (inner[at, :] + nn(adjp[at, :], halo[...])).astype(BF)
        emb_o[at, :] = jnp.maximum(selfp[at, :] + nn(agg, wnbr[...]), 0.0).astype(BF)

    @pl.loop(0, slots // gtile)
    def _(i):
        at = pl.ds(pl.multiple_of(i * gtile, gtile), gtile)
        block = nn(hot_g[at, :], emb_o[...]).astype(BF)
        fet_s[pl.ds(i * per, per)] = block.reshape(per, SLOTS, width)

    left, right = pl.ds(0, half), pl.ds(half, half)

    def both_ways(base, send, mid_a, mid_b, recv):
        send4 = send.reshape(n_y, n_zc, SLOTS, width)
        along_zc(base, lambda p: send4.at[:, p, :, left], lambda m: mid_a.at[m], mid_a.at[pl.ds(0, n_zc - 1)])
        along_y(base + 1, lambda p: send4.at[p, :, :, right], lambda m: mid_b.at[m], mid_b.at[pl.ds(0, n_y - 1)])

    def both_ways_on(base, mid_a, mid_b, recv):
        copies(mid_a, rsem.at[base]).wait()
        along_y(base + 2, lambda p: mid_a.at[:, p], lambda m: recv.at[m, :, :, left], mid_b.at[pl.ds(0, n_y - 1)])
        copies(mid_b, rsem.at[base + 1]).wait()
        along_zc(base + 3, lambda p: mid_b.at[:, p], lambda m: recv.at[:, m, :, right], mid_a.at[pl.ds(0, n_zc - 1)])

    both_ways(4, fet_s, fet_a, fet_b, fet_r)
    place_col = column_of(place[0:1, :])
    etile = min(256, ends)
    for i in range(ends // etile):
        hot_e[i * etile : (i + 1) * etile, :] = hot(
            place_col[i * etile : (i + 1) * etile, :] == iota((etile, slots), 1).astype(F32)
        )

    @pl.loop(0, slots // gtile)
    def _(i):
        at = pl.ds(pl.multiple_of(i * gtile, gtile), gtile)
        hot_et[at, :] = hot((iota((gtile, ends), 0) + i * gtile).astype(F32) == place[0:1, :])

    target = column_of(lab[...].astype(F32))

    both_ways_on(4, fet_a, fet_b, fet_r)

    @pl.loop(0, nodes // tile)
    def _(i):
        at = pl.ds(pl.multiple_of(i * tile, tile), tile)
        hot_gt[at, :] = hot((iota((tile, slots), 0) + i * tile).astype(F32) == id_row)

    copies(fet_r.at[:, :, :, left], rsem.at[6]).wait()
    copies(fet_r.at[:, :, :, right], rsem.at[7]).wait()

    got = fet_r[...].reshape(slots, width)
    head = nn(hot_e[:queries, :], got)
    tail = nn(hot_e[queries:, :], got)
    zprod = (head * tail).astype(BF)
    pre = nn(zprod, wdec1[...]) + b_dec1[...]
    sig = jax.nn.sigmoid(pre)
    hidden = (pre * sig).astype(BF).astype(F32)
    wout = w_dec2[...].astype(F32).reshape(1, width)
    logit = jnp.sum(hidden * wout, axis=1, keepdims=True)
    dlogit = jax.nn.sigmoid(logit) - target
    d_pre = (dlogit * wout * (sig * (1.0 + pre * (1.0 - sig)))).astype(BF)
    grad1 = tn(zprod, d_pre)
    gb1 = jnp.sum(d_pre.astype(F32), axis=0, keepdims=True)
    gd2 = jnp.sum(hidden * dlogit, axis=0, keepdims=True)
    vrow = iota((8, width), 0)
    vecs = jnp.where(vrow == 0, gb1, jnp.where(vrow == 1, gd2, 0.0))
    crows = width // 2
    zrows = crows // n_z
    for h in range(2):
        dc_s[h, :crows] = grad1[h * crows : (h + 1) * crows]
        dc_s[h, crows:] = vecs
    other = 1 - core
    pair = pltpu.make_async_remote_copy(
        src_ref=dc_s.at[other], dst_ref=dc_r, send_sem=ssem.at[12], recv_sem=rsem.at[12],
        device_id={"dom": y * n_zc + 2 * z + other}, device_id_type=MESH,
    )
    pair.start()

    def along_z(index, source, goal, sent_size):
        for k in far_first(n_z):
            peer = lax.rem(z + k, n_z)
            pltpu.make_async_remote_copy(
                src_ref=source(peer), dst_ref=goal(z), send_sem=ssem.at[index], recv_sem=rsem.at[index],
                device_id={"dom": y * n_zc + 2 * peer + core}, device_id_type=MESH,
            ).start()
        pltpu.make_async_copy(source(z), goal(z), rsem.at[index]).start()
        sent.append((index, sent_size))

    dz = nt(d_pre, wdec1[...])
    gpair[:queries, :] = (dz * tail).astype(BF)
    gpair[queries:, :] = (dz * head).astype(BF)

    @pl.loop(0, slots // gtile)
    def _(i):
        at = pl.ds(pl.multiple_of(i * gtile, gtile), gtile)
        block = nn(hot_et[at, :], gpair[...]).astype(BF)
        gra_s[pl.ds(i * per, per)] = block.reshape(per, SLOTS, width)

    gra_s4 = gra_s.reshape(n_y, n_zc, SLOTS, width)
    along_y(9, lambda p: gra_s4.at[p, :, :, right], lambda m: gra_b.at[m], gra_b.at[pl.ds(0, n_y - 1)])

    pair.wait_recv()
    for j in range(n_z):
        dz_s[j, :zrows] = (dc_s[core, j * zrows : (j + 1) * zrows] + dc_r[j * zrows : (j + 1) * zrows]).astype(BF)
        dz_s[j, zrows:] = (dc_s[core, crows:] + dc_r[crows:]).astype(BF)
    along_z(13, lambda p: dz_s.at[p], lambda m: dz_r.at[m], dz_s.at[pl.ds(0, n_z - 1)])

    along_zc(8, lambda p: gra_s4.at[:, p, :, left], lambda m: gra_a.at[m], gra_a.at[pl.ds(0, n_zc - 1)])

    copies(dz_r, rsem.at[13]).wait()
    total = dz_r[0].astype(F32)
    for j in range(1, n_z):
        total = total + dz_r[j].astype(F32)
    zbuf[...] = total.astype(BF)
    along_y(14, lambda p: zbuf, lambda m: dy_r.at[m], dy_r.at[pl.ds(0, n_y - 1)])

    both_ways_on(8, gra_a, gra_b, gra_r)

    copies(dy_r, rsem.at[14]).wait()
    total = dy_r[0].astype(F32)
    for j in range(1, n_y):
        total = total + dy_r[j].astype(F32)
    dbuf[...] = total
    for k in range(1, n_x):
        pltpu.make_async_remote_copy(
            src_ref=dbuf, dst_ref=dx_r.at[rep], send_sem=ssem.at[15], recv_sem=rsem.at[15],
            device_id={"rep": lax.rem(rep + k, n_x)}, device_id_type=MESH,
        ).start()
    pltpu.make_async_copy(dbuf, dx_r.at[rep], rsem.at[15]).start()
    sent.append((15, dx_r.at[pl.ds(0, n_x - 1)]))

    copies(dx_r, rsem.at[15]).wait()
    total = dx_r[0]
    for j in range(1, n_x):
        total = total + dx_r[j]
    gv_o[...] = total[zrows:]
    dc_r[:zrows] = total[:zrows]
    along_z(20, lambda p: dc_r.at[pl.ds(0, zrows)], lambda m: dg_r.at[core, m], dg_r.at[0, pl.ds(0, n_z - 1)])

    flip = rep + 1 - 2 * lax.rem(rep, 2)
    wrap = 3 - rep
    wflip = wrap + 1 - 2 * lax.rem(wrap, 2)
    quarter = nodes // n_x
    jtile = min(64, quarter)

    def local_sum(q):
        at = pl.ds(pl.multiple_of(q * quarter, quarter), quarter)
        return nn(hot_gt[at, :], gra_r[...].reshape(slots, width))

    def trade(index, source, goal, partner):
        copy = pltpu.make_async_remote_copy(
            src_ref=source, dst_ref=goal, send_sem=ssem.at[index], recv_sem=rsem.at[index],
            device_id={"rep": partner}, device_id_type=MESH,
        )
        copy.start()
        return copy

    def joined(way, part):
        @pl.loop(0, quarter // jtile)
        def _(i):
            at = pl.ds(pl.multiple_of(i * jtile, jtile), jtile)
            xs2[way, at, :] = (xk[part, at, :] + xr1[way, 1, at, :].astype(F32)).astype(BF)

    copies(gra_r.at[:, :, :, left], rsem.at[10]).wait()
    copies(gra_r.at[:, :, :, right], rsem.at[11]).wait()
    part = local_sum(wflip)
    xs1[0, 1] = part[:, :half].astype(BF)
    xs1[1, 1] = part[:, half:].astype(BF)
    part = local_sum(flip)
    xs1[0, 0] = part[:, :half].astype(BF)
    one = trade(16, xs1.at[0], xr1.at[0], flip)
    xk[3] = part[:, half:]
    part = local_sum(wrap)
    xs1[1, 0] = part[:, half:].astype(BF)
    two = trade(17, xs1.at[1], xr1.at[1], wrap)
    xk[2] = part[:, :half]
    part = local_sum(rep)
    xk[0] = part[:, :half]
    xk[1] = part[:, half:]
    one.wait_recv()
    joined(0, 2)
    three = trade(18, xs2.at[0], xr2.at[0], wrap)
    two.wait_recv()
    joined(1, 3)
    four = trade(19, xs2.at[1], xr2.at[1], flip)

    copies(dg_r.at[0], rsem.at[20]).wait()
    last = pltpu.make_async_remote_copy(
        src_ref=dg_r.at[core], dst_ref=dg_r.at[core], send_sem=ssem.at[21], recv_sem=rsem.at[21],
        device_id={"dom": y * n_zc + 2 * z + other}, device_id_type=MESH,
    )
    last.start()

    three.wait_recv()
    ge_o[:, :half] = xk[0] + xr1[0, 0].astype(F32) + xr2[0].astype(F32)
    four.wait_recv()
    ge_o[:, half:] = xk[1] + xr1[1, 0].astype(F32) + xr2[1].astype(F32)

    drain()
    pair.wait_send()
    for copy in (one, two, three, four):
        copy.wait_send()
    last.wait()
    gd_o[...] = dg_r[...].reshape(width, width)


def put_out(emb, ge, gd, gv, emb_h, ge_h, gd_h, gb_h, g2_h, sem):
    pairs = ((emb, emb_h), (ge, ge_h), (gd, gd_h), (gv.at[pl.ds(0, 1)], gb_h), (gv.at[pl.ds(1, 1)], g2_h))
    copies_out = [pltpu.make_async_copy(src, dst, sem.at[i]) for i, (src, dst) in enumerate(pairs)]
    for copy in copies_out:
        copy.start()
    for copy in copies_out:
        copy.wait()


def per_device(
    feats, history, adj_inner, adj_halo, halo_rows, w_self, w_nbr, b_enc,
    edge_owner, edge_rows, labels, w_dec1, b_dec1, w_dec2,
):
    n_dom, n_x = lax.axis_size("dom"), lax.axis_size("rep")
    n_zc = 16 if n_dom == 128 else 4
    n_y = n_dom // n_zc
    nodes, width = feats.shape
    halos = adj_halo.shape[1]
    queries = edge_owner.shape[0]
    ends = 2 * queries
    slots = n_dom * SLOTS
    half = width // 2
    n_z = n_zc // 2
    quarter = nodes // n_x
    crows = width // 2
    zrows = crows // n_z
    vmem = pl.BlockSpec(memory_space=pltpu.VMEM)
    any_ = pl.BlockSpec(memory_space=pl.ANY)
    V = pltpu.VMEM
    outs = pl.pallas_call(
        functools.partial(kernel, n_y, n_zc, n_x),
        out_shape=(
            V((nodes, width), BF),
            V((quarter, width), F32),
            V((width, width), F32),
            V((8, width), F32),
        ),
        in_specs=[any_] * 14,
        out_specs=(vmem,) * 4,
        scratch_shapes=[
            V((2, queries), I32), V((2, queries), I32), V((2, n_dom), I32), V((1, queries), I32), V((1, width), F32),
            V((1, width), F32), V((width,), BF),
            V((nodes, width), BF), V((nodes, width), BF), V((nodes, nodes), BF), V((nodes, halos), BF),
            V((width, width), BF), V((width, width), BF), V((width, width), BF),
            V((n_zc, n_y, LANES), BF), V((n_zc, n_y, LANES), BF), V((n_y, n_zc, LANES), BF), V((n_y, n_zc, LANES), BF),
            V((n_zc, 2, n_y, half), BF), V((n_zc, 2, n_y, half), BF), V((n_y, 2 * n_zc, half), BF),
            V((n_y, 2 * n_zc, half), BF), V((n_zc, 2, n_y, half), BF), V((n_y, 2 * n_zc, half), BF),
            V((n_y, 2 * n_zc, half), BF), V((n_zc, 2, n_y, half), BF), V((halos, width), BF), V((nodes, halos), BF),
            V((nodes, width), F32), V((nodes, width), F32), V((8, ends), F32),
            V((ends, slots), BF), V((slots, ends), BF), V((slots, nodes), BF), V((nodes, slots), BF),
            V((n_dom, SLOTS, width), BF), V((n_zc, n_y, SLOTS, half), BF), V((n_y, n_zc, SLOTS, half), BF),
            V((n_y, n_zc, SLOTS, width), BF),
            V((n_dom, SLOTS, width), BF), V((n_zc, n_y, SLOTS, half), BF), V((n_y, n_zc, SLOTS, half), BF),
            V((n_y, n_zc, SLOTS, width), BF), V((ends, width), BF),
            V((zrows + 8, width), BF), V((zrows + 8, width), F32),
            V((2, 2, quarter, half), BF), V((2, 2, quarter, half), BF), V((2, quarter, half), BF),
            V((2, quarter, half), BF), V((4, quarter, half), F32),
            V((2, crows + 8, width), F32), V((crows + 8, width), F32),
            V((n_z, zrows + 8, width), BF), V((n_z, zrows + 8, width), BF),
            V((n_y, zrows + 8, width), BF), V((n_x, zrows + 8, width), F32), V((2, n_z, zrows, width), F32),
            pltpu.SemaphoreType.DMA((7,)), pltpu.SemaphoreType.DMA((7,)),
            pltpu.SemaphoreType.DMA((24,)), pltpu.SemaphoreType.DMA((24,)),
        ],
        compiler_params=pltpu.CompilerParams(
            collective_id=0, has_side_effects=True, vmem_limit_bytes=60 * 1024 * 1024
        ),
        name="encode_decode",
    )(
        edge_owner.T, edge_rows.T, halo_rows.T, labels.reshape(1, -1), b_enc.reshape(1, -1), b_dec1.reshape(1, -1),
        w_dec2, feats, history, adj_inner, adj_halo, w_self, w_nbr, w_dec1,
    )
    shapes = ((nodes, width, BF), (quarter, width, F32), (width, width, F32), (1, width, F32), (1, width, F32))
    embed, grad_embed, grad_dec1, bias1, dec2 = pl.pallas_call(
        put_out,
        out_shape=tuple(jax.ShapeDtypeStruct(shape[:2], shape[2]) for shape in shapes),
        in_specs=[vmem] * 4,
        out_specs=(any_,) * 5,
        scratch_shapes=[pltpu.SemaphoreType.DMA((5,))],
        name="put_out",
    )(*[pltpu.with_memory_space_constraint(out, pltpu.VMEM) for out in outs])
    return embed, grad_embed, grad_dec1, bias1.reshape(-1), dec2.reshape(-1)


def solution(mesh):
    placed = (
        P("dom", None), P("dom", None), P("dom", None), P("dom", None), P("dom", None), P(), P(), P(),
        P(("dom", "rep"), None), P(("dom", "rep"), None), P(("dom", "rep")), P(), P(), P(),
    )
    return jax.shard_map(
        per_device,
        mesh=mesh,
        in_specs=placed,
        out_specs=(P("dom", None), P(("dom", "rep"), None), P(), P(), P()),
        check_vma=False,
    )
```

```python
import functools

import jax
import jax.numpy as jnp
from jax import lax
from jax.experimental import pallas as pl
from jax.experimental.pallas import tpu as pltpu
from jax.sharding import PartitionSpec as P

BF = jnp.bfloat16
F32 = jnp.float32
I32 = jnp.int32
MESH = pl.DeviceIdType.MESH
SLOTS = 8
LANES = 128


def log2(value):
    return value.bit_length() - 1


def iota(shape, dim):
    return lax.broadcasted_iota(I32, shape, dim)


def nn(a, b):
    return lax.dot_general(a, b, (((1,), (0,)), ((), ())), preferred_element_type=F32)


def nt(a, b):
    return lax.dot_general(a, b, (((1,), (1,)), ((), ())), preferred_element_type=F32)


def tn(a, b):
    return lax.dot_general(a, b, (((0,), (0,)), ((), ())), preferred_element_type=F32)


def hot(cond):
    return jnp.where(cond, 1.0, 0.0).astype(BF)


def column_of(row):
    n = row.shape[1]
    return jnp.sum(jnp.where(iota((n, n), 0) == iota((n, n), 1), row, 0.0), axis=1, keepdims=True)


def row_of(column):
    n = column.shape[0]
    return jnp.sum(jnp.where(iota((n, n), 0) == iota((n, n), 1), column, 0.0), axis=0, keepdims=True)


def far_first(n):
    return sorted(range(1, n), key=lambda k: -min(k, n - k))


def offset_at(place, n):
    return jnp.where((place & 1) == 1, n // 2 - ((place + 1) >> 1), n // 2 + (place >> 1))


def place_of(offset, n):
    d = (offset & (n - 1)) - n // 2
    return jnp.where(d < 0, -2 * d - 1, 2 * d)


def far_places(n):
    return [n // 2 - (p + 1) // 2 if p % 2 else n // 2 + p // 2 for p in range(n)]


def copies(ref, sem):
    return pltpu.make_async_copy(ref, ref, sem)


def kernel(
    n_y, n_zc, n_x,
    eo_h, er_h, hr_h, lab_h, b_enc_h, b_dec1_h, w_dec2_h,
    feats_h, hist_h, adji_h, adjh_h, wself_h, wnbr_h, wdec1_h,
    emb_o, ge_o, gd_o, gv_o,
    eo, er, hr, lab, b_enc, b_dec1, w_dec2,
    feats, hist, adji, adjh, wself, wnbr, wdec1,
    ids_s, ids_r1, ids_t, ids_r2,
    hal_s, hal_r1, hal_t, hal_r2, hal_m, hal_u, hal_v, hal_w, halo, adjp,
    inner, selfp, place, far_place,
    hot_e, hot_et, hot_g, hot_gt,
    fet_s, fet_a, fet_b, fet_r,
    gra_s, gra_a, gra_b, gra_r, gpair,
    zbuf, dbuf,
    xs1, xr1, xs2, xr2, xk,
    dc_s, dc_r, dz_s, dz_r, dy_r, dx_r, dg_r,
    small_sem, load_sem,
    ssem, rsem,
):
    n_dom = n_y * n_zc
    nodes, width = feats.shape
    half = width // 2
    queries = eo.shape[1]
    ends = 2 * queries
    slots = n_dom * SLOTS
    halos = 2 * n_dom
    n_z = n_zc // 2
    ly, lzc = log2(n_y), log2(n_zc)
    me = lax.axis_index("dom")
    rep = lax.axis_index("rep")
    y = lax.div(me, n_zc)
    zc = lax.rem(me, n_zc)
    z = lax.div(zc, 2)
    core = lax.rem(zc, 2)

    small = [
        pltpu.make_async_copy(src, dst, small_sem.at[i])
        for i, (src, dst) in enumerate(
            ((eo_h, eo), (er_h, er), (hr_h, hr), (lab_h, lab), (b_enc_h, b_enc), (b_dec1_h, b_dec1), (w_dec2_h, w_dec2))
        )
    ]
    loads = [
        pltpu.make_async_copy(src, dst, load_sem.at[i])
        for i, (src, dst) in enumerate(
            ((feats_h, feats), (adji_h, adji), (wself_h, wself), (adjh_h, adjh), (hist_h, hist), (wnbr_h, wnbr), (wdec1_h, wdec1))
        )
    ]
    barrier = pltpu.get_barrier_semaphore()

    def zc_peer(k):
        return lax.rem(zc + k, n_zc)

    def y_peer(k):
        return lax.rem(y + k, n_y)

    for k in far_first(n_zc):
        pl.semaphore_signal(barrier, inc=1, device_id={"dom": y * n_zc + zc_peer(k)}, device_id_type=MESH)
    for k in far_first(n_y):
        pl.semaphore_signal(barrier, inc=1, device_id={"dom": y_peer(k) * n_zc + zc}, device_id_type=MESH)
    for k in range(1, n_x):
        pl.semaphore_signal(barrier, inc=1, device_id={"rep": lax.rem(rep + k, n_x)}, device_id_type=MESH)

    sent = []

    def drain():
        for index, size in sent:
            copies(size, ssem.at[index]).wait()

    def along_zc(index, source, target, sent_size):
        for k in far_first(n_zc):
            peer = zc_peer(k)
            pltpu.make_async_remote_copy(
                src_ref=source(peer), dst_ref=target(zc), send_sem=ssem.at[index], recv_sem=rsem.at[index],
                device_id={"dom": y * n_zc + peer}, device_id_type=MESH,
            ).start()
        pltpu.make_async_copy(source(zc), target(zc), rsem.at[index]).start()
        sent.append((index, sent_size))

    def along_y(index, source, target, sent_size):
        for k in far_first(n_y):
            peer = y_peer(k)
            pltpu.make_async_remote_copy(
                src_ref=source(peer), dst_ref=target(y), send_sem=ssem.at[index], recv_sem=rsem.at[index],
                device_id={"dom": peer * n_zc + zc}, device_id_type=MESH,
            ).start()
        pltpu.make_async_copy(source(y), target(y), rsem.at[index]).start()
        sent.append((index, sent_size))

    for load in small + loads:
        load.start()
    for load in small:
        load.wait()

    owner = jnp.concatenate([eo[0:1, :], eo[1:2, :]], axis=1)
    local = jnp.concatenate([er[0:1, :], er[1:2, :]], axis=1)
    rows = iota((n_dom, ends), 0)
    turned = ((rows & (n_y - 1)) << lzc) + (rows >> ly)
    match = owner == turned
    match_hot = hot(match)
    before = hot(iota((ends, ends), 0) < iota((ends, ends), 1))
    rank = nn(match_hot, before)
    slot = jnp.sum(jnp.where(match, rank, 0.0), axis=0, keepdims=True)
    place[...] = jnp.broadcast_to(owner.astype(F32) * float(SLOTS) + slot, place.shape)
    far = (place_of((owner >> lzc) - y, n_y) << lzc) + place_of((owner & (n_zc - 1)) - zc, n_zc)
    far_place[...] = jnp.broadcast_to(far.astype(F32) * float(SLOTS) + slot, far_place.shape)

    def lane_rows(at, value):
        lane = iota((LANES, value.shape[1]), 0)
        part = jnp.where(lane < 16, value >> 5, value & 31)
        return jnp.where(at & (lane < 32), part.astype(F32), 0.0).astype(BF)

    wanted = lane_rows(slot == (iota((LANES, ends), 0) & 15).astype(F32), local)
    lane = iota((LANES, n_dom), 0) & 15
    halo_ids = jnp.where(lane == SLOTS, hr[0:1, :], hr[1:2, :])
    halo_wanted = lane_rows((lane == SLOTS) | (lane == SLOTS + 1), halo_ids)
    prow, pcol = iota((n_dom, n_dom), 0), iota((n_dom, n_dom), 1)
    to_zc_y = hot(pcol == ((prow & (n_y - 1)) << lzc) + (prow >> ly))
    to_y_zc = hot(pcol == ((prow & (n_zc - 1)) << ly) + (prow >> lzc))
    requests = nt(match_hot, wanted) + nt(to_zc_y, halo_wanted)
    ids_s[...] = requests.astype(BF).reshape(n_zc, n_y, LANES)

    pl.semaphore_wait(barrier, (n_zc - 1) + (n_y - 1) + (n_x - 1))
    along_zc(0, lambda p: ids_s.at[p], lambda m: ids_r1.at[m], ids_s.at[pl.ds(0, n_zc - 1)])

    tile = min(256, nodes)
    loads[0].wait()
    loads[1].wait()

    @pl.loop(0, nodes // tile)
    def _(i):
        at = pl.ds(pl.multiple_of(i * tile, tile), tile)
        inner[at, :] = nn(adji[at, :], feats[...])

    copies(ids_r1, rsem.at[0]).wait()
    ids_t[...] = nn(to_y_zc, ids_r1[...].reshape(n_dom, LANES)).astype(BF).reshape(n_y, n_zc, LANES)
    along_y(1, lambda p: ids_t.at[p], lambda m: ids_r2.at[m], ids_t.at[pl.ds(0, n_y - 1)])

    loads[2].wait()
    loads[3].wait()

    @pl.loop(0, nodes // tile)
    def _(i):
        at = pl.ds(pl.multiple_of(i * tile, tile), tile)
        selfp[at, :] = nn(feats[at, :], wself[...]) + b_enc[...]

    ko, jo = iota((halos, halos), 0), iota((halos, halos), 1)
    std = ((((jo >> (lzc + 1)) << lzc) + (jo & (n_zc - 1))) << 1) + ((jo >> lzc) & 1)
    adjp[...] = nn(adjh[...], hot(ko == std)).astype(BF)

    for i in (4, 5, 6):
        loads[i].wait()

    copies(ids_r2, rsem.at[1]).wait()
    asked = nn(to_zc_y, ids_r2[...].reshape(n_dom, LANES))
    asked_c = [32.0 * asked[:, at : at + 1] + asked[:, at + 16 : at + 17] for at in (SLOTS, SLOTS + 1)]
    pick = hot(jnp.concatenate(asked_c, axis=0) == iota((halos, nodes), 1).astype(F32))
    picked = nn(pick, hist[...]).astype(BF)
    for c in range(2):
        hal_s[:, c] = picked[c * n_dom : (c + 1) * n_dom, :half].reshape(n_zc, n_y, half)
        hal_m[:, c] = picked[c * n_dom : (c + 1) * n_dom, half:].reshape(n_zc, n_y, half)
    along_zc(2, lambda p: hal_s.at[p], lambda m: hal_r1.at[m], hal_s.at[pl.ds(0, n_zc - 1)])
    io, oo = iota((halos, halos), 1), iota((halos, halos), 0)
    turn = hot(io == ((oo & (n_zc - 1)) << (ly + 1)) + (((oo >> lzc) & 1) << ly) + (oo >> (lzc + 1)))
    back = hot(io == ((oo & (n_y - 1)) << (lzc + 1)) + (((oo >> ly) & 1) << lzc) + (oo >> (ly + 1)))
    hal_u[...] = nn(turn, hal_m[...].reshape(halos, half)).astype(BF).reshape(n_y, 2 * n_zc, half)
    along_y(22, lambda p: hal_u.at[p], lambda m: hal_v.at[m], hal_u.at[pl.ds(0, n_y - 1)])

    gtile = min(256, slots)
    per = gtile // SLOTS

    def ids_column(asked):
        n = asked.shape[0] * SLOTS
        spread = jnp.broadcast_to(asked[:, None, :], (asked.shape[0], SLOTS, LANES)).reshape(n, LANES)
        lane, mine = iota((n, LANES), 1), iota((n, LANES), 0) & (SLOTS - 1)
        weight = jnp.where(lane == mine, 32.0, jnp.where(lane == mine + 16, 1.0, 0.0))
        return jnp.sum(spread * weight, axis=1, keepdims=True)

    by_y = (offset_at(prow >> lzc, n_y) + y) & (n_y - 1)
    by_zc = (offset_at(prow & (n_zc - 1), n_zc) + zc) & (n_zc - 1)
    asked_far = nn(hot(pcol == (by_y << lzc) + by_zc), ids_r2[...].reshape(n_dom, LANES))
    for i in range(slots // gtile):
        id_col = ids_column(asked_far[i * per : (i + 1) * per])
        hot_g[i * gtile : (i + 1) * gtile, :] = hot(id_col == iota((gtile, nodes), 1).astype(F32))

    copies(hal_r1, rsem.at[2]).wait()
    hal_t[...] = nn(turn, hal_r1[...].reshape(halos, half)).astype(BF).reshape(n_y, 2 * n_zc, half)
    along_y(3, lambda p: hal_t.at[p], lambda m: hal_r2.at[m], hal_t.at[pl.ds(0, n_y - 1)])
    copies(hal_v, rsem.at[22]).wait()
    hal_m[...] = nn(back, hal_v[...].reshape(halos, half)).astype(BF).reshape(n_zc, 2, n_y, half)
    along_zc(23, lambda p: hal_m.at[p], lambda m: hal_w.at[m], hal_m.at[pl.ds(0, n_zc - 1)])

    copies(hal_r2, rsem.at[3]).wait()
    copies(hal_w, rsem.at[23]).wait()
    halo[:, :half] = hal_r2[...].reshape(halos, half)
    halo[:, half:] = nn(turn, hal_w[...].reshape(halos, half)).astype(BF)

    @pl.loop(0, nodes // tile)
    def _(i):
        at = pl.ds(pl.multiple_of(i * tile, tile), tile)
        agg = (inner[at, :] + nn(adjp[at, :], halo[...])).astype(BF)
        emb_o[at, :] = jnp.maximum(selfp[at, :] + nn(agg, wnbr[...]), 0.0).astype(BF)

    @pl.loop(0, slots // gtile)
    def _(i):
        at = pl.ds(pl.multiple_of(i * gtile, gtile), gtile)
        block = nn(hot_g[at, :], emb_o[...]).astype(BF)
        fet_s[pl.ds(i * per, per)] = block.reshape(per, SLOTS, width)

    left, right = pl.ds(0, half), pl.ds(half, half)

    y_off, zc_off = far_places(n_y), far_places(n_zc)
    y_part, zc_part = n_y // 2, n_zc // 2

    def send_to(index, peer, source, goal, signal):
        pltpu.make_async_remote_copy(
            src_ref=source, dst_ref=goal, send_sem=ssem.at[index], recv_sem=rsem.at[signal],
            device_id={"dom": peer}, device_id_type=MESH,
        ).start()

    def zc_at(p):
        return lax.rem(zc + zc_off[p], n_zc)

    def y_at(p):
        return lax.rem(y + y_off[p], n_y)

    def first_hop_zc(base, send, mid, group):
        ys = pl.ds(group * y_part, y_part)
        for p in range(n_zc):
            source, goal = send.at[ys, p, :, left], mid.at[zc, ys]
            if zc_off[p]:
                send_to(base, y * n_zc + zc_at(p), source, goal, base + 2 * group)
            else:
                pltpu.make_async_copy(source, goal, rsem.at[base + 2 * group]).start()

    def first_hop_y(base, send, mid, group):
        zcs = pl.ds(group * zc_part, zc_part)
        for p in range(n_y):
            source, goal = send.at[p, zcs, :, right], mid.at[y, zcs]
            if y_off[p]:
                send_to(base + 1, y_at(p) * n_zc + zc, source, goal, base + 1 + 2 * group)
            else:
                pltpu.make_async_copy(source, goal, rsem.at[base + 1 + 2 * group]).start()

    def second_hop_y(base, mid, recv, group):
        copies(mid.at[:, pl.ds(group * y_part, y_part)], rsem.at[base + 2 * group]).wait()
        for p in range(group * y_part, (group + 1) * y_part):
            source, goal = mid.at[:, p], recv.at[y, :, :, left]
            if y_off[p]:
                send_to(base + 2, y_at(p) * n_zc + zc, source, goal, base + 4)
            else:
                pltpu.make_async_copy(source, goal, rsem.at[base + 4]).start()

    def second_hop_zc(base, mid, recv, group):
        copies(mid.at[:, pl.ds(group * zc_part, zc_part)], rsem.at[base + 1 + 2 * group]).wait()
        for p in range(group * zc_part, (group + 1) * zc_part):
            source, goal = mid.at[:, p], recv.at[:, zc, :, right]
            if zc_off[p]:
                send_to(base + 3, y * n_zc + zc_at(p), source, goal, base + 5)
            else:
                pltpu.make_async_copy(source, goal, rsem.at[base + 5]).start()

    def second_hops(base, mid_a, mid_b, recv):
        for group in range(2):
            second_hop_y(base, mid_a, recv, group)
            second_hop_zc(base, mid_b, recv, group)
        sent.append((base, mid_a.at[pl.ds(0, n_zc - 1)]))
        sent.append((base + 1, mid_b.at[pl.ds(0, n_y - 1)]))
        sent.append((base + 2, mid_b.at[pl.ds(0, n_y - 1)]))
        sent.append((base + 3, mid_a.at[pl.ds(0, n_zc - 1)]))

    def arrived(base, recv):
        copies(recv.at[:, :, :, left], rsem.at[base + 4]).wait()
        copies(recv.at[:, :, :, right], rsem.at[base + 5]).wait()

    fet_s4, gra_s4 = (send.reshape(n_y, n_zc, SLOTS, width) for send in (fet_s, gra_s))
    for group in range(2):
        first_hop_zc(24, fet_s4, fet_a, group)
        first_hop_y(24, fet_s4, fet_b, group)
    place_col = column_of(place[0:1, :])
    etile = min(256, ends)
    for i in range(ends // etile):
        hot_e[i * etile : (i + 1) * etile, :] = hot(
            place_col[i * etile : (i + 1) * etile, :] == iota((etile, slots), 1).astype(F32)
        )

    @pl.loop(0, slots // gtile)
    def _(i):
        at = pl.ds(pl.multiple_of(i * gtile, gtile), gtile)
        hot_et[at, :] = hot((iota((gtile, ends), 0) + i * gtile).astype(F32) == far_place[0:1, :])

    target = column_of(lab[...].astype(F32))

    second_hops(24, fet_a, fet_b, fet_r)

    asked = ids_r2[...].reshape(n_dom, LANES).astype(F32)
    id_row = jnp.concatenate(
        [row_of(ids_column(asked[i * per : (i + 1) * per])) for i in range(slots // gtile)], axis=1
    )

    @pl.loop(0, nodes // tile)
    def _(i):
        at = pl.ds(pl.multiple_of(i * tile, tile), tile)
        hot_gt[at, :] = hot((iota((tile, slots), 0) + i * tile).astype(F32) == id_row)

    arrived(24, fet_r)

    got = fet_r[...].reshape(slots, width)
    head = nn(hot_e[:queries, :], got)
    tail = nn(hot_e[queries:, :], got)
    zprod = (head * tail).astype(BF)
    pre = nn(zprod, wdec1[...]) + b_dec1[...]
    sig = jax.nn.sigmoid(pre)
    hidden = (pre * sig).astype(BF).astype(F32)
    wout = w_dec2[...].astype(F32).reshape(1, width)
    logit = jnp.sum(hidden * wout, axis=1, keepdims=True)
    dlogit = jax.nn.sigmoid(logit) - target
    d_pre = (dlogit * wout * (sig * (1.0 + pre * (1.0 - sig)))).astype(BF)
    grad1 = tn(zprod, d_pre)
    gb1 = jnp.sum(d_pre.astype(F32), axis=0, keepdims=True)
    gd2 = jnp.sum(hidden * dlogit, axis=0, keepdims=True)
    vrow = iota((8, width), 0)
    vecs = jnp.where(vrow == 0, gb1, jnp.where(vrow == 1, gd2, 0.0))
    crows = width // 2
    zrows = crows // n_z
    for h in range(2):
        dc_s[h, :crows] = grad1[h * crows : (h + 1) * crows]
        dc_s[h, crows:] = vecs
    other = 1 - core
    pair = pltpu.make_async_remote_copy(
        src_ref=dc_s.at[other], dst_ref=dc_r, send_sem=ssem.at[12], recv_sem=rsem.at[12],
        device_id={"dom": y * n_zc + 2 * z + other}, device_id_type=MESH,
    )
    pair.start()

    def along_z(index, source, goal, sent_size):
        for k in far_first(n_z):
            peer = lax.rem(z + k, n_z)
            pltpu.make_async_remote_copy(
                src_ref=source(peer), dst_ref=goal(z), send_sem=ssem.at[index], recv_sem=rsem.at[index],
                device_id={"dom": y * n_zc + 2 * peer + core}, device_id_type=MESH,
            ).start()
        pltpu.make_async_copy(source(z), goal(z), rsem.at[index]).start()
        sent.append((index, sent_size))

    dz = nt(d_pre, wdec1[...])
    gpair[:queries, :] = (dz * tail).astype(BF)
    gpair[queries:, :] = (dz * head).astype(BF)

    @pl.loop(0, slots // gtile)
    def _(i):
        at = pl.ds(pl.multiple_of(i * gtile, gtile), gtile)
        block = nn(hot_et[at, :], gpair[...]).astype(BF)
        gra_s[pl.ds(i * per, per)] = block.reshape(per, SLOTS, width)

    for group in range(2):
        first_hop_y(30, gra_s4, gra_b, group)

    pair.wait_recv()
    for j in range(n_z):
        dz_s[j, :zrows] = (dc_s[core, j * zrows : (j + 1) * zrows] + dc_r[j * zrows : (j + 1) * zrows]).astype(BF)
        dz_s[j, zrows:] = (dc_s[core, crows:] + dc_r[crows:]).astype(BF)
    along_z(13, lambda p: dz_s.at[p], lambda m: dz_r.at[m], dz_s.at[pl.ds(0, n_z - 1)])

    for group in range(2):
        first_hop_zc(30, gra_s4, gra_a, group)

    copies(dz_r, rsem.at[13]).wait()
    total = dz_r[0].astype(F32)
    for j in range(1, n_z):
        total = total + dz_r[j].astype(F32)
    zbuf[...] = total.astype(BF)
    along_y(14, lambda p: zbuf, lambda m: dy_r.at[m], dy_r.at[pl.ds(0, n_y - 1)])

    second_hops(30, gra_a, gra_b, gra_r)

    copies(dy_r, rsem.at[14]).wait()
    total = dy_r[0].astype(F32)
    for j in range(1, n_y):
        total = total + dy_r[j].astype(F32)
    dbuf[...] = total
    for k in range(1, n_x):
        pltpu.make_async_remote_copy(
            src_ref=dbuf, dst_ref=dx_r.at[rep], send_sem=ssem.at[15], recv_sem=rsem.at[15],
            device_id={"rep": lax.rem(rep + k, n_x)}, device_id_type=MESH,
        ).start()
    pltpu.make_async_copy(dbuf, dx_r.at[rep], rsem.at[15]).start()
    sent.append((15, dx_r.at[pl.ds(0, n_x - 1)]))

    copies(dx_r, rsem.at[15]).wait()
    total = dx_r[0]
    for j in range(1, n_x):
        total = total + dx_r[j]
    gv_o[...] = total[zrows:]
    dc_r[:zrows] = total[:zrows]
    along_z(20, lambda p: dc_r.at[pl.ds(0, zrows)], lambda m: dg_r.at[core, m], dg_r.at[0, pl.ds(0, n_z - 1)])

    flip = rep + 1 - 2 * lax.rem(rep, 2)
    wrap = 3 - rep
    wflip = wrap + 1 - 2 * lax.rem(wrap, 2)
    quarter = nodes // n_x
    jtile = min(64, quarter)

    def local_sum(q):
        at = pl.ds(pl.multiple_of(q * quarter, quarter), quarter)
        return nn(hot_gt[at, :], gra_r[...].reshape(slots, width))

    def trade(index, source, goal, partner):
        copy = pltpu.make_async_remote_copy(
            src_ref=source, dst_ref=goal, send_sem=ssem.at[index], recv_sem=rsem.at[index],
            device_id={"rep": partner}, device_id_type=MESH,
        )
        copy.start()
        return copy

    def joined(way, part):
        @pl.loop(0, quarter // jtile)
        def _(i):
            at = pl.ds(pl.multiple_of(i * jtile, jtile), jtile)
            xs2[way, at, :] = (xk[part, at, :] + xr1[way, 1, at, :].astype(F32)).astype(BF)

    arrived(30, gra_r)
    part = local_sum(wflip)
    xs1[0, 1] = part[:, :half].astype(BF)
    xs1[1, 1] = part[:, half:].astype(BF)
    part = local_sum(flip)
    xs1[0, 0] = part[:, :half].astype(BF)
    one = trade(16, xs1.at[0], xr1.at[0], flip)
    xk[3] = part[:, half:]
    part = local_sum(wrap)
    xs1[1, 0] = part[:, half:].astype(BF)
    two = trade(17, xs1.at[1], xr1.at[1], wrap)
    xk[2] = part[:, :half]
    part = local_sum(rep)
    xk[0] = part[:, :half]
    xk[1] = part[:, half:]
    one.wait_recv()
    joined(0, 2)
    three = trade(18, xs2.at[0], xr2.at[0], wrap)
    two.wait_recv()
    joined(1, 3)
    four = trade(19, xs2.at[1], xr2.at[1], flip)

    copies(dg_r.at[0], rsem.at[20]).wait()
    last = pltpu.make_async_remote_copy(
        src_ref=dg_r.at[core], dst_ref=dg_r.at[core], send_sem=ssem.at[21], recv_sem=rsem.at[21],
        device_id={"dom": y * n_zc + 2 * z + other}, device_id_type=MESH,
    )
    last.start()

    three.wait_recv()
    ge_o[:, :half] = xk[0] + xr1[0, 0].astype(F32) + xr2[0].astype(F32)
    four.wait_recv()
    ge_o[:, half:] = xk[1] + xr1[1, 0].astype(F32) + xr2[1].astype(F32)

    drain()
    pair.wait_send()
    for copy in (one, two, three, four):
        copy.wait_send()
    last.wait()
    gd_o[...] = dg_r[...].reshape(width, width)


def put_out(emb, ge, gd, gv, emb_h, ge_h, gd_h, gb_h, g2_h, sem):
    pairs = ((emb, emb_h), (ge, ge_h), (gd, gd_h), (gv.at[pl.ds(0, 1)], gb_h), (gv.at[pl.ds(1, 1)], g2_h))
    copies_out = [pltpu.make_async_copy(src, dst, sem.at[i]) for i, (src, dst) in enumerate(pairs)]
    for copy in copies_out:
        copy.start()
    for copy in copies_out:
        copy.wait()


def per_device(
    feats, history, adj_inner, adj_halo, halo_rows, w_self, w_nbr, b_enc,
    edge_owner, edge_rows, labels, w_dec1, b_dec1, w_dec2,
):
    n_dom, n_x = lax.axis_size("dom"), lax.axis_size("rep")
    n_zc = 16 if n_dom == 128 else 4
    n_y = n_dom // n_zc
    nodes, width = feats.shape
    halos = adj_halo.shape[1]
    queries = edge_owner.shape[0]
    ends = 2 * queries
    slots = n_dom * SLOTS
    half = width // 2
    n_z = n_zc // 2
    quarter = nodes // n_x
    crows = width // 2
    zrows = crows // n_z
    vmem = pl.BlockSpec(memory_space=pltpu.VMEM)
    any_ = pl.BlockSpec(memory_space=pl.ANY)
    V = pltpu.VMEM
    outs = pl.pallas_call(
        functools.partial(kernel, n_y, n_zc, n_x),
        out_shape=(
            V((nodes, width), BF),
            V((quarter, width), F32),
            V((width, width), F32),
            V((8, width), F32),
        ),
        in_specs=[any_] * 14,
        out_specs=(vmem,) * 4,
        scratch_shapes=[
            V((2, queries), I32), V((2, queries), I32), V((2, n_dom), I32), V((1, queries), I32), V((1, width), F32),
            V((1, width), F32), V((width,), BF),
            V((nodes, width), BF), V((nodes, width), BF), V((nodes, nodes), BF), V((nodes, halos), BF),
            V((width, width), BF), V((width, width), BF), V((width, width), BF),
            V((n_zc, n_y, LANES), BF), V((n_zc, n_y, LANES), BF), V((n_y, n_zc, LANES), BF), V((n_y, n_zc, LANES), BF),
            V((n_zc, 2, n_y, half), BF), V((n_zc, 2, n_y, half), BF), V((n_y, 2 * n_zc, half), BF),
            V((n_y, 2 * n_zc, half), BF), V((n_zc, 2, n_y, half), BF), V((n_y, 2 * n_zc, half), BF),
            V((n_y, 2 * n_zc, half), BF), V((n_zc, 2, n_y, half), BF), V((halos, width), BF), V((nodes, halos), BF),
            V((nodes, width), F32), V((nodes, width), F32), V((8, ends), F32), V((8, ends), F32),
            V((ends, slots), BF), V((slots, ends), BF), V((slots, nodes), BF), V((nodes, slots), BF),
            V((n_dom, SLOTS, width), BF), V((n_zc, n_y, SLOTS, half), BF), V((n_y, n_zc, SLOTS, half), BF),
            V((n_y, n_zc, SLOTS, width), BF),
            V((n_dom, SLOTS, width), BF), V((n_zc, n_y, SLOTS, half), BF), V((n_y, n_zc, SLOTS, half), BF),
            V((n_y, n_zc, SLOTS, width), BF), V((ends, width), BF),
            V((zrows + 8, width), BF), V((zrows + 8, width), F32),
            V((2, 2, quarter, half), BF), V((2, 2, quarter, half), BF), V((2, quarter, half), BF),
            V((2, quarter, half), BF), V((4, quarter, half), F32),
            V((2, crows + 8, width), F32), V((crows + 8, width), F32),
            V((n_z, zrows + 8, width), BF), V((n_z, zrows + 8, width), BF),
            V((n_y, zrows + 8, width), BF), V((n_x, zrows + 8, width), F32), V((2, n_z, zrows, width), F32),
            pltpu.SemaphoreType.DMA((7,)), pltpu.SemaphoreType.DMA((7,)),
            pltpu.SemaphoreType.DMA((36,)), pltpu.SemaphoreType.DMA((36,)),
        ],
        compiler_params=pltpu.CompilerParams(
            collective_id=0, has_side_effects=True, vmem_limit_bytes=60 * 1024 * 1024
        ),
        name="encode_decode",
    )(
        edge_owner.T, edge_rows.T, halo_rows.T, labels.reshape(1, -1), b_enc.reshape(1, -1), b_dec1.reshape(1, -1),
        w_dec2, feats, history, adj_inner, adj_halo, w_self, w_nbr, w_dec1,
    )
    shapes = ((nodes, width, BF), (quarter, width, F32), (width, width, F32), (1, width, F32), (1, width, F32))
    embed, grad_embed, grad_dec1, bias1, dec2 = pl.pallas_call(
        put_out,
        out_shape=tuple(jax.ShapeDtypeStruct(shape[:2], shape[2]) for shape in shapes),
        in_specs=[vmem] * 4,
        out_specs=(any_,) * 5,
        scratch_shapes=[pltpu.SemaphoreType.DMA((5,))],
        name="put_out",
    )(*[pltpu.with_memory_space_constraint(out, pltpu.VMEM) for out in outs])
    return embed, grad_embed, grad_dec1, bias1.reshape(-1), dec2.reshape(-1)


def solution(mesh):
    placed = (
        P("dom", None), P("dom", None), P("dom", None), P("dom", None), P("dom", None), P(), P(), P(),
        P(("dom", "rep"), None), P(("dom", "rep"), None), P(("dom", "rep")), P(), P(), P(),
    )
    return jax.shard_map(
        per_device,
        mesh=mesh,
        in_specs=placed,
        out_specs=(P("dom", None), P(("dom", "rep"), None), P(), P(), P()),
        check_vma=False,
    )
```

```python
import functools

import jax
import jax.numpy as jnp
from jax import lax
from jax.experimental import pallas as pl
from jax.experimental.pallas import tpu as pltpu
from jax.sharding import PartitionSpec as P

BF = jnp.bfloat16
F32 = jnp.float32
I32 = jnp.int32
MESH = pl.DeviceIdType.MESH
SLOTS = 8
LANES = 128


def log2(value):
    return value.bit_length() - 1


def iota(shape, dim):
    return lax.broadcasted_iota(I32, shape, dim)


def nn(a, b):
    return lax.dot_general(a, b, (((1,), (0,)), ((), ())), preferred_element_type=F32)


def nt(a, b):
    return lax.dot_general(a, b, (((1,), (1,)), ((), ())), preferred_element_type=F32)


def tn(a, b):
    return lax.dot_general(a, b, (((0,), (0,)), ((), ())), preferred_element_type=F32)


def hot(cond):
    return jnp.where(cond, 1.0, 0.0).astype(BF)


def column_of(row):
    n = row.shape[1]
    return jnp.sum(jnp.where(iota((n, n), 0) == iota((n, n), 1), row, 0.0), axis=1, keepdims=True)


def row_of(column):
    n = column.shape[0]
    return jnp.sum(jnp.where(iota((n, n), 0) == iota((n, n), 1), column, 0.0), axis=0, keepdims=True)


def far_first(n):
    return sorted(range(1, n), key=lambda k: -min(k, n - k))


def offset_at(place, n):
    return jnp.where((place & 1) == 1, n // 2 - ((place + 1) >> 1), n // 2 + (place >> 1))


def place_of(offset, n):
    d = (offset & (n - 1)) - n // 2
    return jnp.where(d < 0, -2 * d - 1, 2 * d)


def far_places(n):
    return [n // 2 - (p + 1) // 2 if p % 2 else n // 2 + p // 2 for p in range(n)]


def copies(ref, sem):
    return pltpu.make_async_copy(ref, ref, sem)


def kernel(
    n_y, n_zc, n_x,
    eo_h, er_h, hr_h, lab_h, b_enc_h, b_dec1_h, w_dec2_h,
    feats_h, hist_h, adji_h, adjh_h, wself_h, wnbr_h, wdec1_h,
    emb_o, ge_o, gd_o, gv_o,
    eo, er, hr, lab, b_enc, b_dec1, w_dec2,
    feats, hist, adji, adjh, wself, wnbr, wdec1,
    ids_s, ids_r1, ids_t, ids_r2,
    hal_s, hal_r1, hal_t, hal_r2, hal_m, hal_u, hal_v, hal_w, halo, turn, back, adjp,
    inner, selfp, place, far_place,
    hot_e, hot_et, hot_g, hot_gt,
    fet_s, fet_a, fet_b, fet_r,
    gra_s, gra_a, gra_b, gra_r, gpair,
    zbuf, dbuf,
    xs1, xr1, xs2, xr2, xk,
    dc_s, dc_r, dz_s, dz_r, dy_r, dx_r, dg_r,
    small_sem, load_sem,
    ssem, rsem,
):
    n_dom = n_y * n_zc
    nodes, width = feats.shape
    half = width // 2
    queries = eo.shape[1]
    ends = 2 * queries
    slots = n_dom * SLOTS
    halos = 2 * n_dom
    n_z = n_zc // 2
    ly, lzc = log2(n_y), log2(n_zc)
    me = lax.axis_index("dom")
    rep = lax.axis_index("rep")
    y = lax.div(me, n_zc)
    zc = lax.rem(me, n_zc)
    z = lax.div(zc, 2)
    core = lax.rem(zc, 2)

    small = [
        pltpu.make_async_copy(src, dst, small_sem.at[i])
        for i, (src, dst) in enumerate(
            ((eo_h, eo), (er_h, er), (hr_h, hr), (lab_h, lab), (b_enc_h, b_enc), (b_dec1_h, b_dec1), (w_dec2_h, w_dec2))
        )
    ]
    loads = [
        pltpu.make_async_copy(src, dst, load_sem.at[i])
        for i, (src, dst) in enumerate(
            ((feats_h, feats), (adji_h, adji), (wself_h, wself), (adjh_h, adjh), (hist_h, hist), (wnbr_h, wnbr), (wdec1_h, wdec1))
        )
    ]
    barrier = pltpu.get_barrier_semaphore()

    def zc_peer(k):
        return lax.rem(zc + k, n_zc)

    def y_peer(k):
        return lax.rem(y + k, n_y)

    for k in far_first(n_zc):
        pl.semaphore_signal(barrier, inc=1, device_id={"dom": y * n_zc + zc_peer(k)}, device_id_type=MESH)
    for k in far_first(n_y):
        pl.semaphore_signal(barrier, inc=1, device_id={"dom": y_peer(k) * n_zc + zc}, device_id_type=MESH)
    for k in range(1, n_x):
        pl.semaphore_signal(barrier, inc=1, device_id={"rep": lax.rem(rep + k, n_x)}, device_id_type=MESH)

    sent = []

    def drain():
        for index, size in sent:
            copies(size, ssem.at[index]).wait()

    def along_zc(index, source, target, sent_size):
        for k in far_first(n_zc):
            peer = zc_peer(k)
            pltpu.make_async_remote_copy(
                src_ref=source(peer), dst_ref=target(zc), send_sem=ssem.at[index], recv_sem=rsem.at[index],
                device_id={"dom": y * n_zc + peer}, device_id_type=MESH,
            ).start()
        pltpu.make_async_copy(source(zc), target(zc), rsem.at[index]).start()
        sent.append((index, sent_size))

    def along_y(index, source, target, sent_size):
        for k in far_first(n_y):
            peer = y_peer(k)
            pltpu.make_async_remote_copy(
                src_ref=source(peer), dst_ref=target(y), send_sem=ssem.at[index], recv_sem=rsem.at[index],
                device_id={"dom": peer * n_zc + zc}, device_id_type=MESH,
            ).start()
        pltpu.make_async_copy(source(y), target(y), rsem.at[index]).start()
        sent.append((index, sent_size))

    for load in small + loads:
        load.start()
    for load in small:
        load.wait()

    owner = jnp.concatenate([eo[0:1, :], eo[1:2, :]], axis=1)
    local = jnp.concatenate([er[0:1, :], er[1:2, :]], axis=1)
    rows = iota((n_dom, ends), 0)
    turned = ((rows & (n_y - 1)) << lzc) + (rows >> ly)
    match = owner == turned
    match_hot = hot(match)
    before = hot(iota((ends, ends), 0) < iota((ends, ends), 1))
    rank = nn(match_hot, before)
    slot = jnp.sum(jnp.where(match, rank, 0.0), axis=0, keepdims=True)
    place[...] = jnp.broadcast_to(owner.astype(F32) * float(SLOTS) + slot, place.shape)
    far = (place_of((owner >> lzc) - y, n_y) << lzc) + place_of((owner & (n_zc - 1)) - zc, n_zc)
    far_place[...] = jnp.broadcast_to(far.astype(F32) * float(SLOTS) + slot, far_place.shape)

    def lane_rows(at, value):
        lane = iota((LANES, value.shape[1]), 0)
        part = jnp.where(lane < 16, value >> 5, value & 31)
        return jnp.where(at & (lane < 32), part.astype(F32), 0.0).astype(BF)

    wanted = lane_rows(slot == (iota((LANES, ends), 0) & 15).astype(F32), local)
    lane = iota((LANES, n_dom), 0) & 15
    halo_ids = jnp.where(lane == SLOTS, hr[0:1, :], hr[1:2, :])
    halo_wanted = lane_rows((lane == SLOTS) | (lane == SLOTS + 1), halo_ids)
    prow, pcol = iota((n_dom, n_dom), 0), iota((n_dom, n_dom), 1)
    to_zc_y = hot(pcol == ((prow & (n_y - 1)) << lzc) + (prow >> ly))
    to_y_zc = hot(pcol == ((prow & (n_zc - 1)) << ly) + (prow >> lzc))
    requests = nt(match_hot, wanted) + nt(to_zc_y, halo_wanted)
    ids_s[...] = requests.astype(BF).reshape(n_zc, n_y, LANES)

    pl.semaphore_wait(barrier, (n_zc - 1) + (n_y - 1) + (n_x - 1))
    along_zc(0, lambda p: ids_s.at[p], lambda m: ids_r1.at[m], ids_s.at[pl.ds(0, n_zc - 1)])

    tile = min(256, nodes)
    loads[0].wait()
    loads[1].wait()

    @pl.loop(0, nodes // tile)
    def _(i):
        at = pl.ds(pl.multiple_of(i * tile, tile), tile)
        inner[at, :] = nn(adji[at, :], feats[...])

    copies(ids_r1, rsem.at[0]).wait()
    ids_t[...] = nn(to_y_zc, ids_r1[...].reshape(n_dom, LANES)).astype(BF).reshape(n_y, n_zc, LANES)
    along_y(1, lambda p: ids_t.at[p], lambda m: ids_r2.at[m], ids_t.at[pl.ds(0, n_y - 1)])

    loads[2].wait()
    loads[3].wait()

    @pl.loop(0, nodes // tile)
    def _(i):
        at = pl.ds(pl.multiple_of(i * tile, tile), tile)
        selfp[at, :] = nn(feats[at, :], wself[...]) + b_enc[...]

    ko, jo = iota((halos, halos), 0), iota((halos, halos), 1)
    std = ((((jo >> (lzc + 1)) << lzc) + (jo & (n_zc - 1))) << 1) + ((jo >> lzc) & 1)
    adjp[...] = nn(adjh[...], hot(ko == std)).astype(BF)

    io, oo = iota((halos, halos), 1), iota((halos, halos), 0)
    turn[...] = hot(io == ((oo & (n_zc - 1)) << (ly + 1)) + (((oo >> lzc) & 1) << ly) + (oo >> (lzc + 1)))
    back[...] = hot(io == ((oo & (n_y - 1)) << (lzc + 1)) + (((oo >> ly) & 1) << lzc) + (oo >> (ly + 1)))

    for i in (4, 5, 6):
        loads[i].wait()

    copies(ids_r2, rsem.at[1]).wait()
    asked = nn(to_zc_y, ids_r2[...].reshape(n_dom, LANES))
    asked_c = [32.0 * asked[:, at : at + 1] + asked[:, at + 16 : at + 17] for at in (SLOTS, SLOTS + 1)]
    pick = hot(jnp.concatenate(asked_c, axis=0) == iota((halos, nodes), 1).astype(F32))
    picked = nn(pick, hist[...]).astype(BF)
    for c in range(2):
        hal_s[:, c] = picked[c * n_dom : (c + 1) * n_dom, :half].reshape(n_zc, n_y, half)
        hal_m[:, c] = picked[c * n_dom : (c + 1) * n_dom, half:].reshape(n_zc, n_y, half)
    along_zc(2, lambda p: hal_s.at[p], lambda m: hal_r1.at[m], hal_s.at[pl.ds(0, n_zc - 1)])
    hal_u[...] = nn(turn[...], hal_m[...].reshape(halos, half)).astype(BF).reshape(n_y, 2 * n_zc, half)
    along_y(22, lambda p: hal_u.at[p], lambda m: hal_v.at[m], hal_u.at[pl.ds(0, n_y - 1)])

    gtile = min(256, slots)
    per = gtile // SLOTS

    def ids_column(asked):
        n = asked.shape[0] * SLOTS
        spread = jnp.broadcast_to(asked[:, None, :], (asked.shape[0], SLOTS, LANES)).reshape(n, LANES)
        lane, mine = iota((n, LANES), 1), iota((n, LANES), 0) & (SLOTS - 1)
        weight = jnp.where(lane == mine, 32.0, jnp.where(lane == mine + 16, 1.0, 0.0))
        return jnp.sum(spread * weight, axis=1, keepdims=True)

    by_y = (offset_at(prow >> lzc, n_y) + y) & (n_y - 1)
    by_zc = (offset_at(prow & (n_zc - 1), n_zc) + zc) & (n_zc - 1)
    asked_far = nn(hot(pcol == (by_y << lzc) + by_zc), ids_r2[...].reshape(n_dom, LANES))

    def rows_named(tiles):
        for i in tiles:
            id_col = ids_column(asked_far[i * per : (i + 1) * per])
            hot_g[i * gtile : (i + 1) * gtile, :] = hot(id_col == iota((gtile, nodes), 1).astype(F32))

    tiles = slots // gtile
    rows_named(range(tiles // 2))

    copies(hal_r1, rsem.at[2]).wait()
    hal_t[...] = nn(turn[...], hal_r1[...].reshape(halos, half)).astype(BF).reshape(n_y, 2 * n_zc, half)
    along_y(3, lambda p: hal_t.at[p], lambda m: hal_r2.at[m], hal_t.at[pl.ds(0, n_y - 1)])
    copies(hal_v, rsem.at[22]).wait()
    hal_m[...] = nn(back[...], hal_v[...].reshape(halos, half)).astype(BF).reshape(n_zc, 2, n_y, half)
    along_zc(23, lambda p: hal_m.at[p], lambda m: hal_w.at[m], hal_m.at[pl.ds(0, n_zc - 1)])

    rows_named(range(tiles // 2, tiles))

    copies(hal_r2, rsem.at[3]).wait()
    copies(hal_w, rsem.at[23]).wait()
    halo[:, :half] = hal_r2[...].reshape(halos, half)
    halo[:, half:] = nn(turn[...], hal_w[...].reshape(halos, half)).astype(BF)

    @pl.loop(0, nodes // tile)
    def _(i):
        at = pl.ds(pl.multiple_of(i * tile, tile), tile)
        agg = (inner[at, :] + nn(adjp[at, :], halo[...])).astype(BF)
        emb_o[at, :] = jnp.maximum(selfp[at, :] + nn(agg, wnbr[...]), 0.0).astype(BF)

    left, right = pl.ds(0, half), pl.ds(half, half)

    y_off, zc_off = far_places(n_y), far_places(n_zc)
    y_part, zc_part = n_y // 2, n_zc // 2

    def send_to(index, peer, source, goal, signal):
        pltpu.make_async_remote_copy(
            src_ref=source, dst_ref=goal, send_sem=ssem.at[index], recv_sem=rsem.at[signal],
            device_id={"dom": peer}, device_id_type=MESH,
        ).start()

    def zc_at(p):
        return lax.rem(zc + zc_off[p], n_zc)

    def y_at(p):
        return lax.rem(y + y_off[p], n_y)

    def first_hop_zc(base, send, mid, group):
        ys = pl.ds(group * y_part, y_part)
        for p in range(n_zc):
            source, goal = send.at[ys, p, :, left], mid.at[zc, ys]
            if zc_off[p]:
                send_to(base, y * n_zc + zc_at(p), source, goal, base + 2 * group)
            else:
                pltpu.make_async_copy(source, goal, rsem.at[base + 2 * group]).start()

    def first_hop_y(base, send, mid, group, places):
        zcs = pl.ds(group * zc_part, zc_part)
        for p in places:
            source, goal = send.at[p, zcs, :, right], mid.at[y, zcs]
            if y_off[p]:
                send_to(base + 1, y_at(p) * n_zc + zc, source, goal, base + 1 + 2 * group)
            else:
                pltpu.make_async_copy(source, goal, rsem.at[base + 1 + 2 * group]).start()

    def second_hop_y(base, mid, recv, group):
        copies(mid.at[:, pl.ds(group * y_part, y_part)], rsem.at[base + 2 * group]).wait()
        for p in range(group * y_part, (group + 1) * y_part):
            source, goal = mid.at[:, p], recv.at[y, :, :, left]
            if y_off[p]:
                send_to(base + 2, y_at(p) * n_zc + zc, source, goal, base + 4)
            else:
                pltpu.make_async_copy(source, goal, rsem.at[base + 4]).start()

    def second_hop_zc(base, mid, recv, group):
        copies(mid.at[:, pl.ds(group * zc_part, zc_part)], rsem.at[base + 1 + 2 * group]).wait()
        for p in range(group * zc_part, (group + 1) * zc_part):
            source, goal = mid.at[:, p], recv.at[:, zc, :, right]
            if zc_off[p]:
                send_to(base + 3, y * n_zc + zc_at(p), source, goal, base + 5)
            else:
                pltpu.make_async_copy(source, goal, rsem.at[base + 5]).start()

    def second_hops(base, mid_a, mid_b, recv, group):
        second_hop_y(base, mid_a, recv, group)
        second_hop_zc(base, mid_b, recv, group)
        if group == 0:
            return
        sent.append((base, mid_a.at[pl.ds(0, n_zc - 1)]))
        sent.append((base + 1, mid_b.at[pl.ds(0, n_y - 1)]))
        sent.append((base + 2, mid_b.at[pl.ds(0, n_y - 1)]))
        sent.append((base + 3, mid_a.at[pl.ds(0, n_zc - 1)]))

    def arrived(base, recv):
        copies(recv.at[:, :, :, left], rsem.at[base + 4]).wait()
        copies(recv.at[:, :, :, right], rsem.at[base + 5]).wait()

    fet_s4, gra_s4 = (send.reshape(n_y, n_zc, SLOTS, width) for send in (fet_s, gra_s))
    far_y, near_y = range(y_part), range(y_part, n_y)

    def selected(select, rows, goal, low, high):
        @pl.loop(low, high)
        def _(i):
            at = pl.ds(pl.multiple_of(i * gtile, gtile), gtile)
            goal[pl.ds(i * per, per)] = nn(select[at, :], rows[...]).astype(BF).reshape(per, SLOTS, width)

    selected(hot_g, emb_o, fet_s, 0, tiles // 2)
    first_hop_zc(24, fet_s4, fet_a, 0)
    first_hop_y(24, fet_s4, fet_b, 0, far_y)
    selected(hot_g, emb_o, fet_s, tiles // 2, tiles)
    first_hop_y(24, fet_s4, fet_b, 0, near_y)
    first_hop_zc(24, fet_s4, fet_a, 1)
    first_hop_y(24, fet_s4, fet_b, 1, range(n_y))
    place_col = column_of(place[0:1, :])
    etile = min(256, ends)
    for i in range(ends // etile):
        hot_e[i * etile : (i + 1) * etile, :] = hot(
            place_col[i * etile : (i + 1) * etile, :] == iota((etile, slots), 1).astype(F32)
        )

    @pl.loop(0, slots // gtile)
    def _(i):
        at = pl.ds(pl.multiple_of(i * gtile, gtile), gtile)
        hot_et[at, :] = hot((iota((gtile, ends), 0) + i * gtile).astype(F32) == far_place[0:1, :])

    target = column_of(lab[...].astype(F32))

    second_hops(24, fet_a, fet_b, fet_r, 0)
    second_hops(24, fet_a, fet_b, fet_r, 1)

    asked = ids_r2[...].reshape(n_dom, LANES).astype(F32)
    id_row = jnp.concatenate(
        [row_of(ids_column(asked[i * per : (i + 1) * per])) for i in range(slots // gtile)], axis=1
    )

    @pl.loop(0, nodes // tile)
    def _(i):
        at = pl.ds(pl.multiple_of(i * tile, tile), tile)
        hot_gt[at, :] = hot((iota((tile, slots), 0) + i * tile).astype(F32) == id_row)

    arrived(24, fet_r)

    got = fet_r[...].reshape(slots, width)
    head = nn(hot_e[:queries, :], got)
    tail = nn(hot_e[queries:, :], got)
    zprod = (head * tail).astype(BF)
    pre = nn(zprod, wdec1[...]) + b_dec1[...]
    sig = jax.nn.sigmoid(pre)
    hidden = (pre * sig).astype(BF).astype(F32)
    wout = w_dec2[...].astype(F32).reshape(1, width)
    logit = jnp.sum(hidden * wout, axis=1, keepdims=True)
    dlogit = jax.nn.sigmoid(logit) - target
    d_pre = (dlogit * wout * (sig * (1.0 + pre * (1.0 - sig)))).astype(BF)
    grad1 = tn(zprod, d_pre)
    gb1 = jnp.sum(d_pre.astype(F32), axis=0, keepdims=True)
    gd2 = jnp.sum(hidden * dlogit, axis=0, keepdims=True)
    vrow = iota((8, width), 0)
    vecs = jnp.where(vrow == 0, gb1, jnp.where(vrow == 1, gd2, 0.0))
    crows = width // 2
    zrows = crows // n_z
    for h in range(2):
        dc_s[h, :crows] = grad1[h * crows : (h + 1) * crows]
        dc_s[h, crows:] = vecs
    other = 1 - core
    pair = pltpu.make_async_remote_copy(
        src_ref=dc_s.at[other], dst_ref=dc_r, send_sem=ssem.at[12], recv_sem=rsem.at[12],
        device_id={"dom": y * n_zc + 2 * z + other}, device_id_type=MESH,
    )
    pair.start()

    def along_z(index, source, goal, sent_size):
        for k in far_first(n_z):
            peer = lax.rem(z + k, n_z)
            pltpu.make_async_remote_copy(
                src_ref=source(peer), dst_ref=goal(z), send_sem=ssem.at[index], recv_sem=rsem.at[index],
                device_id={"dom": y * n_zc + 2 * peer + core}, device_id_type=MESH,
            ).start()
        pltpu.make_async_copy(source(z), goal(z), rsem.at[index]).start()
        sent.append((index, sent_size))

    dz = nt(d_pre, wdec1[...])
    gpair[:queries, :] = (dz * tail).astype(BF)
    gpair[queries:, :] = (dz * head).astype(BF)

    selected(hot_et, gpair, gra_s, 0, tiles // 2)
    first_hop_y(30, gra_s4, gra_b, 0, far_y)

    pair.wait_recv()
    for j in range(n_z):
        dz_s[j, :zrows] = (dc_s[core, j * zrows : (j + 1) * zrows] + dc_r[j * zrows : (j + 1) * zrows]).astype(BF)
        dz_s[j, zrows:] = (dc_s[core, crows:] + dc_r[crows:]).astype(BF)
    along_z(13, lambda p: dz_s.at[p], lambda m: dz_r.at[m], dz_s.at[pl.ds(0, n_z - 1)])
    first_hop_zc(30, gra_s4, gra_a, 0)
    selected(hot_et, gpair, gra_s, tiles // 2, tiles)
    first_hop_y(30, gra_s4, gra_b, 0, near_y)

    first_hop_zc(30, gra_s4, gra_a, 1)
    first_hop_y(30, gra_s4, gra_b, 1, range(n_y))

    copies(dz_r, rsem.at[13]).wait()
    total = dz_r[0].astype(F32)
    for j in range(1, n_z):
        total = total + dz_r[j].astype(F32)
    zbuf[...] = total.astype(BF)
    along_y(14, lambda p: zbuf, lambda m: dy_r.at[m], dy_r.at[pl.ds(0, n_y - 1)])

    second_hops(30, gra_a, gra_b, gra_r, 0)
    second_hops(30, gra_a, gra_b, gra_r, 1)

    copies(dy_r, rsem.at[14]).wait()
    total = dy_r[0].astype(F32)
    for j in range(1, n_y):
        total = total + dy_r[j].astype(F32)
    dbuf[...] = total
    for k in range(1, n_x):
        pltpu.make_async_remote_copy(
            src_ref=dbuf, dst_ref=dx_r.at[rep], send_sem=ssem.at[15], recv_sem=rsem.at[15],
            device_id={"rep": lax.rem(rep + k, n_x)}, device_id_type=MESH,
        ).start()
    pltpu.make_async_copy(dbuf, dx_r.at[rep], rsem.at[15]).start()
    sent.append((15, dx_r.at[pl.ds(0, n_x - 1)]))

    flip = rep + 1 - 2 * lax.rem(rep, 2)
    wrap = 3 - rep
    wflip = wrap + 1 - 2 * lax.rem(wrap, 2)
    quarter = nodes // n_x
    jtile = min(64, quarter)

    crow = quarter // 2
    chunks = [(ch, pl.ds(ch * crow, crow)) for ch in range(2)]

    def local_sum(q, ch):
        at = pl.ds(pl.multiple_of(q * quarter + ch * crow, crow), crow)
        return nn(hot_gt[at, :], gra_r[...].reshape(slots, width))

    def trade(index, source, goal, partner):
        copy = pltpu.make_async_remote_copy(
            src_ref=source, dst_ref=goal, send_sem=ssem.at[index], recv_sem=rsem.at[index],
            device_id={"rep": partner}, device_id_type=MESH,
        )
        copy.start()
        return copy

    def joined(way, part, ch):
        @pl.loop(0, crow // jtile)
        def _(i):
            at = pl.ds(pl.multiple_of(ch * crow + i * jtile, jtile), jtile)
            xs2[way, at, :] = (xk[part, at, :] + xr1[way, 1, at, :].astype(F32)).astype(BF)

    arrived(30, gra_r)
    firsts, seconds = [], []
    for ch, at in chunks:
        part = local_sum(wflip, ch)
        xs1[0, 1, at] = part[:, :half].astype(BF)
        xs1[1, 1, at] = part[:, half:].astype(BF)
        part = local_sum(flip, ch)
        xs1[0, 0, at] = part[:, :half].astype(BF)
        one = trade(36 + ch, xs1.at[0, :, at], xr1.at[0, :, at], flip)
        xk[3, at] = part[:, half:]
        part = local_sum(wrap, ch)
        xs1[1, 0, at] = part[:, half:].astype(BF)
        two = trade(38 + ch, xs1.at[1, :, at], xr1.at[1, :, at], wrap)
        xk[2, at] = part[:, :half]
        firsts.append((one, two))

    copies(dx_r, rsem.at[15]).wait()
    total = dx_r[0]
    for j in range(1, n_x):
        total = total + dx_r[j]
    gv_o[...] = total[zrows:]
    dc_r[:zrows] = total[:zrows]
    along_z(20, lambda p: dc_r.at[pl.ds(0, zrows)], lambda m: dg_r.at[core, m], dg_r.at[0, pl.ds(0, n_z - 1)])

    for ch, at in chunks:
        part = local_sum(rep, ch)
        xk[0, at] = part[:, :half]
        xk[1, at] = part[:, half:]
    for ch, at in chunks:
        one, two = firsts[ch]
        one.wait_recv()
        joined(0, 2, ch)
        three = trade(40 + ch, xs2.at[0, at], xr2.at[0, at], wrap)
        two.wait_recv()
        joined(1, 3, ch)
        four = trade(42 + ch, xs2.at[1, at], xr2.at[1, at], flip)
        seconds.append((three, four))

    copies(dg_r.at[0], rsem.at[20]).wait()
    last = pltpu.make_async_remote_copy(
        src_ref=dg_r.at[core], dst_ref=dg_r.at[core], send_sem=ssem.at[21], recv_sem=rsem.at[21],
        device_id={"dom": y * n_zc + 2 * z + other}, device_id_type=MESH,
    )
    last.start()

    for ch, at in chunks:
        three, four = seconds[ch]
        three.wait_recv()
        ge_o[at, :half] = xk[0, at] + xr1[0, 0, at].astype(F32) + xr2[0, at].astype(F32)
        four.wait_recv()
        ge_o[at, half:] = xk[1, at] + xr1[1, 0, at].astype(F32) + xr2[1, at].astype(F32)

    drain()
    pair.wait_send()
    for pair_of in firsts + seconds:
        for copy in pair_of:
            copy.wait_send()
    last.wait()
    gd_o[...] = dg_r[...].reshape(width, width)


def put_out(emb, ge, gd, gv, emb_h, ge_h, gd_h, gb_h, g2_h, sem):
    pairs = ((emb, emb_h), (ge, ge_h), (gd, gd_h), (gv.at[pl.ds(0, 1)], gb_h), (gv.at[pl.ds(1, 1)], g2_h))
    copies_out = [pltpu.make_async_copy(src, dst, sem.at[i]) for i, (src, dst) in enumerate(pairs)]
    for copy in copies_out:
        copy.start()
    for copy in copies_out:
        copy.wait()


def per_device(
    feats, history, adj_inner, adj_halo, halo_rows, w_self, w_nbr, b_enc,
    edge_owner, edge_rows, labels, w_dec1, b_dec1, w_dec2,
):
    n_dom, n_x = lax.axis_size("dom"), lax.axis_size("rep")
    n_zc = 16 if n_dom == 128 else 4
    n_y = n_dom // n_zc
    nodes, width = feats.shape
    halos = adj_halo.shape[1]
    queries = edge_owner.shape[0]
    ends = 2 * queries
    slots = n_dom * SLOTS
    half = width // 2
    n_z = n_zc // 2
    quarter = nodes // n_x
    crows = width // 2
    zrows = crows // n_z
    vmem = pl.BlockSpec(memory_space=pltpu.VMEM)
    any_ = pl.BlockSpec(memory_space=pl.ANY)
    V = pltpu.VMEM
    outs = pl.pallas_call(
        functools.partial(kernel, n_y, n_zc, n_x),
        out_shape=(
            V((nodes, width), BF),
            V((quarter, width), F32),
            V((width, width), F32),
            V((8, width), F32),
        ),
        in_specs=[any_] * 14,
        out_specs=(vmem,) * 4,
        scratch_shapes=[
            V((2, queries), I32), V((2, queries), I32), V((2, n_dom), I32), V((1, queries), I32), V((1, width), F32),
            V((1, width), F32), V((width,), BF),
            V((nodes, width), BF), V((nodes, width), BF), V((nodes, nodes), BF), V((nodes, halos), BF),
            V((width, width), BF), V((width, width), BF), V((width, width), BF),
            V((n_zc, n_y, LANES), BF), V((n_zc, n_y, LANES), BF), V((n_y, n_zc, LANES), BF), V((n_y, n_zc, LANES), BF),
            V((n_zc, 2, n_y, half), BF), V((n_zc, 2, n_y, half), BF), V((n_y, 2 * n_zc, half), BF),
            V((n_y, 2 * n_zc, half), BF), V((n_zc, 2, n_y, half), BF), V((n_y, 2 * n_zc, half), BF),
            V((n_y, 2 * n_zc, half), BF), V((n_zc, 2, n_y, half), BF), V((halos, width), BF), V((halos, halos), BF), V((halos, halos), BF), V((nodes, halos), BF),
            V((nodes, width), F32), V((nodes, width), F32), V((8, ends), F32), V((8, ends), F32),
            V((ends, slots), BF), V((slots, ends), BF), V((slots, nodes), BF), V((nodes, slots), BF),
            V((n_dom, SLOTS, width), BF), V((n_zc, n_y, SLOTS, half), BF), V((n_y, n_zc, SLOTS, half), BF),
            V((n_y, n_zc, SLOTS, width), BF),
            V((n_dom, SLOTS, width), BF), V((n_zc, n_y, SLOTS, half), BF), V((n_y, n_zc, SLOTS, half), BF),
            V((n_y, n_zc, SLOTS, width), BF), V((ends, width), BF),
            V((zrows + 8, width), BF), V((zrows + 8, width), F32),
            V((2, 2, quarter, half), BF), V((2, 2, quarter, half), BF), V((2, quarter, half), BF),
            V((2, quarter, half), BF), V((4, quarter, half), F32),
            V((2, crows + 8, width), F32), V((crows + 8, width), F32),
            V((n_z, zrows + 8, width), BF), V((n_z, zrows + 8, width), BF),
            V((n_y, zrows + 8, width), BF), V((n_x, zrows + 8, width), F32), V((2, n_z, zrows, width), F32),
            pltpu.SemaphoreType.DMA((7,)), pltpu.SemaphoreType.DMA((7,)),
            pltpu.SemaphoreType.DMA((44,)), pltpu.SemaphoreType.DMA((44,)),
        ],
        compiler_params=pltpu.CompilerParams(
            collective_id=0, has_side_effects=True, vmem_limit_bytes=60 * 1024 * 1024
        ),
        name="encode_decode",
    )(
        edge_owner.T, edge_rows.T, halo_rows.T, labels.reshape(1, -1), b_enc.reshape(1, -1), b_dec1.reshape(1, -1),
        w_dec2, feats, history, adj_inner, adj_halo, w_self, w_nbr, w_dec1,
    )
    shapes = ((nodes, width, BF), (quarter, width, F32), (width, width, F32), (1, width, F32), (1, width, F32))
    embed, grad_embed, grad_dec1, bias1, dec2 = pl.pallas_call(
        put_out,
        out_shape=tuple(jax.ShapeDtypeStruct(shape[:2], shape[2]) for shape in shapes),
        in_specs=[vmem] * 4,
        out_specs=(any_,) * 5,
        scratch_shapes=[pltpu.SemaphoreType.DMA((5,))],
        name="put_out",
    )(*[pltpu.with_memory_space_constraint(out, pltpu.VMEM) for out in outs])
    return embed, grad_embed, grad_dec1, bias1.reshape(-1), dec2.reshape(-1)


def solution(mesh):
    placed = (
        P("dom", None), P("dom", None), P("dom", None), P("dom", None), P("dom", None), P(), P(), P(),
        P(("dom", "rep"), None), P(("dom", "rep"), None), P(("dom", "rep")), P(), P(), P(),
    )
    return jax.shard_map(
        per_device,
        mesh=mesh,
        in_specs=placed,
        out_specs=(P("dom", None), P(("dom", "rep"), None), P(), P(), P()),
        check_vma=False,
    )
```

```python
import functools

import jax
import jax.numpy as jnp
from jax import lax
from jax.experimental import pallas as pl
from jax.experimental.pallas import tpu as pltpu
from jax.sharding import PartitionSpec as P

BF = jnp.bfloat16
F32 = jnp.float32
I32 = jnp.int32
MESH = pl.DeviceIdType.MESH
SLOTS = 8
LANES = 128


def log2(value):
    return value.bit_length() - 1


def iota(shape, dim):
    return lax.broadcasted_iota(I32, shape, dim)


def nn(a, b):
    return lax.dot_general(a, b, (((1,), (0,)), ((), ())), preferred_element_type=F32)


def nt(a, b):
    return lax.dot_general(a, b, (((1,), (1,)), ((), ())), preferred_element_type=F32)


def tn(a, b):
    return lax.dot_general(a, b, (((0,), (0,)), ((), ())), preferred_element_type=F32)


def hot(cond):
    return jnp.where(cond, 1.0, 0.0).astype(BF)


def column_of(row):
    n = row.shape[1]
    return jnp.sum(jnp.where(iota((n, n), 0) == iota((n, n), 1), row, 0.0), axis=1, keepdims=True)


def row_of(column):
    n = column.shape[0]
    return jnp.sum(jnp.where(iota((n, n), 0) == iota((n, n), 1), column, 0.0), axis=0, keepdims=True)


def far_first(n):
    return sorted(range(1, n), key=lambda k: -min(k, n - k))


def offset_at(place, n):
    return jnp.where((place & 1) == 1, n // 2 - ((place + 1) >> 1), n // 2 + (place >> 1))


def place_of(offset, n):
    d = (offset & (n - 1)) - n // 2
    return jnp.where(d < 0, -2 * d - 1, 2 * d)


def far_places(n):
    return [n // 2 - (p + 1) // 2 if p % 2 else n // 2 + p // 2 for p in range(n)]


def copies(ref, sem):
    return pltpu.make_async_copy(ref, ref, sem)


def kernel(
    n_y, n_zc, n_x,
    eo_h, er_h, hr_h, lab_h, b_enc_h, b_dec1_h, w_dec2_h,
    feats_h, hist_h, adji_h, adjh_h, wself_h, wnbr_h, wdec1_h,
    emb_o, ge_o, gd_o, gv_o,
    eo, er, hr, lab, b_enc, b_dec1, w_dec2,
    feats, hist, adji, adjh, wself, wnbr, wdec1,
    ids_s, ids_r1, ids_t, ids_r2,
    hal_s, hal_r1, hal_t, hal_r2, hal_m, hal_u, hal_v, hal_w, turn, back, adjp, adjq,
    inner, selfp, place, far_place,
    hot_e, hot_et, hot_g, hot_gt,
    fet_s, fet_a, fet_b, fet_r,
    gra_s, gra_a, gra_b, gra_r, gpair,
    zbuf, dbuf,
    xs1, xr1, xs2, xr2, xk,
    dc_s, dc_r, dz_s, dz_r, dy_r, dx_r, dg_r,
    small_sem, load_sem,
    ssem, rsem,
):
    n_dom = n_y * n_zc
    nodes, width = feats.shape
    half = width // 2
    queries = eo.shape[1]
    ends = 2 * queries
    slots = n_dom * SLOTS
    halos = 2 * n_dom
    n_z = n_zc // 2
    ly, lzc = log2(n_y), log2(n_zc)
    me = lax.axis_index("dom")
    rep = lax.axis_index("rep")
    y = lax.div(me, n_zc)
    zc = lax.rem(me, n_zc)
    z = lax.div(zc, 2)
    core = lax.rem(zc, 2)

    small = [
        pltpu.make_async_copy(src, dst, small_sem.at[i])
        for i, (src, dst) in enumerate(
            ((eo_h, eo), (er_h, er), (hr_h, hr), (lab_h, lab), (b_enc_h, b_enc), (b_dec1_h, b_dec1), (w_dec2_h, w_dec2))
        )
    ]
    loads = [
        pltpu.make_async_copy(src, dst, load_sem.at[i])
        for i, (src, dst) in enumerate(
            ((feats_h, feats), (adji_h, adji), (wself_h, wself), (adjh_h, adjh), (hist_h, hist), (wnbr_h, wnbr), (wdec1_h, wdec1))
        )
    ]
    barrier = pltpu.get_barrier_semaphore()

    def zc_peer(k):
        return lax.rem(zc + k, n_zc)

    def y_peer(k):
        return lax.rem(y + k, n_y)

    for k in far_first(n_zc):
        pl.semaphore_signal(barrier, inc=1, device_id={"dom": y * n_zc + zc_peer(k)}, device_id_type=MESH)
    for k in far_first(n_y):
        pl.semaphore_signal(barrier, inc=1, device_id={"dom": y_peer(k) * n_zc + zc}, device_id_type=MESH)
    for k in range(1, n_x):
        pl.semaphore_signal(barrier, inc=1, device_id={"rep": lax.rem(rep + k, n_x)}, device_id_type=MESH)

    sent = []

    def drain():
        for index, size in sent:
            copies(size, ssem.at[index]).wait()

    def along_zc(index, source, target, sent_size):
        for k in far_first(n_zc):
            peer = zc_peer(k)
            pltpu.make_async_remote_copy(
                src_ref=source(peer), dst_ref=target(zc), send_sem=ssem.at[index], recv_sem=rsem.at[index],
                device_id={"dom": y * n_zc + peer}, device_id_type=MESH,
            ).start()
        pltpu.make_async_copy(source(zc), target(zc), rsem.at[index]).start()
        sent.append((index, sent_size))

    def along_y(index, source, target, sent_size):
        for k in far_first(n_y):
            peer = y_peer(k)
            pltpu.make_async_remote_copy(
                src_ref=source(peer), dst_ref=target(y), send_sem=ssem.at[index], recv_sem=rsem.at[index],
                device_id={"dom": peer * n_zc + zc}, device_id_type=MESH,
            ).start()
        pltpu.make_async_copy(source(y), target(y), rsem.at[index]).start()
        sent.append((index, sent_size))

    for load in small + loads:
        load.start()
    for load in small:
        load.wait()

    owner = jnp.concatenate([eo[0:1, :], eo[1:2, :]], axis=1)
    local = jnp.concatenate([er[0:1, :], er[1:2, :]], axis=1)
    rows = iota((n_dom, ends), 0)
    turned = ((rows & (n_y - 1)) << lzc) + (rows >> ly)
    match = owner == turned
    match_hot = hot(match)
    before = hot(iota((ends, ends), 0) < iota((ends, ends), 1))
    rank = nn(match_hot, before)
    slot = jnp.sum(jnp.where(match, rank, 0.0), axis=0, keepdims=True)
    place[...] = jnp.broadcast_to(owner.astype(F32) * float(SLOTS) + slot, place.shape)
    far = (place_of((owner >> lzc) - y, n_y) << lzc) + place_of((owner & (n_zc - 1)) - zc, n_zc)
    far_place[...] = jnp.broadcast_to(far.astype(F32) * float(SLOTS) + slot, far_place.shape)

    def lane_rows(at, value):
        lane = iota((LANES, value.shape[1]), 0)
        part = jnp.where(lane < 16, value >> 5, value & 31)
        return jnp.where(at & (lane < 32), part.astype(F32), 0.0).astype(BF)

    wanted = lane_rows(slot == (iota((LANES, ends), 0) & 15).astype(F32), local)
    lane = iota((LANES, n_dom), 0) & 15
    halo_ids = jnp.where(lane == SLOTS, hr[0:1, :], hr[1:2, :])
    halo_wanted = lane_rows((lane == SLOTS) | (lane == SLOTS + 1), halo_ids)
    prow, pcol = iota((n_dom, n_dom), 0), iota((n_dom, n_dom), 1)
    to_zc_y = hot(pcol == ((prow & (n_y - 1)) << lzc) + (prow >> ly))
    to_y_zc = hot(pcol == ((prow & (n_zc - 1)) << ly) + (prow >> lzc))
    requests = nt(match_hot, wanted) + nt(to_zc_y, halo_wanted)
    ids_s[...] = requests.astype(BF).reshape(n_zc, n_y, LANES)

    pl.semaphore_wait(barrier, (n_zc - 1) + (n_y - 1) + (n_x - 1))
    along_zc(0, lambda p: ids_s.at[p], lambda m: ids_r1.at[m], ids_s.at[pl.ds(0, n_zc - 1)])

    tile = min(256, nodes)
    loads[0].wait()
    loads[1].wait()

    @pl.loop(0, nodes // tile)
    def _(i):
        at = pl.ds(pl.multiple_of(i * tile, tile), tile)
        inner[at, :] = nn(adji[at, :], feats[...])

    copies(ids_r1, rsem.at[0]).wait()
    ids_t[...] = nn(to_y_zc, ids_r1[...].reshape(n_dom, LANES)).astype(BF).reshape(n_y, n_zc, LANES)
    along_y(1, lambda p: ids_t.at[p], lambda m: ids_r2.at[m], ids_t.at[pl.ds(0, n_y - 1)])

    loads[2].wait()
    loads[3].wait()

    @pl.loop(0, nodes // tile)
    def _(i):
        at = pl.ds(pl.multiple_of(i * tile, tile), tile)
        selfp[at, :] = nn(feats[at, :], wself[...]) + b_enc[...]

    ko, jo = iota((halos, halos), 0), iota((halos, halos), 1)
    std = ((((jo >> (lzc + 1)) << lzc) + (jo & (n_zc - 1))) << 1) + ((jo >> lzc) & 1)
    adjp[...] = nn(adjh[...], hot(ko == std)).astype(BF)
    std = ((((jo & (n_y - 1)) << lzc) + (jo >> (ly + 1))) << 1) + ((jo >> ly) & 1)
    adjq[...] = nn(adjh[...], hot(ko == std)).astype(BF)

    io, oo = iota((halos, halos), 1), iota((halos, halos), 0)
    turn[...] = hot(io == ((oo & (n_zc - 1)) << (ly + 1)) + (((oo >> lzc) & 1) << ly) + (oo >> (lzc + 1)))
    back[...] = hot(io == ((oo & (n_y - 1)) << (lzc + 1)) + (((oo >> ly) & 1) << lzc) + (oo >> (ly + 1)))

    for i in (4, 5, 6):
        loads[i].wait()

    copies(ids_r2, rsem.at[1]).wait()
    asked = nn(to_zc_y, ids_r2[...].reshape(n_dom, LANES))
    asked_c = [32.0 * asked[:, at : at + 1] + asked[:, at + 16 : at + 17] for at in (SLOTS, SLOTS + 1)]
    pick = hot(jnp.concatenate(asked_c, axis=0) == iota((halos, nodes), 1).astype(F32))
    picked = nn(pick, hist[...]).astype(BF)
    for c in range(2):
        hal_s[:, c] = picked[c * n_dom : (c + 1) * n_dom, :half].reshape(n_zc, n_y, half)
        hal_m[:, c] = picked[c * n_dom : (c + 1) * n_dom, half:].reshape(n_zc, n_y, half)
    along_zc(2, lambda p: hal_s.at[p], lambda m: hal_r1.at[m], hal_s.at[pl.ds(0, n_zc - 1)])
    hal_u[...] = nn(turn[...], hal_m[...].reshape(halos, half)).astype(BF).reshape(n_y, 2 * n_zc, half)
    along_y(22, lambda p: hal_u.at[p], lambda m: hal_v.at[m], hal_u.at[pl.ds(0, n_y - 1)])

    gtile = min(256, slots)
    per = gtile // SLOTS

    def ids_column(asked):
        n = asked.shape[0] * SLOTS
        spread = jnp.broadcast_to(asked[:, None, :], (asked.shape[0], SLOTS, LANES)).reshape(n, LANES)
        lane, mine = iota((n, LANES), 1), iota((n, LANES), 0) & (SLOTS - 1)
        weight = jnp.where(lane == mine, 32.0, jnp.where(lane == mine + 16, 1.0, 0.0))
        return jnp.sum(spread * weight, axis=1, keepdims=True)

    by_y = (offset_at(prow >> lzc, n_y) + y) & (n_y - 1)
    by_zc = (offset_at(prow & (n_zc - 1), n_zc) + zc) & (n_zc - 1)
    asked_far = nn(hot(pcol == (by_y << lzc) + by_zc), ids_r2[...].reshape(n_dom, LANES))

    def rows_named(tiles):
        for i in tiles:
            id_col = ids_column(asked_far[i * per : (i + 1) * per])
            hot_g[i * gtile : (i + 1) * gtile, :] = hot(id_col == iota((gtile, nodes), 1).astype(F32))

    tiles = slots // gtile
    rows_named(range(tiles // 2))

    copies(hal_r1, rsem.at[2]).wait()
    hal_t[...] = nn(turn[...], hal_r1[...].reshape(halos, half)).astype(BF).reshape(n_y, 2 * n_zc, half)
    along_y(3, lambda p: hal_t.at[p], lambda m: hal_r2.at[m], hal_t.at[pl.ds(0, n_y - 1)])
    copies(hal_v, rsem.at[22]).wait()
    hal_m[...] = nn(back[...], hal_v[...].reshape(halos, half)).astype(BF).reshape(n_zc, 2, n_y, half)
    along_zc(23, lambda p: hal_m.at[p], lambda m: hal_w.at[m], hal_m.at[pl.ds(0, n_zc - 1)])

    rows_named(range(tiles // 2, tiles))

    copies(hal_r2, rsem.at[3]).wait()
    copies(hal_w, rsem.at[23]).wait()

    @pl.loop(0, nodes // tile)
    def _(i):
        at = pl.ds(pl.multiple_of(i * tile, tile), tile)
        outer = [nn(adjp[at, :], hal_r2[...].reshape(halos, half)), nn(adjq[at, :], hal_w[...].reshape(halos, half))]
        agg = (inner[at, :] + jnp.concatenate(outer, axis=1)).astype(BF)
        emb_o[at, :] = jnp.maximum(selfp[at, :] + nn(agg, wnbr[...]), 0.0).astype(BF)

    left, right = pl.ds(0, half), pl.ds(half, half)

    y_off, zc_off = far_places(n_y), far_places(n_zc)
    y_part, zc_part = n_y // 2, n_zc // 2

    def send_to(index, peer, source, goal, signal):
        pltpu.make_async_remote_copy(
            src_ref=source, dst_ref=goal, send_sem=ssem.at[index], recv_sem=rsem.at[signal],
            device_id={"dom": peer}, device_id_type=MESH,
        ).start()

    def zc_at(p):
        return lax.rem(zc + zc_off[p], n_zc)

    def y_at(p):
        return lax.rem(y + y_off[p], n_y)

    def first_hop_zc(base, send, mid, group):
        ys = pl.ds(group * y_part, y_part)
        for p in range(n_zc):
            source, goal = send.at[ys, p, :, left], mid.at[zc, ys]
            if zc_off[p]:
                send_to(base, y * n_zc + zc_at(p), source, goal, base + 2 * group)
            else:
                pltpu.make_async_copy(source, goal, rsem.at[base + 2 * group]).start()

    def first_hop_y(base, send, mid, group, places):
        zcs = pl.ds(group * zc_part, zc_part)
        for p in places:
            source, goal = send.at[p, zcs, :, right], mid.at[y, zcs]
            if y_off[p]:
                send_to(base + 1, y_at(p) * n_zc + zc, source, goal, base + 1 + 2 * group)
            else:
                pltpu.make_async_copy(source, goal, rsem.at[base + 1 + 2 * group]).start()

    def second_hop_y(base, mid, recv, group):
        copies(mid.at[:, pl.ds(group * y_part, y_part)], rsem.at[base + 2 * group]).wait()
        for p in range(group * y_part, (group + 1) * y_part):
            source, goal = mid.at[:, p], recv.at[y, :, :, left]
            if y_off[p]:
                send_to(base + 2, y_at(p) * n_zc + zc, source, goal, base + 4)
            else:
                pltpu.make_async_copy(source, goal, rsem.at[base + 4]).start()

    def second_hop_zc(base, mid, recv, group):
        copies(mid.at[:, pl.ds(group * zc_part, zc_part)], rsem.at[base + 1 + 2 * group]).wait()
        for p in range(group * zc_part, (group + 1) * zc_part):
            source, goal = mid.at[:, p], recv.at[:, zc, :, right]
            if zc_off[p]:
                send_to(base + 3, y * n_zc + zc_at(p), source, goal, base + 5)
            else:
                pltpu.make_async_copy(source, goal, rsem.at[base + 5]).start()

    def second_hops(base, mid_a, mid_b, recv, group):
        second_hop_y(base, mid_a, recv, group)
        second_hop_zc(base, mid_b, recv, group)
        if group == 0:
            return
        sent.append((base, mid_a.at[pl.ds(0, n_zc - 1)]))
        sent.append((base + 1, mid_b.at[pl.ds(0, n_y - 1)]))
        sent.append((base + 2, mid_b.at[pl.ds(0, n_y - 1)]))
        sent.append((base + 3, mid_a.at[pl.ds(0, n_zc - 1)]))

    def arrived(base, recv):
        copies(recv.at[:, :, :, left], rsem.at[base + 4]).wait()
        copies(recv.at[:, :, :, right], rsem.at[base + 5]).wait()

    fet_s4, gra_s4 = (send.reshape(n_y, n_zc, SLOTS, width) for send in (fet_s, gra_s))
    far_y, near_y = range(y_part), range(y_part, n_y)

    def selected(select, rows, goal, low, high):
        @pl.loop(low, high)
        def _(i):
            at = pl.ds(pl.multiple_of(i * gtile, gtile), gtile)
            goal[pl.ds(i * per, per)] = nn(select[at, :], rows[...]).astype(BF).reshape(per, SLOTS, width)

    selected(hot_g, emb_o, fet_s, 0, tiles // 2)
    first_hop_zc(24, fet_s4, fet_a, 0)
    first_hop_y(24, fet_s4, fet_b, 0, far_y)
    selected(hot_g, emb_o, fet_s, tiles // 2, tiles)
    first_hop_y(24, fet_s4, fet_b, 0, near_y)
    first_hop_zc(24, fet_s4, fet_a, 1)
    first_hop_y(24, fet_s4, fet_b, 1, range(n_y))
    place_col = column_of(place[0:1, :])
    etile = min(256, ends)
    for i in range(ends // etile):
        hot_e[i * etile : (i + 1) * etile, :] = hot(
            place_col[i * etile : (i + 1) * etile, :] == iota((etile, slots), 1).astype(F32)
        )

    @pl.loop(0, slots // gtile)
    def _(i):
        at = pl.ds(pl.multiple_of(i * gtile, gtile), gtile)
        hot_et[at, :] = hot((iota((gtile, ends), 0) + i * gtile).astype(F32) == far_place[0:1, :])

    target = column_of(lab[...].astype(F32))

    second_hops(24, fet_a, fet_b, fet_r, 0)
    second_hops(24, fet_a, fet_b, fet_r, 1)

    asked = ids_r2[...].reshape(n_dom, LANES).astype(F32)
    id_row = jnp.concatenate(
        [row_of(ids_column(asked[i * per : (i + 1) * per])) for i in range(slots // gtile)], axis=1
    )

    @pl.loop(0, nodes // tile)
    def _(i):
        at = pl.ds(pl.multiple_of(i * tile, tile), tile)
        hot_gt[at, :] = hot((iota((tile, slots), 0) + i * tile).astype(F32) == id_row)

    arrived(24, fet_r)

    got = fet_r[...].reshape(slots, width)
    head = nn(hot_e[:queries, :], got)
    tail = nn(hot_e[queries:, :], got)
    zprod = (head * tail).astype(BF)
    pre = nn(zprod, wdec1[...]) + b_dec1[...]
    sig = jax.nn.sigmoid(pre)
    hidden = (pre * sig).astype(BF).astype(F32)
    wout = w_dec2[...].astype(F32).reshape(1, width)
    logit = jnp.sum(hidden * wout, axis=1, keepdims=True)
    dlogit = jax.nn.sigmoid(logit) - target
    d_pre = (dlogit * wout * (sig * (1.0 + pre * (1.0 - sig)))).astype(BF)
    grad1 = tn(zprod, d_pre)
    gb1 = jnp.sum(d_pre.astype(F32), axis=0, keepdims=True)
    gd2 = jnp.sum(hidden * dlogit, axis=0, keepdims=True)
    vrow = iota((8, width), 0)
    vecs = jnp.where(vrow == 0, gb1, jnp.where(vrow == 1, gd2, 0.0))
    crows = width // 2
    zrows = crows // n_z
    for h in range(2):
        dc_s[h, :crows] = grad1[h * crows : (h + 1) * crows]
        dc_s[h, crows:] = vecs
    other = 1 - core
    pair = pltpu.make_async_remote_copy(
        src_ref=dc_s.at[other], dst_ref=dc_r, send_sem=ssem.at[12], recv_sem=rsem.at[12],
        device_id={"dom": y * n_zc + 2 * z + other}, device_id_type=MESH,
    )
    pair.start()

    def along_z(index, source, goal, sent_size):
        for k in far_first(n_z):
            peer = lax.rem(z + k, n_z)
            pltpu.make_async_remote_copy(
                src_ref=source(peer), dst_ref=goal(z), send_sem=ssem.at[index], recv_sem=rsem.at[index],
                device_id={"dom": y * n_zc + 2 * peer + core}, device_id_type=MESH,
            ).start()
        pltpu.make_async_copy(source(z), goal(z), rsem.at[index]).start()
        sent.append((index, sent_size))

    dz = nt(d_pre, wdec1[...])
    gpair[:queries, :] = (dz * tail).astype(BF)
    gpair[queries:, :] = (dz * head).astype(BF)

    selected(hot_et, gpair, gra_s, 0, tiles // 2)
    first_hop_y(30, gra_s4, gra_b, 0, far_y)

    pair.wait_recv()
    for j in range(n_z):
        dz_s[j, :zrows] = (dc_s[core, j * zrows : (j + 1) * zrows] + dc_r[j * zrows : (j + 1) * zrows]).astype(BF)
        dz_s[j, zrows:] = (dc_s[core, crows:] + dc_r[crows:]).astype(BF)
    along_z(13, lambda p: dz_s.at[p], lambda m: dz_r.at[m], dz_s.at[pl.ds(0, n_z - 1)])
    first_hop_zc(30, gra_s4, gra_a, 0)
    selected(hot_et, gpair, gra_s, tiles // 2, tiles)
    first_hop_y(30, gra_s4, gra_b, 0, near_y)

    first_hop_zc(30, gra_s4, gra_a, 1)
    first_hop_y(30, gra_s4, gra_b, 1, range(n_y))

    copies(dz_r, rsem.at[13]).wait()
    total = dz_r[0].astype(F32)
    for j in range(1, n_z):
        total = total + dz_r[j].astype(F32)
    zbuf[...] = total.astype(BF)
    along_y(14, lambda p: zbuf, lambda m: dy_r.at[m], dy_r.at[pl.ds(0, n_y - 1)])

    second_hops(30, gra_a, gra_b, gra_r, 0)
    second_hops(30, gra_a, gra_b, gra_r, 1)

    copies(dy_r, rsem.at[14]).wait()
    total = dy_r[0].astype(F32)
    for j in range(1, n_y):
        total = total + dy_r[j].astype(F32)
    dbuf[...] = total
    for k in range(1, n_x):
        pltpu.make_async_remote_copy(
            src_ref=dbuf, dst_ref=dx_r.at[rep], send_sem=ssem.at[15], recv_sem=rsem.at[15],
            device_id={"rep": lax.rem(rep + k, n_x)}, device_id_type=MESH,
        ).start()
    pltpu.make_async_copy(dbuf, dx_r.at[rep], rsem.at[15]).start()
    sent.append((15, dx_r.at[pl.ds(0, n_x - 1)]))

    flip = rep + 1 - 2 * lax.rem(rep, 2)
    wrap = 3 - rep
    wflip = wrap + 1 - 2 * lax.rem(wrap, 2)
    quarter = nodes // n_x
    jtile = min(64, quarter)

    crow = quarter // 2
    chunks = [(ch, pl.ds(ch * crow, crow)) for ch in range(2)]

    def local_sum(q, ch):
        at = pl.ds(pl.multiple_of(q * quarter + ch * crow, crow), crow)
        return nn(hot_gt[at, :], gra_r[...].reshape(slots, width))

    def trade(index, source, goal, partner):
        copy = pltpu.make_async_remote_copy(
            src_ref=source, dst_ref=goal, send_sem=ssem.at[index], recv_sem=rsem.at[index],
            device_id={"rep": partner}, device_id_type=MESH,
        )
        copy.start()
        return copy

    def joined(way, part, ch):
        @pl.loop(0, crow // jtile)
        def _(i):
            at = pl.ds(pl.multiple_of(ch * crow + i * jtile, jtile), jtile)
            xs2[way, at, :] = (xk[part, at, :] + xr1[way, 1, at, :].astype(F32)).astype(BF)

    arrived(30, gra_r)
    firsts, seconds = [], []
    for ch, at in chunks:
        part = local_sum(wflip, ch)
        xs1[0, 1, at] = part[:, :half].astype(BF)
        xs1[1, 1, at] = part[:, half:].astype(BF)
        part = local_sum(flip, ch)
        xs1[0, 0, at] = part[:, :half].astype(BF)
        one = trade(36 + ch, xs1.at[0, :, at], xr1.at[0, :, at], flip)
        xk[3, at] = part[:, half:]
        part = local_sum(wrap, ch)
        xs1[1, 0, at] = part[:, half:].astype(BF)
        two = trade(38 + ch, xs1.at[1, :, at], xr1.at[1, :, at], wrap)
        xk[2, at] = part[:, :half]
        firsts.append((one, two))

    copies(dx_r, rsem.at[15]).wait()
    total = dx_r[0]
    for j in range(1, n_x):
        total = total + dx_r[j]
    gv_o[...] = total[zrows:]
    dc_r[:zrows] = total[:zrows]
    along_z(20, lambda p: dc_r.at[pl.ds(0, zrows)], lambda m: dg_r.at[core, m], dg_r.at[0, pl.ds(0, n_z - 1)])

    for ch, at in chunks:
        part = local_sum(rep, ch)
        xk[0, at] = part[:, :half]
        xk[1, at] = part[:, half:]
    for ch, at in chunks:
        one, two = firsts[ch]
        one.wait_recv()
        joined(0, 2, ch)
        three = trade(40 + ch, xs2.at[0, at], xr2.at[0, at], wrap)
        two.wait_recv()
        joined(1, 3, ch)
        four = trade(42 + ch, xs2.at[1, at], xr2.at[1, at], flip)
        seconds.append((three, four))

    copies(dg_r.at[0], rsem.at[20]).wait()
    last = pltpu.make_async_remote_copy(
        src_ref=dg_r.at[core], dst_ref=dg_r.at[core], send_sem=ssem.at[21], recv_sem=rsem.at[21],
        device_id={"dom": y * n_zc + 2 * z + other}, device_id_type=MESH,
    )
    last.start()

    for ch, at in chunks:
        three, four = seconds[ch]
        three.wait_recv()
        ge_o[at, :half] = xk[0, at] + xr1[0, 0, at].astype(F32) + xr2[0, at].astype(F32)
        four.wait_recv()
        ge_o[at, half:] = xk[1, at] + xr1[1, 0, at].astype(F32) + xr2[1, at].astype(F32)

    drain()
    pair.wait_send()
    for pair_of in firsts + seconds:
        for copy in pair_of:
            copy.wait_send()
    last.wait()
    gd_o[...] = dg_r[...].reshape(width, width)


def put_out(emb, ge, gd, gv, emb_h, ge_h, gd_h, gb_h, g2_h, sem):
    pairs = ((emb, emb_h), (ge, ge_h), (gd, gd_h), (gv.at[pl.ds(0, 1)], gb_h), (gv.at[pl.ds(1, 1)], g2_h))
    copies_out = [pltpu.make_async_copy(src, dst, sem.at[i]) for i, (src, dst) in enumerate(pairs)]
    for copy in copies_out:
        copy.start()
    for copy in copies_out:
        copy.wait()


def per_device(
    feats, history, adj_inner, adj_halo, halo_rows, w_self, w_nbr, b_enc,
    edge_owner, edge_rows, labels, w_dec1, b_dec1, w_dec2,
):
    n_dom, n_x = lax.axis_size("dom"), lax.axis_size("rep")
    n_zc = 16 if n_dom == 128 else 4
    n_y = n_dom // n_zc
    nodes, width = feats.shape
    halos = adj_halo.shape[1]
    queries = edge_owner.shape[0]
    ends = 2 * queries
    slots = n_dom * SLOTS
    half = width // 2
    n_z = n_zc // 2
    quarter = nodes // n_x
    crows = width // 2
    zrows = crows // n_z
    vmem = pl.BlockSpec(memory_space=pltpu.VMEM)
    any_ = pl.BlockSpec(memory_space=pl.ANY)
    V = pltpu.VMEM
    outs = pl.pallas_call(
        functools.partial(kernel, n_y, n_zc, n_x),
        out_shape=(
            V((nodes, width), BF),
            V((quarter, width), F32),
            V((width, width), F32),
            V((8, width), F32),
        ),
        in_specs=[any_] * 14,
        out_specs=(vmem,) * 4,
        scratch_shapes=[
            V((2, queries), I32), V((2, queries), I32), V((2, n_dom), I32), V((1, queries), I32), V((1, width), F32),
            V((1, width), F32), V((width,), BF),
            V((nodes, width), BF), V((nodes, width), BF), V((nodes, nodes), BF), V((nodes, halos), BF),
            V((width, width), BF), V((width, width), BF), V((width, width), BF),
            V((n_zc, n_y, LANES), BF), V((n_zc, n_y, LANES), BF), V((n_y, n_zc, LANES), BF), V((n_y, n_zc, LANES), BF),
            V((n_zc, 2, n_y, half), BF), V((n_zc, 2, n_y, half), BF), V((n_y, 2 * n_zc, half), BF),
            V((n_y, 2 * n_zc, half), BF), V((n_zc, 2, n_y, half), BF), V((n_y, 2 * n_zc, half), BF),
            V((n_y, 2 * n_zc, half), BF), V((n_zc, 2, n_y, half), BF), V((halos, halos), BF), V((halos, halos), BF), V((nodes, halos), BF), V((nodes, halos), BF),
            V((nodes, width), F32), V((nodes, width), F32), V((8, ends), F32), V((8, ends), F32),
            V((ends, slots), BF), V((slots, ends), BF), V((slots, nodes), BF), V((nodes, slots), BF),
            V((n_dom, SLOTS, width), BF), V((n_zc, n_y, SLOTS, half), BF), V((n_y, n_zc, SLOTS, half), BF),
            V((n_y, n_zc, SLOTS, width), BF),
            V((n_dom, SLOTS, width), BF), V((n_zc, n_y, SLOTS, half), BF), V((n_y, n_zc, SLOTS, half), BF),
            V((n_y, n_zc, SLOTS, width), BF), V((ends, width), BF),
            V((zrows + 8, width), BF), V((zrows + 8, width), F32),
            V((2, 2, quarter, half), BF), V((2, 2, quarter, half), BF), V((2, quarter, half), BF),
            V((2, quarter, half), BF), V((4, quarter, half), F32),
            V((2, crows + 8, width), F32), V((crows + 8, width), F32),
            V((n_z, zrows + 8, width), BF), V((n_z, zrows + 8, width), BF),
            V((n_y, zrows + 8, width), BF), V((n_x, zrows + 8, width), F32), V((2, n_z, zrows, width), F32),
            pltpu.SemaphoreType.DMA((7,)), pltpu.SemaphoreType.DMA((7,)),
            pltpu.SemaphoreType.DMA((44,)), pltpu.SemaphoreType.DMA((44,)),
        ],
        compiler_params=pltpu.CompilerParams(
            collective_id=0, has_side_effects=True, vmem_limit_bytes=60 * 1024 * 1024
        ),
        name="encode_decode",
    )(
        edge_owner.T, edge_rows.T, halo_rows.T, labels.reshape(1, -1), b_enc.reshape(1, -1), b_dec1.reshape(1, -1),
        w_dec2, feats, history, adj_inner, adj_halo, w_self, w_nbr, w_dec1,
    )
    shapes = ((nodes, width, BF), (quarter, width, F32), (width, width, F32), (1, width, F32), (1, width, F32))
    embed, grad_embed, grad_dec1, bias1, dec2 = pl.pallas_call(
        put_out,
        out_shape=tuple(jax.ShapeDtypeStruct(shape[:2], shape[2]) for shape in shapes),
        in_specs=[vmem] * 4,
        out_specs=(any_,) * 5,
        scratch_shapes=[pltpu.SemaphoreType.DMA((5,))],
        name="put_out",
    )(*[pltpu.with_memory_space_constraint(out, pltpu.VMEM) for out in outs])
    return embed, grad_embed, grad_dec1, bias1.reshape(-1), dec2.reshape(-1)


def solution(mesh):
    placed = (
        P("dom", None), P("dom", None), P("dom", None), P("dom", None), P("dom", None), P(), P(), P(),
        P(("dom", "rep"), None), P(("dom", "rep"), None), P(("dom", "rep")), P(), P(), P(),
    )
    return jax.shard_map(
        per_device,
        mesh=mesh,
        in_specs=placed,
        out_specs=(P("dom", None), P(("dom", "rep"), None), P(), P(), P()),
        check_vma=False,
    )
```
